32 devices in a mesh: expert: 16 (over z, y, x), tensor: 2 (over core).
Axes of the slice: x: 2, y: 2, z: 4, core: 2. Of those that a mesh axis runs over, the one named last changes fastest.
Arguments:
- block_input: bfloat16 [3152, 512], P('expert'), may hold values from -6 to 6
- routes: int32 [3152, 2], P('expert'), may hold values from 0 to 15, all different within a row; in each aligned block of 197 rows (0 to 196, 197 to 393, ...) at most 49 rows name the same one
- w_query: float32 [512, 512], P('expert', 'tensor'), may hold values from -0.25 to 0.25
- w_key: float32 [512, 512], P('expert', 'tensor'), may hold values from -0.25 to 0.25
- w_value: float32 [512, 512], P('expert', 'tensor'), may hold values from -0.25 to 0.25
- w_output: float32 [512, 512], P('tensor', 'expert'), may hold values from -1 to 1
- w_router: float32 [512, 16], P('expert'), may hold values from -0.1875 to 0.1875
- norm1_gain: float32 [512], P('expert'), may hold values from 0.5 to 1.5
- norm1_bias: float32 [512], P('expert'), may hold values from -1.25 to 1.25
- norm2_gain: float32 [512], P('expert'), may hold values from 0.5 to 1.5
- norm2_bias: float32 [512], P('expert'), may hold values from -1.25 to 1.25
- expert_in: float32 [16, 512, 2048], P('expert', None, 'tensor'), may hold values from -0.25 to 0.25
- expert_in_bias: float32 [16, 2048], P('expert', 'tensor'), may hold values from -0.625 to 0.625
- expert_out: float32 [16, 2048, 512], P('expert', 'tensor'), may hold values from -0.1875 to 0.1875
- expert_out_bias: float32 [16, 512], P('expert'), may hold values from -0.625 to 0.625
- cotangent: bfloat16 [3152, 512], P('expert', 'tensor'), may hold values from -6 to 6
Outputs:
- block_output: bfloat16 [3152, 512], P('expert', 'tensor')
- input_grad: float32 [3152, 512], P('expert')
- grad_query: float32 [512, 512], P('expert', 'tensor')
- grad_key: float32 [512, 512], P('expert', 'tensor')
- grad_value: float32 [512, 512], P('expert', 'tensor')
- grad_output: float32 [512, 512], P('tensor', 'expert')
- grad_router: float32 [512, 16], P('expert')
- grad_norm1_gain: float32 [512], P('expert')
- grad_norm1_bias: float32 [512], P('expert')
- grad_norm2_gain: float32 [512], P('expert')
- grad_norm2_bias: float32 [512], P('expert')
- grad_expert_in: float32 [16, 512, 2048], P('expert', None, 'tensor')
- grad_expert_in_bias: float32 [16, 2048], P('expert', 'tensor')
- grad_expert_out: float32 [16, 2048, 512], P('expert', 'tensor')
- grad_expert_out_bias: float32 [16, 512], P('expert')
The draws below stay inside these ranges and needn't reach their ends.
Inputs may be any that keep to these rules, and one draw needn't show every extreme that they name: `routes`: each row names 2 different experts. Within the 197 rows of one index of expert (aligned blocks), no expert is named more than 49 times, and in every draw some expert is named exactly 49 times in some block.
All inputs are finite; a program needn't handle non-finite values.
Results may differ from the reference program's by a relative error of at most 0.02.
Values may be sent and summed in bfloat16 or wider, within the bound.
A program may use at most 64 MiB of HBM per device.

```python
import math
import jax
import jax.numpy as jnp
import numpy as np
from jax import lax

D = 512
FF = 2048
HEADS = 8
HEAD_DIM = 64
SEQ = 197
TOPK = 2
IMG_DEV = 1
TOK_DEV = 197
TOKENS = 3152
EXPERTS = 16
CAP = 49
N_EXPERT = 16


def strengthened(values, key, source, target, parts, factor):
    def block_of(position):
        return (jnp.arange(values.shape[position]) // (values.shape[position] // parts)).reshape((-1,) + (1,) * (values.ndim - 1 - position))

    one_side = jax.random.permutation(key, parts)[block_of(target)]
    second = (block_of(target) + parts // 2) % parts
    return jnp.where((block_of(source) == one_side) | (block_of(source) == second), factor * values, values)


def steps_of(key, shape, shards, least, high):
    factor_of = 1.0
    for axis_at, shards_of in shards:
        steps = jax.random.uniform(jax.random.fold_in(jax.random.fold_in(key, 6), axis_at), (shards_of,), jnp.float32, least / len(shards), high / len(shards))
        factor_of = factor_of * jnp.repeat(jnp.exp(steps), shape[axis_at] // shards_of).reshape((-1,) + (1,) * (len(shape) - 1 - axis_at))
    return factor_of


def deal_out(own_key, own, number, rows, number_of, top, most, lean):
    ranking = jax.random.permutation(own_key, number_of)
    packed, ordinary = shares(number_of, rows * top, most, lean, True), shares(number_of, rows * top, most, lean, False)
    places = jnp.arange(number_of)

    def named(tallies, turn):
        used = int((tallies > 0).sum())
        fixed = max(1, used // 4)
        passed = fixed + (places - fixed + turn * (used - fixed)) % max(1, number_of - fixed)
        return jnp.zeros((number_of,), jnp.int32).at[ranking[jnp.where(places < fixed, places, passed)]].set(jnp.asarray(tallies, jnp.int32))

    tallies = jnp.where(number % 4 == 0, named(packed, number // 4), named(ordinary, number - number // 4 - 1))
    mixed = jax.random.permutation(jax.random.fold_in(own, 3), number_of)
    source_of, sink = mixed[0:number_of // 2 * 2:2], mixed[1:number_of // 2 * 2:2]
    slack = jnp.minimum(tallies[source_of] - 1, most - tallies[sink]) // 2
    slack = jnp.where((source_of == ranking[0]) | (sink == ranking[0]) | (tallies[sink] == 0), 0, jnp.maximum(slack, 0))
    passed = jax.random.randint(jax.random.fold_in(own, 4), (number_of // 2,), 0, 1 << 20) % (slack + 1)
    tallies = tallies.at[source_of].add(-passed).at[sink].add(passed)
    labels = jnp.searchsorted(jnp.cumsum(tallies), jnp.arange(rows * top), side="right").astype(jnp.int32)
    table = labels.reshape(top, rows).T
    table = table[jax.random.permutation(jax.random.fold_in(own, 1), rows)]
    turn = jax.random.randint(jax.random.fold_in(own, 2), (rows, 1), 0, top)
    return jnp.take_along_axis(table, (jnp.arange(top)[None, :] + turn) % top, axis=1)


def shares(count, total, most, slope, full):
    weights = [(1 << 20) // math.isqrt(rank ** slope) + 1 for rank in range(1, count + 1)]
    largest = most if full else min(most, max(-(-total // count), total * weights[0] // sum(weights)))
    least = 1 if total - largest >= count - 1 else 0
    given, surplus = [largest] + [least] * (count - 1), total - largest - least * (count - 1)
    while surplus > 0:
        movable = [i for i in range(1, count) if given[i] < largest] or [i for i in range(1, count) if given[i] < most]
        mass, left = sum([weights[i] for i in movable]), surplus
        for i in movable:
            extra = min(most - given[i], max(1, left * weights[i] // mass), surplus)
            given[i] = given[i] + extra
            surplus = surplus - extra
    return np.array(given)


def scatter_about(own_key, dims, spread, limit, cuts=(), kind=jnp.bfloat16):
    entries = spread * jax.random.normal(own_key, dims, jnp.float32)
    if cuts:
        entries = entries * steps_of(own_key, dims, cuts, -0.22, 0.18)
    return jnp.clip(entries, -limit, limit).astype(kind)


def heavy_noise(rng, extent, scale, limit, split, heavy, held_as=jnp.bfloat16):
    values = scale * jax.random.normal(rng, extent, jnp.float32)
    if split:
        values = values * steps_of(rng, extent, split, -0.22, 0.18)
    return jnp.clip(strengthened(values, jax.random.fold_in(rng, 3), *heavy), -limit, limit).astype(held_as)


def setup_inputs(seed: int = 0) -> dict:
    key_list = jax.random.split(jax.random.key(seed), 17)
    block_input = heavy_noise(key_list[0], (TOKENS, D), 1.0, 6.0, ((0, 16),), (0, 1, 16, 2.0))
    routes_keys = jax.random.split(jax.random.fold_in(key_list[1], 1), TOKENS // TOK_DEV)
    routes_turns = jax.random.permutation(jax.random.fold_in(key_list[1], 3), TOKENS // TOK_DEV)
    routes = jax.vmap(lambda own, number: deal_out(jax.random.fold_in(key_list[1], 2), own, number, TOK_DEV, EXPERTS, TOPK, CAP, 2))(routes_keys, routes_turns).reshape((TOKENS, TOPK))
    w_query = scatter_about(key_list[2], (D, D), D ** -0.5, 0.25, ((0, 16), (1, 2)), jnp.float32)
    w_key = scatter_about(key_list[3], (D, D), D ** -0.5, 0.25, ((0, 16), (1, 2)), jnp.float32)
    w_value = scatter_about(key_list[4], (D, D), D ** -0.5, 0.25, ((0, 16), (1, 2)), jnp.float32)
    w_output = scatter_about(key_list[5], (D, D), (D // 16) ** -0.5, 1.0, ((0, 2), (1, 16)), jnp.float32)
    w_router = scatter_about(key_list[6], (D, EXPERTS), (2 * D) ** -0.5, 0.1875, ((0, 16),), jnp.float32)
    norm1_gain = jnp.clip(1.0 + 0.1 * jax.random.normal(key_list[7], (D,), jnp.float32), 0.5, 1.5)
    norm1_bias = scatter_about(key_list[8], (D,), 0.2, 1.25, ((0, 16),), jnp.float32)
    norm2_gain = jnp.clip(1.0 + 0.1 * jax.random.normal(key_list[9], (D,), jnp.float32), 0.5, 1.5)
    norm2_bias = scatter_about(key_list[10], (D,), 0.2, 1.25, ((0, 16),), jnp.float32)
    expert_in = scatter_about(key_list[11], (EXPERTS, D, FF), D ** -0.5, 0.25, ((0, 16), (2, 2)), jnp.float32)
    expert_in_bias = scatter_about(key_list[12], (EXPERTS, FF), 0.1, 0.625, ((0, 16), (1, 2)), jnp.float32)
    expert_out = scatter_about(key_list[13], (EXPERTS, FF, D), (FF // 2) ** -0.5, 0.1875, ((0, 16), (1, 2)), jnp.float32)
    expert_out_bias = scatter_about(key_list[14], (EXPERTS, D), 0.1, 0.625, ((0, 16),), jnp.float32)
    cotangent = heavy_noise(key_list[15], (TOKENS, D), 1.0, 6.0, ((0, 16), (1, 2)), (0, 1, 16, 2.0))
    return {"block_input": block_input, "routes": routes, "w_query": w_query, "w_key": w_key, "w_value": w_value, "w_output": w_output, "w_router": w_router, "norm1_gain": norm1_gain, "norm1_bias": norm1_bias, "norm2_gain": norm2_gain, "norm2_bias": norm2_bias, "expert_in": expert_in, "expert_in_bias": expert_in_bias, "expert_out": expert_out, "expert_out_bias": expert_out_bias, "cotangent": cotangent}


EPS = 1e-06

@jax.custom_vjp
def low(v):
    return lax.optimization_barrier(v.astype(jnp.bfloat16)).astype(jnp.float32)

@jax.custom_vjp
def low_back(v):
    return v

def low_keep(v):
    return (low(v), None)

def low_pass(kept, grad):
    return (grad,)

def back_keep(v):
    return (v, None)

def back_low(kept, grad):
    return (low(grad),)
low.defvjp(low_keep, low_pass)
low_back.defvjp(back_keep, back_low)

def high_dot(left, right):
    return jnp.dot(left, right, precision=lax.Precision.HIGHEST, preferred_element_type=jnp.float32)

def layer_norm(value, gain, bias):
    center = value - lax.optimization_barrier(jnp.mean(value, -1, keepdims=True))
    var = lax.optimization_barrier(jnp.mean(center * center, -1, keepdims=True))
    return center * lax.rsqrt(var + EPS) * gain + bias

def attend(blocks):
    query, keys, values = blocks
    scores = jnp.einsum('ishd,ithd->ihst', query, keys, precision=lax.Precision.HIGHEST) * (1.0 / math.sqrt(HEAD_DIM))
    scores = low_back(scores)
    probs = jax.nn.softmax(scores, axis=-1)
    return jnp.einsum('ihst,ithd->ishd', low(probs), values, precision=lax.Precision.HIGHEST)

def expert_block(pieces):
    rows, win, bin_, wout, bout = pieces
    rows = low_back(rows.reshape(N_EXPERT * CAP, D))
    hidden = low_back(high_dot(rows, low(win)) + bin_)
    active = low(jax.nn.gelu(hidden))
    result = high_dot(active, low(wout)) + bout
    return low_back(low(result)).reshape(N_EXPERT, CAP, D)

def reference(block_input, routes, w_query, w_key, w_value, w_output, w_router, norm1_gain, norm1_bias, norm2_gain, norm2_bias, expert_in, expert_in_bias, expert_out, expert_out_bias, cotangent):
    flat = routes.reshape(N_EXPERT, TOK_DEV * TOPK)
    hits = (flat[:, :, None] == jnp.arange(EXPERTS, dtype=jnp.int32)).astype(jnp.int32)
    slot = lax.optimization_barrier(jnp.sum((jnp.cumsum(hits, 1) - hits) * hits, -1)).astype(jnp.int32)
    block = jnp.broadcast_to(jnp.arange(N_EXPERT, dtype=jnp.int32)[:, None], flat.shape)

    def forward(xf, wq, wk, wv, wo, wr, ga1, be1, ga2, be2, win, bin_, wout, bout):
        xn1 = low(layer_norm(xf, low(ga1), low(be1)))
        query = low_back(low(high_dot(xn1, low(wq))))
        keys = low_back(low(high_dot(xn1, low(wk))))
        values = low_back(low(high_dot(xn1, low(wv))))
        shape5 = (N_EXPERT, IMG_DEV, SEQ, HEADS, HEAD_DIM)
        attended = lax.map(jax.checkpoint(attend), (query.reshape(shape5), keys.reshape(shape5), values.reshape(shape5)))
        attended = low_back(low(attended.reshape(TOKENS, D)))
        att = low_back(high_dot(attended, low(wo)))
        x1 = xf + att
        xn2 = low(layer_norm(x1, low(ga2), low(be2)))
        logits = low_back(high_dot(xn2, low(wr)))
        chosen = jnp.take_along_axis(logits, routes, axis=1)
        gates = jax.nn.softmax(chosen, axis=-1)
        rows = jnp.repeat(xn2, TOPK, axis=0).reshape(N_EXPERT, TOK_DEV * TOPK, D)
        buffer = jnp.zeros((EXPERTS, N_EXPERT, CAP, D), jnp.float32).at[flat, block, slot].set(rows)
        outputs = lax.map(jax.checkpoint(expert_block), (buffer, win, bin_, wout, bout))
        picked = outputs[flat, block, slot].reshape(TOKENS, TOPK, D)
        return x1 + lax.optimization_barrier(jnp.sum(gates[:, :, None] * picked, 1))
    result, pull = jax.vjp(forward, block_input.astype(jnp.float32), w_query, w_key, w_value, w_output, w_router, norm1_gain, norm1_bias, norm2_gain, norm2_bias, expert_in, expert_in_bias, expert_out, expert_out_bias)
    grads = pull(cotangent.astype(jnp.float32))
    return (result.astype(jnp.bfloat16), grads[0], grads[1], grads[2], grads[3], grads[4], grads[5], grads[6], grads[7], grads[8], grads[9], grads[10], grads[11], grads[12], grads[13])
```

```python
import functools
import math

import jax
import jax.numpy as jnp
from jax import lax
from jax.experimental import pallas as pl
from jax.experimental.pallas import tpu as pltpu
from jax.sharding import PartitionSpec as P

HEAD_DIM = 64
EPS = 1e-06
MESH = pl.DeviceIdType.MESH
BF = jnp.bfloat16
F32 = jnp.float32
LANES = 128


def dot_nn(a, b):
    return lax.dot_general(a, b, (((1,), (0,)), ((), ())), preferred_element_type=F32)


def dot_nt(a, b):
    return lax.dot_general(a, b, (((1,), (1,)), ((), ())), preferred_element_type=F32)


def dot_tn(a, b):
    return lax.dot_general(a, b, (((0,), (0,)), ((), ())), preferred_element_type=F32)


def halves(v):
    first = v.astype(BF)
    rest = v - first.astype(F32)
    second = rest.astype(BF)
    return first, second, (rest - second.astype(F32)).astype(BF)


def pick_nn(select, v):
    a, b, c = halves(v)
    return dot_nn(select, a) + dot_nn(select, b) + dot_nn(select, c)


def colsum(v):
    return jnp.sum(v, axis=0, keepdims=True)


def rowmean(v):
    return jnp.mean(v, -1, keepdims=True)


def rowsum(v):
    return jnp.sum(v, -1, keepdims=True)


def iota(shape, axis):
    return lax.broadcasted_iota(jnp.int32, shape, axis)


class Sizes:
    pass


def block_kernel(
    z,
    x_ref, routes_ref, wq_ref, wk_ref, wv_ref, wo_ref, small_ref, ebin_ref, ebout_ref, cot_ref, win_hbm, wout_hbm,
    y_ref, gx_ref, rs_ref, rsmall_ref, gwin_ref, gbin_ref, gwout_ref, gbout_ref,
    win32, wout32, win_s, wout_s,
    wst, wg, smst, smg, pads, pt_s, hat1_s, xn1_s, qkv_s, p_s, o_s, parts, partr,
    x1_s, hat2_s, xn2_s, cotf, gs, gr, xs, xr, growst, grow, x2, c2, a_s, gp_s, dh_s,
    tsend, trecv, es, er, dxs, dxr, dgst, dgr, hsend, hrecv, dx1_s, dqkv_s, gsend, smsend, bfpart,
    hbm_sem, send_sem, recv_sem, ssend, srecv,
):
    n, T, D, HW, R, F, rows, M, heads = z.n, z.T, z.D, z.HW, z.R, z.F, z.rows, z.M, z.heads
    me = lax.axis_index("expert")
    tn = lax.axis_index("tensor")
    other = 1 - tn
    partner = {"tensor": other}
    col = pl.multiple_of(tn * HW, HW)
    ocol = pl.multiple_of(other * HW, HW)

    def peer(k):
        return lax.rem(me + k, n)

    barrier = pltpu.get_barrier_semaphore()

    def greet(k, _):
        pl.semaphore_signal(barrier, inc=1, device_id={"expert": peer(k)}, device_id_type=MESH)
        return 0

    lax.fori_loop(1, n, greet, 0)
    pl.semaphore_signal(barrier, inc=1, device_id=partner, device_id_type=MESH)

    win_copy = pltpu.make_async_copy(win_hbm.at[0], win32, hbm_sem.at[0])
    wout_copy = pltpu.make_async_copy(wout_hbm.at[0], wout32, hbm_sem.at[1])
    win_copy.start()
    wout_copy.start()

    def remote(src, dst, i, dev):
        return pltpu.make_async_remote_copy(
            src_ref=src, dst_ref=dst, send_sem=send_sem.at[i], recv_sem=recv_sem.at[i], device_id=dev, device_id_type=MESH
        )

    def to_all(src_of, dst, i):
        def step(k, _):
            e = peer(k)
            remote(src_of(e), dst, i, {"expert": e}).start()
            return 0

        lax.fori_loop(1, n, step, 0)

    def all_done(buf, i):
        d = remote(buf.at[pl.ds(0, n - 1)], buf.at[pl.ds(0, n - 1)], i, partner)
        d.wait_send()
        d.wait_recv()

    wst[0] = wq_ref[...].astype(BF)
    wst[1] = wk_ref[...].astype(BF)
    wst[2] = wv_ref[...].astype(BF)
    wst[3] = wo_ref[...].T.astype(BF)
    smst[...] = small_ref[...]
    wg[me] = wst[...]
    smg[me] = smst[...]

    r = routes_ref[...]
    r0, r1 = r[:, 0:1], r[:, 1:2]
    ie = iota((T, n), 1)
    h0, h1 = r0 == ie, r1 == ie
    hit = jnp.logical_or(h0, h1).astype(F32).astype(BF)
    tri = (iota((T, T), 0) > iota((T, T), 1)).astype(F32).astype(BF)
    count = dot_nn(tri, hit)
    slot0 = rowsum(jnp.where(h0, count, 0.0))
    slot1 = rowsum(jnp.where(h1, count, 0.0))
    pos0 = r0.astype(F32) * R + slot0
    pos1 = r1.astype(F32) * R + slot1
    pads[...] = jnp.full(pads.shape, -1.0, F32)
    pads[0:T, 0:1] = pos0
    pads[0:T, 1:2] = pos1
    post = pads[...].T
    slots = iota((M, T), 0).astype(F32)
    pt_s[...] = jnp.logical_or(slots == post[0:1, 0:T], slots == post[1:2, 0:T]).astype(F32).astype(BF)

    gs[...] = dot_nn(pt_s[...], cot_ref[...]).reshape(n, R, HW).astype(BF)
    cotf[tn] = cot_ref[...]

    x = x_ref[...].astype(F32)
    center = x - rowmean(x)
    rstd1 = lax.rsqrt(rowmean(center * center) + EPS)
    hat1_s[...] = center * rstd1

    pl.semaphore_wait(barrier, n)

    to_all(lambda e: smst, smg.at[me], 0)
    to_all(lambda e: wst, wg.at[me], 1)
    cot_copy = remote(cot_ref, cotf.at[tn], 2, partner)
    cot_copy.start()
    to_all(lambda e: gs.at[e], gr.at[tn, me], 3)

    gr[tn, me] = gs[me]
    win_copy.wait()
    win_s[...] = win32[...].astype(BF)
    wout_copy.wait()
    wout_s[...] = wout32[...].astype(BF)

    all_done(smg, 0)
    small = smg[...].astype(F32).reshape(n * rows, smg.shape[2]).T
    ga1, be1 = small[n : n + 1], small[n + 1 : n + 2]
    ga2, be2 = small[n + 2 : n + 3], small[n + 3 : n + 4]
    wr = small[0:n].astype(BF)
    xn1 = (hat1_s[...] * ga1 + be1).astype(BF)
    xn1_s[...] = xn1
    all_done(wg, 1)
    scale = 1.0 / math.sqrt(HEAD_DIM)

    def weight(i):
        return wg[:, i].reshape(D, HW)

    for i in range(3):
        qkv_s[i] = dot_nn(xn1, weight(i)).astype(BF)
    outs = []
    for h in range(heads):
        sl = slice(h * HEAD_DIM, (h + 1) * HEAD_DIM)
        s = dot_nt(qkv_s[0, :, sl], qkv_s[1, :, sl]) * scale
        ex = jnp.exp(s - jnp.max(s, -1, keepdims=True))
        p = ex / rowsum(ex)
        p_s[h] = p
        outs.append(dot_nn(p.astype(BF), qkv_s[2, :, sl]))
    o_s[...] = jnp.concatenate(outs, -1).astype(BF)
    parts[...] = dot_nt(o_s[...], weight(3)).astype(BF)
    part_copy = remote(parts, partr, 4, partner)
    part_copy.start()
    part_copy.wait()
    x1 = x_ref[...].astype(F32) + (parts[...].astype(F32) + partr[...].astype(F32))
    x1_s[...] = x1

    center = x1 - rowmean(x1)
    rstd2 = lax.rsqrt(rowmean(center * center) + EPS)
    hat2 = center * rstd2
    hat2_s[...] = hat2
    xn2 = (hat2 * ga2 + be2).astype(BF)
    xn2_s[...] = xn2
    logits = dot_nt(xn2, wr)
    l0 = rowsum(jnp.where(h0, logits, 0.0))
    l1 = rowsum(jnp.where(h1, logits, 0.0))
    top = jnp.maximum(l0, l1)
    e0, e1 = jnp.exp(l0 - top), jnp.exp(l1 - top)
    gate0, gate1 = e0 / (e0 + e1), e1 / (e0 + e1)
    xs[...] = dot_nn(pt_s[...], xn2_s[:, pl.ds(col, HW)]).reshape(n, R, HW).astype(BF)
    islot = iota((T, LANES), 1).astype(F32)
    at0 = (slot0 == islot).astype(F32).astype(BF)
    at1 = (slot1 == islot).astype(F32).astype(BF)
    gate_rows = jnp.zeros((n, LANES), F32)
    for hh, gg, at in ((h0, gate0, at0), (h1, gate1, at1)):
        for part in halves(jnp.where(hh, gg, 0.0)):
            gate_rows = gate_rows + dot_tn(part, at)
    growst[:, 0, :] = gate_rows

    to_all(lambda e: growst.at[e], grow.at[me], 5)
    to_all(lambda e: xs.at[e], xr.at[tn, me], 6)
    grow[me] = growst[me]
    xr[tn, me] = xs[me]

    def to_partner(buf, i):
        c = remote(buf.at[tn], buf.at[tn], i, partner)
        c.start()
        return c

    all_done(gr.at[tn], 3)
    g_copy = to_partner(gr, 7)
    all_done(grow, 5)
    block_of = iota((M, n), 0) - iota((M, n), 1) * R
    in_block = jnp.logical_and(block_of >= 0, block_of < R)
    sel = in_block.astype(F32).astype(BF)
    at_slot = rowsum(jnp.where(in_block, block_of.astype(F32), 0.0))
    one_slot = at_slot == iota((M, LANES), 1).astype(F32)
    gate_col = rowsum(jnp.where(one_slot, pick_nn(sel, grow[:, 0, :]), 0.0))
    g_copy.wait()

    for hf in range(2):
        g2 = gr[hf].reshape(M, HW).astype(F32)
        c2[:, hf * HW : (hf + 1) * HW] = (gate_col * g2).astype(BF)
    gbout_ref[...] = colsum(c2[...].astype(F32))

    all_done(xr.at[tn], 6)
    x_copy = to_partner(xr, 8)
    x_copy.wait()
    for hf in range(2):
        x2[:, hf * HW : (hf + 1) * HW] = xr[hf].reshape(M, HW)

    FT = 256
    k0 = math.sqrt(2.0 / math.pi)

    def first(i, _):
        f = pl.ds(pl.multiple_of(i * FT, FT), FT)
        h = dot_nn(x2[...], win_s[:, f]) + ebin_ref[:, f]
        hh = h * h
        th = jnp.tanh(k0 * (h + 0.044715 * (hh * h)))
        half = 0.5 * (1.0 + th)
        a_s[:, f] = (h * half).astype(BF)
        slope = half + (0.5 * k0) * h * (1.0 - th * th) * (1.0 + (3 * 0.044715) * hh)
        dh = (slope * dot_nt(c2[...], wout_s[f, :])).astype(BF)
        dh_s[:, f] = dh
        gbin_ref[:, f] = colsum(dh.astype(F32))
        return 0

    lax.fori_loop(0, F // FT, first, 0)

    tsend[0] = dot_nt(dh_s[...], win_s[pl.ds(ocol, HW), :]).astype(BF)
    t0 = remote(tsend.at[0], trecv.at[0], 9, partner)
    t0.start()
    dx_own = dot_nt(dh_s[...], win_s[pl.ds(col, HW), :])
    tsend[1] = dot_nn(a_s[...], wout_s[:, pl.ds(ocol, HW)]).astype(BF)
    t1 = remote(tsend.at[1], trecv.at[1], 10, partner)
    t1.start()
    t0.wait()
    dxs[...] = (dx_own + trecv[0].astype(F32)).reshape(n, R, HW).astype(BF)
    to_all(lambda e: dxs.at[e], dxr.at[me], 11)
    dxr[me] = dxs[me]
    e_own = dot_nn(a_s[...], wout_s[:, pl.ds(col, HW)])
    t1.wait()
    e_row = (e_own + trecv[1].astype(F32) + ebout_ref[:, pl.ds(col, HW)]).astype(BF)
    es[...] = e_row.reshape(n, R, HW)
    dgate = rowsum(gr[tn].reshape(M, HW).astype(F32) * e_row.astype(F32))
    spread = jnp.where(one_slot, dgate, 0.0)
    dg_rows = jnp.zeros((n, LANES), F32)
    for part in halves(spread):
        dg_rows = dg_rows + dot_tn(sel, part)
    dgst[:, 0, :] = dg_rows

    def send_gate(k, _):
        e = peer(k)
        remote(dgst.at[e], dgr.at[tn, me], 12, {"expert": e}).start()
        remote(dgst.at[e], dgr.at[tn, me], 22, {"expert": e, "tensor": other}).start()
        return 0

    lax.fori_loop(1, n, send_gate, 0)
    own_gate = remote(dgst.at[me], dgr.at[tn, me], 13, partner)
    own_gate.start()
    dgr[tn, me] = dgst[me]
    to_all(lambda e: es.at[e], er.at[me], 14)
    er[me] = es[me]

    def grads(i, _):
        f = pl.ds(pl.multiple_of(i * FT, FT), FT)
        gwout_ref[f, :] = dot_tn(a_s[:, f], c2[...])
        gwin_ref[:, f] = dot_tn(x2[...], dh_s[:, f])
        return 0

    lax.fori_loop(0, F // FT, grads, 0)

    all_done(dgr.at[tn], 12)
    all_done(dgr.at[other], 22)
    own_gate.wait()
    dg_all = dgr[0, :, 0, :] + dgr[1, :, 0, :]
    hb0, hb1 = h0.astype(F32).astype(BF), h1.astype(F32).astype(BF)
    dg0 = rowsum(jnp.where(slot0 == islot, pick_nn(hb0, dg_all), 0.0))
    dg1 = rowsum(jnp.where(slot1 == islot, pick_nn(hb1, dg_all), 0.0))
    mean_gate = gate0 * dg0 + gate1 * dg1
    dl0, dl1 = gate0 * (dg0 - mean_gate), gate1 * (dg1 - mean_gate)
    dlog = (jnp.where(h0, dl0, 0.0) + jnp.where(h1, dl1, 0.0)).astype(BF)

    all_done(dxr, 11)
    hsend[...] = dot_tn(pt_s[...], dxr[...].reshape(M, HW))
    hc = remote(hsend, hrecv.at[tn], 15, partner)
    hc.start()
    hrecv[tn] = hsend[...]
    by_router = dot_nn(dlog, wr)
    hc.wait()
    cot_copy.wait()
    dxn2 = jnp.concatenate([hrecv[0], hrecv[1]], -1) + by_router
    hat2 = hat2_s[...]
    gg2, gb2 = colsum(dxn2 * hat2), colsum(dxn2)
    u = dxn2 * ga2
    dx1 = jnp.concatenate([cotf[0], cotf[1]], -1).astype(F32) + rstd2 * (u - rowmean(u) - hat2 * rowmean(u * hat2))
    dx1_s[...] = dx1
    datt = dx1.astype(BF)
    do = dot_nn(datt, weight(3)).astype(BF)
    gsend[:, 0] = dot_tn(datt, o_s[...]).reshape(n, rows, HW).astype(BF)
    to_all(lambda e: gsend.at[e, 0], rs_ref.at[me, 0], 16)

    dqs, dks, dvs = [], [], []
    for h in range(heads):
        sl = slice(h * HEAD_DIM, (h + 1) * HEAD_DIM)
        p = p_s[h]
        doh = do[:, sl]
        dp = dot_nt(doh, qkv_s[2, :, sl])
        dvs.append(dot_tn(p.astype(BF), doh))
        ds = (p * (dp - rowsum(p * dp))).astype(BF)
        dqs.append(dot_nn(ds, qkv_s[1, :, sl]) * scale)
        dks.append(dot_tn(ds, qkv_s[0, :, sl]) * scale)
    for i, v in enumerate((dqs, dks, dvs)):
        dqkv_s[i] = jnp.concatenate(v, -1).astype(BF)
    bfpart[0] = (
        dot_nt(dqkv_s[0], weight(0)) + dot_nt(dqkv_s[1], weight(1)) + dot_nt(dqkv_s[2], weight(2))
    ).astype(BF)
    bc = remote(bfpart.at[0], bfpart.at[1], 17, partner)
    bc.start()
    for i in range(3):
        gsend[:, i + 1] = dot_tn(xn1_s[...], dqkv_s[i]).reshape(n, rows, HW).astype(BF)
        to_all(lambda e: gsend.at[e, i + 1], rs_ref.at[me, i + 1], 18 + i)
    rs_ref[me] = gsend[me]
    bc.wait()
    dxn1 = bfpart[0].astype(F32) + bfpart[1].astype(F32)
    hat1 = hat1_s[...]
    gg1, gb1 = colsum(dxn1 * hat1), colsum(dxn1)
    u = dxn1 * ga1
    gx_ref[...] = dx1_s[...] + rstd1 * (u - rowmean(u) - hat1 * rowmean(u * hat1))
    smsend[...] = jnp.zeros(smsend.shape, F32)
    smsend[0:n] = dot_tn(dlog, xn2_s[...])
    smsend[n : n + 1] = gg1
    smsend[n + 1 : n + 2] = gb1
    smsend[n + 2 : n + 3] = gg2
    smsend[n + 3 : n + 4] = gb2
    ssend[...] = smsend[...].T.reshape(n, rows, ssend.shape[2])
    to_all(lambda e: ssend.at[e], rsmall_ref.at[me], 21)
    rsmall_ref[me] = ssend[me]

    all_done(er, 14)
    rows_e = er[...].reshape(M, HW)
    slot_lane = iota((T, M), 1).astype(F32)
    y = x1_s[:, pl.ds(col, HW)]
    y = y + gate0 * dot_nn((slot_lane == pos0).astype(F32).astype(BF), rows_e)
    y = y + gate1 * dot_nn((slot_lane == pos1).astype(F32).astype(BF), rows_e)
    y_ref[...] = y.astype(BF)

    for i, j in enumerate((16, 18, 19, 20)):
        all_done(rs_ref.at[:, i], j)
    all_done(rsmall_ref, 21)


def shards(
    block_input, routes, w_query, w_key, w_value, w_output, w_router, norm1_gain, norm1_bias, norm2_gain, norm2_bias,
    expert_in, expert_in_bias, expert_out, expert_out_bias, cotangent,
):
    z = Sizes()
    z.n = lax.axis_size("expert")
    z.T, z.D = block_input.shape
    z.HW = cotangent.shape[1]
    z.F = expert_in.shape[2]
    z.rows = w_query.shape[0]
    z.heads = z.HW // HEAD_DIM
    experts, topk = w_router.shape[1], routes.shape[1]
    cap = max(2, 2 * topk * z.T // experts)
    z.R = -(-cap // 8) * 8
    z.M = z.n * z.R
    n, T, D, HW, R, F, rows, M = z.n, z.T, z.D, z.HW, z.R, z.F, z.rows, z.M
    small = jnp.concatenate([w_router] + [v[:, None] for v in (norm1_gain, norm1_bias, norm2_gain, norm2_bias)], 1)
    wide = -(-small.shape[1] // LANES) * LANES
    small = jnp.pad(small, ((0, 0), (0, wide - small.shape[1]))).astype(BF)
    vm = pl.BlockSpec(memory_space=pltpu.VMEM)
    hbm = pl.BlockSpec(memory_space=pl.ANY)
    out_shape = (
        jax.ShapeDtypeStruct((T, HW), BF),
        jax.ShapeDtypeStruct((T, D), F32),
        jax.ShapeDtypeStruct((n, 4, rows, HW), BF),
        jax.ShapeDtypeStruct((n, rows, wide), F32),
        jax.ShapeDtypeStruct((D, F), F32),
        jax.ShapeDtypeStruct((1, F), F32),
        jax.ShapeDtypeStruct((F, D), F32),
        jax.ShapeDtypeStruct((1, D), F32),
    )
    V = pltpu.VMEM
    tp = -(-T // LANES) * LANES
    scratch = [
        V((D, F), F32), V((F, D), F32), V((D, F), BF), V((F, D), BF),
        V((4, rows, HW), BF), V((n, 4, rows, HW), BF), V((rows, wide), BF), V((n, rows, wide), BF),
        V((tp, LANES), F32), V((M, T), BF), V((T, D), F32), V((T, D), BF), V((3, T, HW), BF), V((z.heads, T, T), F32),
        V((T, HW), BF), V((T, D), BF), V((T, D), BF),
        V((T, D), F32), V((T, D), F32), V((T, D), BF), V((2, T, HW), BF),
        V((n, R, HW), BF), V((2, n, R, HW), BF), V((n, R, HW), BF), V((2, n, R, HW), BF),
        V((n, 1, LANES), F32), V((n, 1, LANES), F32), V((M, D), BF), V((M, D), BF), V((M, F), BF), V((8, LANES), F32), V((M, F), BF),
        V((2, M, HW), BF), V((2, M, HW), BF), V((n, R, HW), BF), V((n, R, HW), BF), V((n, R, HW), BF), V((n, R, HW), BF),
        V((n, 1, LANES), F32), V((2, n, 1, LANES), F32), V((T, HW), F32), V((2, T, HW), F32), V((T, D), F32), V((3, T, HW), BF),
        V((n, 4, rows, HW), BF), V((wide, D), F32), V((2, T, D), BF),
        pltpu.SemaphoreType.DMA((2,)), pltpu.SemaphoreType.DMA((23,)), pltpu.SemaphoreType.DMA((23,)),
        V((n, rows, wide), F32), V((8, LANES), F32),
    ]
    y, gx, rs, rsmall, gwin, gbin, gwout, gbout = pl.pallas_call(
        functools.partial(block_kernel, z),
        out_shape=out_shape,
        in_specs=[vm] * 10 + [hbm] * 2,
        out_specs=[vm] * 8,
        scratch_shapes=scratch,
        compiler_params=pltpu.CompilerParams(collective_id=0, has_side_effects=True, vmem_limit_bytes=62 << 20),
        name="block",
    )(
        block_input, routes, w_query, w_key, w_value, w_output, small, expert_in_bias, expert_out_bias, cotangent,
        expert_in, expert_out,
    )
    sums = jnp.sum(rs.astype(F32), 0)
    sm = jnp.sum(rsmall, 0)
    return (
        y, gx, sums[1], sums[2], sums[3], sums[0].T, sm[:, :n], sm[:, n], sm[:, n + 1], sm[:, n + 2], sm[:, n + 3],
        gwin[None], gbin, gwout[None], gbout,
    )


def solution(mesh):
    row, col = P("expert", None), P("expert", "tensor")
    vec = P("expert")
    in_specs = (
        row, row, col, col, col, P("tensor", "expert"), row, vec, vec, vec, vec,
        P("expert", None, "tensor"), col, P("expert", "tensor", None), row, col,
    )
    out_specs = (
        col, row, col, col, col, P("tensor", "expert"), row, vec, vec, vec, vec,
        P("expert", None, "tensor"), col, P("expert", "tensor", None), row,
    )
    return jax.shard_map(shards, mesh=mesh, in_specs=in_specs, out_specs=out_specs, check_vma=False)
```

```python
import functools
import math

import jax
import jax.numpy as jnp
from jax import lax
from jax.experimental import pallas as pl
from jax.experimental.pallas import tpu as pltpu
from jax.sharding import PartitionSpec as P

HEAD_DIM = 64
EPS = 1e-06
MESH = pl.DeviceIdType.MESH
BF = jnp.bfloat16
F32 = jnp.float32
LANES = 128
CHUNKS = 2


def dot_nn(a, b):
    return lax.dot_general(a, b, (((1,), (0,)), ((), ())), preferred_element_type=F32)


def dot_nt(a, b):
    return lax.dot_general(a, b, (((1,), (1,)), ((), ())), preferred_element_type=F32)


def dot_tn(a, b):
    return lax.dot_general(a, b, (((0,), (0,)), ((), ())), preferred_element_type=F32)


def halves(v):
    first = v.astype(BF)
    rest = v - first.astype(F32)
    second = rest.astype(BF)
    return first, second, (rest - second.astype(F32)).astype(BF)


def pick_nn(select, v):
    a, b, c = halves(v)
    return dot_nn(select, a) + dot_nn(select, b) + dot_nn(select, c)


def colsum(v):
    return jnp.sum(v, axis=0, keepdims=True)


def rowmean(v):
    return jnp.mean(v, -1, keepdims=True)


def rowsum(v):
    return jnp.sum(v, -1, keepdims=True)


def iota(shape, axis):
    return lax.broadcasted_iota(jnp.int32, shape, axis)


class Sizes:
    pass


def block_kernel(
    z,
    x_ref, routes_ref, wq_ref, wk_ref, wv_ref, wo_ref, wr_ref, ga1_ref, be1_ref, ga2_ref, be2_ref, ebin_ref, ebout_ref, cot_ref,
    win_hbm, wout_hbm,
    y_ref, gx_ref, rs_ref, rsmall_ref, gwin_ref, gbin_ref, gwout_ref, gbout_ref,
    win32, wout32, win_s, wout_s, square, flat, pads,
    wst, wg, smst, smg, pt_s, hat1_s, xn1_s, qkv_s, p_s, o_s, parts, partr,
    x1_s, hat2_s, xn2_s, cotf, gs, gr, xs, xr, growst, grow, x2, c2, a_s, dh_s,
    tsend, trecv, es, er, dxs, dxr, dgst, dgr, hsend, hrecv, dx1_s, dqkv_s, gsend, r1, r2s, smsend, ssend, sr1, s2s, bfpart,
    hbm_sem, send_sem, recv_sem,
):
    n, T, D, HW, R, F, rows, M, heads = z.n, z.T, z.D, z.HW, z.R, z.F, z.rows, z.M, z.heads
    lines, plane, chunks = z.lines, z.plane, z.chunks
    KC = n // chunks
    me = lax.axis_index("expert")
    tn = lax.axis_index("tensor")
    other = 1 - tn
    partner = {"tensor": other}
    line, spot = me // plane, lax.rem(me, plane)
    col = pl.multiple_of(tn * HW, HW)
    ocol = pl.multiple_of(other * HW, HW)
    counter = iter(range(z.sems))

    def ahead(k):
        return lax.rem(me + k, n)

    def behind(k):
        return lax.rem(me - k + n, n)

    def in_line(k):
        return lax.rem(line + k, lines)

    def in_plane(j):
        return line * plane + lax.rem(spot + j, plane)

    barrier = pltpu.get_barrier_semaphore()

    def greet(k, _):
        pl.semaphore_signal(barrier, inc=1, device_id={"expert": ahead(k)}, device_id_type=MESH)
        return 0

    lax.fori_loop(1, n, greet, 0)
    pl.semaphore_signal(barrier, inc=1, device_id=partner, device_id_type=MESH)

    win_copy = pltpu.make_async_copy(win_hbm.at[0], win32, hbm_sem.at[0])
    wout_copy = pltpu.make_async_copy(wout_hbm.at[0], wout32, hbm_sem.at[1])
    win_copy.start()
    wout_copy.start()

    def remote(src, dst, i, dev):
        return pltpu.make_async_remote_copy(
            src_ref=src, dst_ref=dst, send_sem=send_sem.at[i], recv_sem=recv_sem.at[i], device_id=dev, device_id_type=MESH
        )

    def spread(low, high, src, dst, to, i, core=None):
        def step(k, _):
            dev = {"expert": to(k)}
            if core is not None:
                dev["tensor"] = core
            remote(src.at[k], dst.at[k], i, dev).start()
            return 0

        lax.fori_loop(low, high, step, 0)

    def finish(ref, i):
        d = remote(ref, ref, i, partner)
        d.wait_send()
        d.wait_recv()

    wst[0] = wq_ref[...].astype(BF)
    wst[1] = wk_ref[...].astype(BF)
    wst[2] = wv_ref[...].astype(BF)
    wst[3] = wo_ref[...].astype(BF)
    square[...] = jnp.zeros(square.shape, F32)
    square[0:n, 0:rows] = wr_ref[...]
    for i, ref in enumerate((ga1_ref, be1_ref, ga2_ref, be2_ref)):
        square[n + i : n + i + 1, 0:rows] = ref[...]
    smst[...] = square[...].T[0:rows].astype(BF)
    wg[me] = wst[...]
    smg[me] = smst[...]

    flat[0:2, 0:T] = routes_ref[...].astype(F32)
    r = flat[...].T
    r0, r1_ = r[0:T, 0:1], r[0:T, 1:2]
    ie = iota((T, n), 1).astype(F32)
    h0, h1 = r0 == ie, r1_ == ie
    mine = me.astype(F32)
    k0 = jnp.where(r0 < mine, r0 - mine + n, r0 - mine)
    k1 = jnp.where(r1_ < mine, r1_ - mine + n, r1_ - mine)
    hk0, hk1 = k0 == ie, k1 == ie
    hit = jnp.logical_or(hk0, hk1).astype(F32).astype(BF)
    tri = (iota((T, T), 0) > iota((T, T), 1)).astype(F32).astype(BF)
    count = dot_nn(tri, hit)
    slot0 = rowsum(jnp.where(hk0, count, 0.0))
    slot1 = rowsum(jnp.where(hk1, count, 0.0))
    pos0 = k0 * R + slot0
    pos1 = k1 * R + slot1
    pads[...] = jnp.full(pads.shape, -1.0, F32)
    pads[0:T, 0:1] = pos0
    pads[0:T, 1:2] = pos1
    post = pads[...].T
    slots = iota((M, T), 0).astype(F32)
    pt_s[...] = jnp.logical_or(slots == post[0:1, 0:T], slots == post[1:2, 0:T]).astype(F32).astype(BF)

    gs[...] = dot_nn(pt_s[...], cot_ref[...]).reshape(n, R, HW).astype(BF)
    cotf[tn] = cot_ref[...]

    x = x_ref[...].astype(F32)
    center = x - rowmean(x)
    rstd1 = lax.rsqrt(rowmean(center * center) + EPS)
    hat1_s[...] = center * rstd1

    pl.semaphore_wait(barrier, n)

    line_sems = [next(counter) for _ in range(lines - 1)]
    small_sems = [next(counter) for _ in range(lines - 1)]
    plane_sem, small_plane_sem = next(counter), next(counter)

    def share(block):
        for j in range(1, plane):
            dev = {"expert": in_plane(j)}
            remote(wg.at[block], wg.at[block], plane_sem, dev).start()
            remote(smg.at[block], smg.at[block], small_plane_sem, dev).start()

    for k in range(1, lines):
        dev = {"expert": in_line(k) * plane + spot}
        remote(smst, smg.at[me], small_sems[k - 1], dev).start()
        remote(wst, wg.at[me], line_sems[k - 1], dev).start()
    share(me)
    cot_sem = next(counter)
    cot_copy = remote(cot_ref, cotf.at[tn], cot_sem, partner)
    cot_copy.start()

    gr[tn, 0] = gs[0]
    win_copy.wait()
    win_s[...] = win32[...].astype(BF)
    wout_copy.wait()
    wout_s[...] = wout32[...].astype(BF)

    for k in range(1, lines):
        finish(wst, line_sems[k - 1])
        finish(smst, small_sems[k - 1])
        share(in_line(lines - k) * plane + spot)

    g_sem = next(counter)
    spread(1, n, gs, gr.at[tn], ahead, g_sem)

    finish(smg.at[pl.ds(0, (plane - 1) * lines)], small_plane_sem)
    small = smg[...].astype(F32).reshape(n * rows, smg.shape[2]).T
    ga1, be1 = small[n : n + 1], small[n + 1 : n + 2]
    ga2, be2 = small[n + 2 : n + 3], small[n + 3 : n + 4]
    wr = small[0:n].astype(BF)
    xn1 = (hat1_s[...] * ga1 + be1).astype(BF)
    xn1_s[...] = xn1

    finish(wg.at[pl.ds(0, (plane - 1) * lines)], plane_sem)
    scale = 1.0 / math.sqrt(HEAD_DIM)

    def weight(i):
        return wg[:, i].reshape(D, HW)

    for i in range(3):
        qkv_s[i] = dot_nn(xn1, weight(i)).astype(BF)

    outs = []
    for h in range(heads):
        sl = slice(h * HEAD_DIM, (h + 1) * HEAD_DIM)
        s = dot_nt(qkv_s[0, :, sl], qkv_s[1, :, sl]) * scale
        ex = jnp.exp(s - jnp.max(s, -1, keepdims=True))
        p = ex / rowsum(ex)
        p_s[h] = p
        outs.append(dot_nn(p.astype(BF), qkv_s[2, :, sl]))
    o_s[...] = jnp.concatenate(outs, -1).astype(BF)

    parts[...] = dot_nt(o_s[...], weight(3)).astype(BF)
    part_sem = next(counter)
    part_copy = remote(parts, partr, part_sem, partner)
    part_copy.start()

    part_copy.wait()
    x1 = x_ref[...].astype(F32) + (parts[...].astype(F32) + partr[...].astype(F32))
    x1_s[...] = x1

    center = x1 - rowmean(x1)
    rstd2 = lax.rsqrt(rowmean(center * center) + EPS)
    hat2 = center * rstd2
    hat2_s[...] = hat2
    xn2 = (hat2 * ga2 + be2).astype(BF)
    xn2_s[...] = xn2
    xs[...] = dot_nn(pt_s[...], xn2_s[:, pl.ds(col, HW)]).reshape(n, R, HW).astype(BF)

    row_sems = [next(counter) for _ in range(chunks)]
    for c in range(chunks):
        spread(max(1, c * KC), (c + 1) * KC, xs, xr.at[tn], ahead, row_sems[c])
    xr[tn, 0] = xs[0]

    logits = dot_nt(xn2, wr)
    l0 = rowsum(jnp.where(h0, logits, 0.0))
    l1 = rowsum(jnp.where(h1, logits, 0.0))
    top = jnp.maximum(l0, l1)
    e0, e1 = jnp.exp(l0 - top), jnp.exp(l1 - top)
    gate0, gate1 = e0 / (e0 + e1), e1 / (e0 + e1)
    islot = iota((T, LANES), 1).astype(F32)
    at0 = (slot0 == islot).astype(F32).astype(BF)
    at1 = (slot1 == islot).astype(F32).astype(BF)
    gate_rows = jnp.zeros((n, LANES), F32)
    for hh, gg, at in ((hk0, gate0, at0), (hk1, gate1, at1)):
        for part in halves(jnp.where(hh, gg, 0.0)):
            gate_rows = gate_rows + dot_tn(part, at)
    growst[:, 0, :] = gate_rows
    gate_sem = next(counter)
    spread(1, n, growst, grow, ahead, gate_sem)
    grow[0] = growst[0]

    finish(gr.at[tn, pl.ds(0, n - 1)], g_sem)
    g2_sem = next(counter)
    g_copy = remote(gr.at[tn], gr.at[tn], g2_sem, partner)
    g_copy.start()

    finish(grow.at[pl.ds(0, n - 1)], gate_sem)
    block_of = iota((M, n), 0) - iota((M, n), 1) * R
    in_block = jnp.logical_and(block_of >= 0, block_of < R)
    sel = in_block.astype(F32).astype(BF)
    at_slot = rowsum(jnp.where(in_block, block_of.astype(F32), 0.0))
    one_slot = at_slot == iota((M, LANES), 1).astype(F32)
    gate_col = rowsum(jnp.where(one_slot, pick_nn(sel, grow[:, 0, :]), 0.0))
    g_copy.wait()

    for hf in range(2):
        g2 = gr[hf].reshape(M, HW).astype(F32)
        c2[:, hf * HW : (hf + 1) * HW] = (gate_col * g2).astype(BF)
    gbout_ref[...] = colsum(c2[...].astype(F32))
    gbin_ref[...] = jnp.zeros(gbin_ref.shape, F32)

    FT = 256
    c0 = math.sqrt(2.0 / math.pi)
    MC = KC * R
    half_sems = [next(counter) for _ in range(chunks)]
    dx_half = [next(counter) for _ in range(chunks)]
    e_half = [next(counter) for _ in range(chunks)]
    dx_sems = [next(counter) for _ in range(chunks)]

    def send_dx(c):
        rc = slice(c * MC, (c + 1) * MC)
        kc = pl.ds(c * KC, KC)
        finish(tsend.at[0, rc], dx_half[c])
        own = dot_nt(dh_s[rc], win_s[pl.ds(col, HW), :])
        dxs[c * KC : (c + 1) * KC] = (own + trecv[0, rc].astype(F32)).reshape(KC, R, HW).astype(BF)
        spread(max(1, c * KC), (c + 1) * KC, dxs, dxr, behind, dx_sems[c])
        if c == 0:
            dxr[0] = dxs[0]

    def arrive(c):
        low = max(1, c * KC)
        finish(xr.at[tn, pl.ds(low, (c + 1) * KC - low)], row_sems[c])
        kc = pl.ds(c * KC, KC)
        copy = remote(xr.at[tn, kc], xr.at[tn, kc], half_sems[c], partner)
        copy.start()
        return copy

    copy = arrive(0)
    for c in range(chunks):
        rc = slice(c * MC, (c + 1) * MC)
        copy.wait()
        for hf in range(2):
            x2[rc, hf * HW : (hf + 1) * HW] = xr[hf, c * KC : (c + 1) * KC].reshape(MC, HW)

        def first(i, _):
            f = pl.ds(pl.multiple_of(i * FT, FT), FT)
            h = dot_nn(x2[rc], win_s[:, f]) + ebin_ref[:, f]
            hh = h * h
            th = jnp.tanh(c0 * (h + 0.044715 * (hh * h)))
            half = 0.5 * (1.0 + th)
            a_s[rc, f] = (h * half).astype(BF)
            slope = half + (0.5 * c0) * h * (1.0 - th * th) * (1.0 + (3 * 0.044715) * hh)
            dh = (slope * dot_nt(c2[rc], wout_s[f, :])).astype(BF)
            dh_s[rc, f] = dh
            gbin_ref[:, f] = gbin_ref[:, f] + colsum(dh.astype(F32))
            return 0

        lax.fori_loop(0, F // FT, first, 0)
        tsend[0, rc] = dot_nt(dh_s[rc], win_s[pl.ds(ocol, HW), :]).astype(BF)
        remote(tsend.at[0, rc], trecv.at[0, rc], dx_half[c], partner).start()
        if c + 1 < chunks:
            copy = arrive(c + 1)
        tsend[1, rc] = dot_nn(a_s[rc], wout_s[:, pl.ds(ocol, HW)]).astype(BF)
        remote(tsend.at[1, rc], trecv.at[1, rc], e_half[c], partner).start()
        send_dx(c)

    for c in range(chunks):
        rc = slice(c * MC, (c + 1) * MC)
        own = dot_nn(a_s[rc], wout_s[:, pl.ds(col, HW)])
        finish(tsend.at[1, rc], e_half[c])
        es[c * KC : (c + 1) * KC] = (
            (own + trecv[1, rc].astype(F32) + ebout_ref[:, pl.ds(col, HW)]).reshape(KC, R, HW).astype(BF)
        )
    dgate = rowsum(gr[tn].reshape(M, HW).astype(F32) * es[...].reshape(M, HW).astype(F32))
    dg_rows = jnp.zeros((n, LANES), F32)
    for part in halves(jnp.where(one_slot, dgate, 0.0)):
        dg_rows = dg_rows + dot_tn(sel, part)
    dgst[:, 0, :] = dg_rows
    dg_same, dg_cross, dg_own = next(counter), next(counter), next(counter)
    spread(1, n, dgst, dgr.at[tn], behind, dg_same)
    spread(1, n, dgst, dgr.at[tn], behind, dg_cross, other)
    own_gate = remote(dgst.at[0], dgr.at[tn, 0], dg_own, partner)
    own_gate.start()
    dgr[tn, 0] = dgst[0]
    e_sem = next(counter)
    spread(1, n, es, er, behind, e_sem)
    er[0] = es[0]

    def grads(i, _):
        f = pl.ds(pl.multiple_of(i * FT, FT), FT)
        gwout_ref[f, :] = dot_tn(a_s[:, f], c2[...])
        gwin_ref[:, f] = dot_tn(x2[...], dh_s[:, f])
        return 0

    lax.fori_loop(0, F // FT, grads, 0)

    finish(dgr.at[tn, pl.ds(0, n - 1)], dg_same)
    finish(dgr.at[other, pl.ds(0, n - 1)], dg_cross)
    own_gate.wait()
    dg_all = dgr[0, :, 0, :] + dgr[1, :, 0, :]
    hb0, hb1 = hk0.astype(F32).astype(BF), hk1.astype(F32).astype(BF)
    dg0 = rowsum(jnp.where(slot0 == islot, pick_nn(hb0, dg_all), 0.0))
    dg1 = rowsum(jnp.where(slot1 == islot, pick_nn(hb1, dg_all), 0.0))
    mean_gate = gate0 * dg0 + gate1 * dg1
    dl0, dl1 = gate0 * (dg0 - mean_gate), gate1 * (dg1 - mean_gate)
    dlog = (jnp.where(h0, dl0, 0.0) + jnp.where(h1, dl1, 0.0)).astype(BF)

    for c in range(chunks):
        low = max(1, c * KC)
        finish(dxr.at[pl.ds(low, (c + 1) * KC - low)], dx_sems[c])

    hsend[...] = dot_tn(pt_s[...], dxr[...].reshape(M, HW))
    h_sem = next(counter)
    hc = remote(hsend, hrecv.at[tn], h_sem, partner)
    hc.start()
    hrecv[tn] = hsend[...]
    by_router = dot_nn(dlog, wr)

    hc.wait()
    cot_copy.wait()

    dxn2 = jnp.concatenate([hrecv[0], hrecv[1]], -1) + by_router
    hat2 = hat2_s[...]
    gg2, gb2 = colsum(dxn2 * hat2), colsum(dxn2)
    u = dxn2 * ga2
    dx1 = jnp.concatenate([cotf[0], cotf[1]], -1).astype(F32) + rstd2 * (u - rowmean(u) - hat2 * rowmean(u * hat2))
    dx1_s[...] = dx1
    datt = dx1.astype(BF)
    do = dot_nn(datt, weight(3)).astype(BF)

    first_sems = [next(counter) for _ in range(5)]
    second_sems = [next(counter) for _ in range(5)]

    def to_plane(i, src, dst):
        for j in range(1, plane):
            remote(src.at[:, lax.rem(spot + j, plane)], dst.at[j - 1], first_sems[i], {"expert": in_plane(j)}).start()

    def to_line(i, src, got, mid, dst):
        finish(got, first_sems[i])
        total = src[:, spot].astype(F32)
        for j in range(plane - 1):
            total = total + got[j].astype(F32)
        mid[...] = total.astype(BF)
        for k in range(1, lines):
            there = in_line(k)
            remote(mid.at[there], dst.at[k], second_sems[i], {"expert": there * plane + spot}).start()
        dst[0] = mid[line]

    def gradient(i, value):
        gsend[i] = value.reshape(lines, plane, rows, HW).astype(BF)
        to_plane(i, gsend.at[i], r1.at[i])

    gradient(0, dot_tn(datt, o_s[...]))

    dqs, dks, dvs = [], [], []
    for h in range(heads):
        sl = slice(h * HEAD_DIM, (h + 1) * HEAD_DIM)
        p = p_s[h]
        doh = do[:, sl]
        dp = dot_nt(doh, qkv_s[2, :, sl])
        dvs.append(dot_tn(p.astype(BF), doh))
        ds = (p * (dp - rowsum(p * dp))).astype(BF)
        dqs.append(dot_nn(ds, qkv_s[1, :, sl]) * scale)
        dks.append(dot_tn(ds, qkv_s[0, :, sl]) * scale)
    for i, v in enumerate((dqs, dks, dvs)):
        dqkv_s[i] = jnp.concatenate(v, -1).astype(BF)

    bfpart[0] = (
        dot_nt(dqkv_s[0], weight(0)) + dot_nt(dqkv_s[1], weight(1)) + dot_nt(dqkv_s[2], weight(2))
    ).astype(BF)
    b_sem = next(counter)
    bc = remote(bfpart.at[0], bfpart.at[1], b_sem, partner)
    bc.start()

    for i in range(3):
        gradient(i + 1, dot_tn(xn1_s[...], dqkv_s[i]))

    bc.wait()
    dxn1 = bfpart[0].astype(F32) + bfpart[1].astype(F32)
    hat1 = hat1_s[...]
    gg1, gb1 = colsum(dxn1 * hat1), colsum(dxn1)
    u = dxn1 * ga1
    gx_ref[...] = dx1_s[...] + rstd1 * (u - rowmean(u) - hat1 * rowmean(u * hat1))

    smsend[...] = jnp.zeros(smsend.shape, F32)
    smsend[0:n] = dot_tn(dlog, xn2_s[...])
    smsend[n : n + 1] = gg1
    smsend[n + 1 : n + 2] = gb1
    smsend[n + 2 : n + 3] = gg2
    smsend[n + 3 : n + 4] = gb2
    ssend[...] = smsend[...].T.reshape(lines, plane, rows, ssend.shape[3]).astype(BF)
    to_plane(4, ssend, sr1)
    to_line(0, gsend.at[0], r1.at[0], r2s.at[0], rs_ref.at[0])

    finish(er.at[pl.ds(0, n - 1)], e_sem)

    rows_e = er[...].reshape(M, HW)
    slot_lane = iota((T, M), 1).astype(F32)
    y = x1_s[:, pl.ds(col, HW)]
    y = y + gate0 * dot_nn((slot_lane == pos0).astype(F32).astype(BF), rows_e)
    y = y + gate1 * dot_nn((slot_lane == pos1).astype(F32).astype(BF), rows_e)
    y_ref[...] = y.astype(BF)

    for i in range(1, 4):
        to_line(i, gsend.at[i], r1.at[i], r2s.at[i], rs_ref.at[i])
    to_line(4, ssend, sr1, s2s, rsmall_ref)

    for i in range(4):
        finish(rs_ref.at[i, pl.ds(1, lines - 1)], second_sems[i])
    finish(rsmall_ref.at[pl.ds(1, lines - 1)], second_sems[4])


def last_kernel(
    y_in, gx_in, rs, rsmall, gwin_in, gbin_in, gwout_in, gbout_in,
    y, gx, gq, gk, gv, go, gr, a1, b1, a2, b2, gwin, gbin, gwout, gbout, sem,
):
    copies = [
        pltpu.make_async_copy(src, dst, sem.at[i])
        for i, (src, dst) in enumerate(((gwin_in, gwin), (gwout_in, gwout), (gx_in, gx), (y_in, y)))
    ]
    for c in copies:
        c.start()
    gbin[...] = gbin_in[...]
    gbout[...] = gbout_in[...]
    for i, ref in enumerate((go, gq, gk, gv)):
        ref[...] = jnp.sum(rs[i].astype(F32), 0)
    n, rows = gr.shape
    small = jnp.sum(rsmall[...].astype(F32), 0).T
    gr[...] = small[0:n, 0:rows]
    for i, ref in enumerate((a1, b1, a2, b2)):
        ref[...] = small[n + i : n + i + 1, 0:rows]
    for c in copies:
        c.wait()


def shards(
    block_input, routes, w_query, w_key, w_value, w_output, w_router, norm1_gain, norm1_bias, norm2_gain, norm2_bias,
    expert_in, expert_in_bias, expert_out, expert_out_bias, cotangent,
):
    z = Sizes()
    z.n = lax.axis_size("expert")
    z.T, z.D = block_input.shape
    z.HW = cotangent.shape[1]
    z.F = expert_in.shape[2]
    z.rows = w_query.shape[0]
    z.heads = z.HW // HEAD_DIM
    experts, topk = w_router.shape[1], routes.shape[1]
    cap = max(2, 2 * topk * z.T // experts)
    z.R = -(-cap // 8) * 8
    z.M = z.n * z.R
    z.lines = 4
    z.plane = z.n // z.lines
    z.chunks = CHUNKS
    z.sems = 64
    n, T, D, HW, R, F, rows, M = z.n, z.T, z.D, z.HW, z.R, z.F, z.rows, z.M
    lines, plane = z.lines, z.plane
    wide = -(-(n + 4) // LANES) * LANES
    vm = pl.BlockSpec(memory_space=pltpu.VMEM)
    hbm = pl.BlockSpec(memory_space=pl.ANY)
    out_shape = (
        jax.ShapeDtypeStruct((T, HW), BF),
        jax.ShapeDtypeStruct((T, D), F32),
        jax.ShapeDtypeStruct((4, lines, rows, HW), BF),
        jax.ShapeDtypeStruct((lines, rows, wide), BF),
        jax.ShapeDtypeStruct((D, F), F32),
        jax.ShapeDtypeStruct((1, F), F32),
        jax.ShapeDtypeStruct((F, D), F32),
        jax.ShapeDtypeStruct((1, D), F32),
    )
    V = pltpu.VMEM
    tp = -(-T // LANES) * LANES
    scratch = [
        V((D, F), F32), V((F, D), F32), V((D, F), BF), V((F, D), BF), V((wide, LANES), F32), V((8, tp), F32), V((tp, LANES), F32),
        V((4, rows, HW), BF), V((n, 4, rows, HW), BF), V((rows, wide), BF), V((n, rows, wide), BF),
        V((M, T), BF), V((T, D), F32), V((T, D), BF), V((3, T, HW), BF), V((z.heads, T, T), F32),
        V((T, HW), BF), V((T, D), BF), V((T, D), BF),
        V((T, D), F32), V((T, D), F32), V((T, D), BF), V((2, T, HW), BF),
        V((n, R, HW), BF), V((2, n, R, HW), BF), V((n, R, HW), BF), V((2, n, R, HW), BF),
        V((n, 1, LANES), F32), V((n, 1, LANES), F32), V((M, D), BF), V((M, D), BF), V((M, F), BF), V((M, F), BF),
        V((2, M, HW), BF), V((2, M, HW), BF), V((n, R, HW), BF), V((n, R, HW), BF), V((n, R, HW), BF), V((n, R, HW), BF),
        V((n, 1, LANES), F32), V((2, n, 1, LANES), F32), V((T, HW), F32), V((2, T, HW), F32), V((T, D), F32), V((3, T, HW), BF),
        V((4, lines, plane, rows, HW), BF), V((4, plane - 1, lines, rows, HW), BF), V((4, lines, rows, HW), BF), V((wide, D), F32),
        V((lines, plane, rows, wide), BF), V((plane - 1, lines, rows, wide), BF), V((lines, rows, wide), BF), V((2, T, D), BF),
        pltpu.SemaphoreType.DMA((2,)), pltpu.SemaphoreType.DMA((z.sems,)), pltpu.SemaphoreType.DMA((z.sems,)),
    ]
    kept = [pltpu.VMEM(v.shape, v.dtype) for v in out_shape]
    done = pl.pallas_call(
        functools.partial(block_kernel, z),
        out_shape=kept,
        in_specs=[vm] * 14 + [pl.BlockSpec(memory_space=pltpu.HBM)] * 2,
        out_specs=[vm] * 8,
        scratch_shapes=scratch,
        compiler_params=pltpu.CompilerParams(collective_id=0, has_side_effects=True, vmem_limit_bytes=40 << 20),
        name="block",
    )(
        *(
            pltpu.with_memory_space_constraint(v, pltpu.HBM)
            for v in (
                block_input, routes.T, w_query, w_key, w_value, w_output.T, w_router.T,
                norm1_gain[None], norm1_bias[None], norm2_gain[None], norm2_bias[None],
                expert_in_bias, expert_out_bias, cotangent, expert_in, expert_out,
            )
        )
    )
    square = jax.ShapeDtypeStruct((rows, HW), F32)
    line = jax.ShapeDtypeStruct((1, rows), F32)
    last_shape = (
        out_shape[0], out_shape[1], square, square, square, square, jax.ShapeDtypeStruct((n, rows), F32), line, line, line, line,
        out_shape[4], out_shape[5], out_shape[6], out_shape[7],
    )
    y, gx, gq, gk, gv, go, gr, a1, b1, a2, b2, gwin, gbin, gwout, gbout = pl.pallas_call(
        last_kernel,
        out_shape=last_shape,
        in_specs=[vm] * 8,
        out_specs=[hbm] * 2 + [vm] * 9 + [hbm, vm, hbm, vm],
        scratch_shapes=[pltpu.SemaphoreType.DMA((4,))],
        compiler_params=pltpu.CompilerParams(vmem_limit_bytes=8 << 20),
        name="last",
    )(*done)
    return (y, gx, gq, gk, gv, go.T, gr.T, a1[0], b1[0], a2[0], b2[0], gwin[None], gbin, gwout[None], gbout)


def solution(mesh):
    row, col = P("expert", None), P("expert", "tensor")
    vec = P("expert")
    in_specs = (
        row, row, col, col, col, P("tensor", "expert"), row, vec, vec, vec, vec,
        P("expert", None, "tensor"), col, P("expert", "tensor", None), row, col,
    )
    out_specs = (
        col, row, col, col, col, P("tensor", "expert"), row, vec, vec, vec, vec,
        P("expert", None, "tensor"), col, P("expert", "tensor", None), row,
    )
    return jax.shard_map(shards, mesh=mesh, in_specs=in_specs, out_specs=out_specs, check_vma=False)
```

```python
import functools
import math

import jax
import jax.numpy as jnp
from jax import lax
from jax.experimental import pallas as pl
from jax.experimental.pallas import tpu as pltpu
from jax.sharding import PartitionSpec as P

HEAD_DIM = 64
EPS = 1e-06
MESH = pl.DeviceIdType.MESH
BF = jnp.bfloat16
F32 = jnp.float32
LANES = 128
CHUNKS = 4
EARLY = 2


def dot_nn(a, b):
    return lax.dot_general(a, b, (((1,), (0,)), ((), ())), preferred_element_type=F32)


def dot_nt(a, b):
    return lax.dot_general(a, b, (((1,), (1,)), ((), ())), preferred_element_type=F32)


def dot_tn(a, b):
    return lax.dot_general(a, b, (((0,), (0,)), ((), ())), preferred_element_type=F32)


def halves(v):
    first = v.astype(BF)
    rest = v - first.astype(F32)
    second = rest.astype(BF)
    return first, second, (rest - second.astype(F32)).astype(BF)


def pick_nn(select, v):
    a, b, c = halves(v)
    return dot_nn(select, a) + dot_nn(select, b) + dot_nn(select, c)


def colsum(v):
    return jnp.sum(v, axis=0, keepdims=True)


def rowmean(v):
    return jnp.mean(v, -1, keepdims=True)


def rowsum(v):
    return jnp.sum(v, -1, keepdims=True)


def iota(shape, axis):
    return lax.broadcasted_iota(jnp.int32, shape, axis)


class Sizes:
    pass


def block_kernel(
    z,
    x_ref, routes_ref, wq_ref, wk_ref, wv_ref, wo_ref, wr_ref, ga1_ref, be1_ref, ga2_ref, be2_ref, ebin_ref, ebout_ref, cot_ref,
    win_hbm, wout_hbm,
    y_ref, gx_ref, rs_ref, rsmall_ref, gwin_ref, gbin_ref, gwout_ref, gbout_ref,
    win32, wout32, win_s, wout_s, square, flat, pads,
    wst, wg, smst, smg, pt_s, hat1_s, xn1_s, qkv_s, p_s, o_s, parts, partr,
    x1_s, hat2_s, xn2_s, cotf, gs, gr, xs, xr, growst, grow, x2, c2, a_s, dh_s,
    tsend, trecv, es, er, dxs, dxr, dgst, dgr, hsend, hrecv, dx1_s, dqkv_s, gsend, r1, r2s, smsend, ssend, sr1, s2s, bfpart,
    hbm_sem, send_sem, recv_sem,
):
    n, T, D, HW, R, F, rows, M, heads = z.n, z.T, z.D, z.HW, z.R, z.F, z.rows, z.M, z.heads
    lines, plane, chunks = z.lines, z.plane, z.chunks
    KC = n // chunks
    me = lax.axis_index("expert")
    tn = lax.axis_index("tensor")
    other = 1 - tn
    partner = {"tensor": other}
    line, spot = me // plane, lax.rem(me, plane)
    col = pl.multiple_of(tn * HW, HW)
    ocol = pl.multiple_of(other * HW, HW)
    counter = iter(range(z.sems))

    low_bit, high_bit = lax.rem(line, 2), line // 2

    def other_line(c):
        a, b = lax.rem(c, 2), c // 2
        return (high_bit + b - 2 * high_bit * b) * 2 + low_bit + a - 2 * low_bit * a

    def ahead(k):
        return other_line(lax.rem(k, lines)) * plane + lax.rem(spot + k // lines, plane)

    def behind(k):
        return other_line(lax.rem(k, lines)) * plane + lax.rem(spot - k // lines + plane, plane)

    def in_line(k):
        return lax.rem(line + k, lines)

    def in_plane(j):
        return line * plane + lax.rem(spot + j, plane)

    barrier = pltpu.get_barrier_semaphore()

    def greet(k, _):
        pl.semaphore_signal(barrier, inc=1, device_id={"expert": ahead(k)}, device_id_type=MESH)
        return 0

    lax.fori_loop(1, n, greet, 0)
    pl.semaphore_signal(barrier, inc=1, device_id=partner, device_id_type=MESH)

    win_copy = pltpu.make_async_copy(win_hbm.at[0], win32, hbm_sem.at[0])
    wout_copy = pltpu.make_async_copy(wout_hbm.at[0], wout32, hbm_sem.at[1])
    win_copy.start()
    wout_copy.start()

    def remote(src, dst, i, dev):
        return pltpu.make_async_remote_copy(
            src_ref=src, dst_ref=dst, send_sem=send_sem.at[i], recv_sem=recv_sem.at[i], device_id=dev, device_id_type=MESH
        )

    def spread(low, high, src, dst, to, i, core=None):
        def step(at, _):
            k = high - 1 - at
            dev = {"expert": to(k)}
            if core is not None:
                dev["tensor"] = core
            remote(src.at[k], dst.at[k], i, dev).start()
            return 0

        lax.fori_loop(0, high - low, step, 0)

    def finish(ref, i):
        d = remote(ref, ref, i, partner)
        d.wait_send()
        d.wait_recv()

    wst[0] = wq_ref[...].astype(BF)
    wst[1] = wk_ref[...].astype(BF)
    wst[2] = wv_ref[...].astype(BF)
    wst[3] = wo_ref[...].astype(BF)
    square[...] = jnp.zeros(square.shape, F32)
    square[0:n, 0:rows] = wr_ref[...]
    for i, ref in enumerate((ga1_ref, be1_ref, ga2_ref, be2_ref)):
        square[n + i : n + i + 1, 0:rows] = ref[...]
    smst[...] = square[...].T[0:rows].astype(BF)
    wg[me] = wst[...]
    smg[me] = smst[...]

    flat[0:2, 0:T] = routes_ref[...].astype(F32)
    r = flat[...].T
    r0, r1_ = r[0:T, 0:1], r[0:T, 1:2]
    ie = iota((T, n), 1).astype(F32)
    h0, h1 = r0 == ie, r1_ == ie
    above = [(ie >= i * plane).astype(F32) for i in range(1, lines)]
    line_of = sum(above)
    high_of = above[1]
    low_of = line_of - 2 * high_of
    low_f, high_f = low_bit.astype(F32), high_bit.astype(F32)
    turn = ie - line_of * plane - spot.astype(F32)
    turn = jnp.where(turn < 0, turn + plane, turn)
    place = (high_of - high_f) ** 2 * 2 + (low_of - low_f) ** 2 + turn * lines
    k0, k1 = rowsum(jnp.where(h0, place, 0.0)), rowsum(jnp.where(h1, place, 0.0))
    hk0, hk1 = k0 == ie, k1 == ie
    hit = jnp.logical_or(hk0, hk1).astype(F32).astype(BF)
    tri = (iota((T, T), 0) > iota((T, T), 1)).astype(F32).astype(BF)
    count = dot_nn(tri, hit)
    slot0 = rowsum(jnp.where(hk0, count, 0.0))
    slot1 = rowsum(jnp.where(hk1, count, 0.0))
    pos0 = k0 * R + slot0
    pos1 = k1 * R + slot1
    pads[...] = jnp.full(pads.shape, -1.0, F32)
    pads[0:T, 0:1] = pos0
    pads[0:T, 1:2] = pos1
    post = pads[...].T
    slots = iota((M, T), 0).astype(F32)
    pt_s[...] = jnp.logical_or(slots == post[0:1, 0:T], slots == post[1:2, 0:T]).astype(F32).astype(BF)

    gs[...] = dot_nn(pt_s[...], cot_ref[...]).reshape(n, R, HW).astype(BF)
    cotf[tn] = cot_ref[...]

    x = x_ref[...].astype(F32)
    center = x - rowmean(x)
    rstd1 = lax.rsqrt(rowmean(center * center) + EPS)
    hat1_s[...] = center * rstd1

    pl.semaphore_wait(barrier, n)

    line_sems = [next(counter) for _ in range(lines - 1)]
    small_sems = [next(counter) for _ in range(lines - 1)]
    plane_sem, small_plane_sem = next(counter), next(counter)

    def share(block):
        for j in range(1, plane):
            dev = {"expert": in_plane(j)}
            remote(wg.at[block], wg.at[block], plane_sem, dev).start()
            remote(smg.at[block], smg.at[block], small_plane_sem, dev).start()

    for k in range(1, lines):
        dev = {"expert": in_line(k) * plane + spot}
        remote(smst, smg.at[me], small_sems[k - 1], dev).start()
        remote(wst, wg.at[me], line_sems[k - 1], dev).start()
    share(me)
    cot_sem = next(counter)
    cot_copy = remote(cot_ref, cotf.at[tn], cot_sem, partner)
    cot_copy.start()

    gr[tn, 0] = gs[0]
    win_copy.wait()
    win_s[...] = win32[...].astype(BF)
    wout_copy.wait()
    wout_s[...] = wout32[...].astype(BF)

    for k in range(1, lines):
        finish(wst, line_sems[k - 1])
        finish(smst, small_sems[k - 1])
        share(in_line(lines - k) * plane + spot)

    finish(smg.at[pl.ds(0, (plane - 1) * lines)], small_plane_sem)
    small = smg[...].astype(F32).reshape(n * rows, smg.shape[2]).T
    ga1, be1 = small[n : n + 1], small[n + 1 : n + 2]
    ga2, be2 = small[n + 2 : n + 3], small[n + 3 : n + 4]
    wr = small[0:n].astype(BF)
    xn1 = (hat1_s[...] * ga1 + be1).astype(BF)
    xn1_s[...] = xn1

    finish(wg.at[pl.ds(0, (plane - 1) * lines)], plane_sem)
    scale = 1.0 / math.sqrt(HEAD_DIM)

    g_sems = [next(counter) for _ in range(chunks)]

    def send_cotangent(c):
        spread(max(1, c * KC), (c + 1) * KC, gs, gr.at[tn], ahead, g_sems[c])

    for c in range(EARLY):
        send_cotangent(c)

    def weight(i):
        return wg[:, i].reshape(D, HW)

    for i in range(3):
        qkv_s[i] = dot_nn(xn1, weight(i)).astype(BF)

    outs = []
    for h in range(heads):
        sl = slice(h * HEAD_DIM, (h + 1) * HEAD_DIM)
        s = dot_nt(qkv_s[0, :, sl], qkv_s[1, :, sl]) * scale
        ex = jnp.exp(s - jnp.max(s, -1, keepdims=True))
        p = ex / rowsum(ex)
        p_s[h] = p
        outs.append(dot_nn(p.astype(BF), qkv_s[2, :, sl]))
    o_s[...] = jnp.concatenate(outs, -1).astype(BF)

    parts[...] = dot_nt(o_s[...], weight(3)).astype(BF)
    part_sem = next(counter)
    part_copy = remote(parts, partr, part_sem, partner)
    part_copy.start()

    part_copy.wait()
    x1 = x_ref[...].astype(F32) + (parts[...].astype(F32) + partr[...].astype(F32))
    x1_s[...] = x1

    center = x1 - rowmean(x1)
    rstd2 = lax.rsqrt(rowmean(center * center) + EPS)
    hat2 = center * rstd2
    hat2_s[...] = hat2
    xn2 = (hat2 * ga2 + be2).astype(BF)
    xn2_s[...] = xn2
    xs[...] = dot_nn(pt_s[...], xn2_s[:, pl.ds(col, HW)]).reshape(n, R, HW).astype(BF)

    row_sems = [next(counter) for _ in range(chunks)]

    def send_rows(c):
        spread(max(1, c * KC), (c + 1) * KC, xs, xr.at[tn], ahead, row_sems[c])

    send_rows(0)
    xr[tn, 0] = xs[0]

    logits = dot_nt(xn2, wr)
    l0 = rowsum(jnp.where(h0, logits, 0.0))
    l1 = rowsum(jnp.where(h1, logits, 0.0))
    top = jnp.maximum(l0, l1)
    e0, e1 = jnp.exp(l0 - top), jnp.exp(l1 - top)
    gate0, gate1 = e0 / (e0 + e1), e1 / (e0 + e1)
    islot = iota((T, LANES), 1).astype(F32)
    at0 = (slot0 == islot).astype(F32).astype(BF)
    at1 = (slot1 == islot).astype(F32).astype(BF)
    gate_rows = jnp.zeros((n, LANES), F32)
    for hh, gg, at in ((hk0, gate0, at0), (hk1, gate1, at1)):
        for part in halves(jnp.where(hh, gg, 0.0)):
            gate_rows = gate_rows + dot_tn(part, at)
    growst[:, 0, :] = gate_rows
    gate_sem = next(counter)
    spread(1, n, growst, grow, ahead, gate_sem)
    grow[0] = growst[0]
    for c in range(1, chunks):
        if c >= EARLY:
            send_cotangent(c)
        send_rows(c)

    finish(grow.at[pl.ds(0, n - 1)], gate_sem)
    block_of = iota((M, n), 0) - iota((M, n), 1) * R
    in_block = jnp.logical_and(block_of >= 0, block_of < R)
    sel = in_block.astype(F32).astype(BF)
    at_slot = rowsum(jnp.where(in_block, block_of.astype(F32), 0.0))
    one_slot = at_slot == iota((M, LANES), 1).astype(F32)
    gate_col = rowsum(jnp.where(one_slot, pick_nn(sel, grow[:, 0, :]), 0.0))

    gbout_ref[...] = jnp.zeros(gbout_ref.shape, F32)
    gbin_ref[...] = jnp.zeros(gbin_ref.shape, F32)

    FT = 256
    c0 = math.sqrt(2.0 / math.pi)
    MC = KC * R
    half_sems = [next(counter) for _ in range(chunks)]
    g_half_sems = [next(counter) for _ in range(chunks)]
    dx_half = [next(counter) for _ in range(chunks)]
    e_half = [next(counter) for _ in range(chunks)]
    dx_sems = [next(counter) for _ in range(chunks)]

    def send_dx(c):
        rc = slice(c * MC, (c + 1) * MC)
        kc = pl.ds(c * KC, KC)
        finish(tsend.at[0, rc], dx_half[c])
        own = dot_nt(dh_s[rc], win_s[pl.ds(col, HW), :])
        dxs[c * KC : (c + 1) * KC] = (own + trecv[0, rc].astype(F32)).reshape(KC, R, HW).astype(BF)
        spread(max(1, c * KC), (c + 1) * KC, dxs, dxr, behind, dx_sems[c])
        if c == 0:
            dxr[0] = dxs[0]

    def arrive(c):
        low = max(1, c * KC)
        kc = pl.ds(c * KC, KC)
        copies = []
        for buf, came, half in ((gr, g_sems, g_half_sems), (xr, row_sems, half_sems)):
            finish(buf.at[tn, pl.ds(low, (c + 1) * KC - low)], came[c])
            copies.append(remote(buf.at[tn, kc], buf.at[tn, kc], half[c], partner))
            copies[-1].start()
        return copies

    copies = arrive(0)
    for c in range(chunks):
        rc = slice(c * MC, (c + 1) * MC)
        for copy in copies:
            copy.wait()
        for hf in range(2):
            wide = slice(hf * HW, (hf + 1) * HW)
            x2[rc, wide] = xr[hf, c * KC : (c + 1) * KC].reshape(MC, HW)
            g2 = gr[hf, c * KC : (c + 1) * KC].reshape(MC, HW).astype(F32)
            c2[rc, wide] = (gate_col[rc] * g2).astype(BF)
        gbout_ref[...] = gbout_ref[...] + colsum(c2[rc].astype(F32))

        def first(i, _):
            f = pl.ds(pl.multiple_of(i * FT, FT), FT)
            h = dot_nn(x2[rc], win_s[:, f]) + ebin_ref[:, f]
            hh = h * h
            th = jnp.tanh(c0 * (h + 0.044715 * (hh * h)))
            half = 0.5 * (1.0 + th)
            a_s[rc, f] = (h * half).astype(BF)
            slope = half + (0.5 * c0) * h * (1.0 - th * th) * (1.0 + (3 * 0.044715) * hh)
            dh = (slope * dot_nt(c2[rc], wout_s[f, :])).astype(BF)
            dh_s[rc, f] = dh
            gbin_ref[:, f] = gbin_ref[:, f] + colsum(dh.astype(F32))
            return 0

        lax.fori_loop(0, F // FT, first, 0)
        tsend[0, rc] = dot_nt(dh_s[rc], win_s[pl.ds(ocol, HW), :]).astype(BF)
        remote(tsend.at[0, rc], trecv.at[0, rc], dx_half[c], partner).start()
        if c + 1 < chunks:
            copies = arrive(c + 1)
        tsend[1, rc] = dot_nn(a_s[rc], wout_s[:, pl.ds(ocol, HW)]).astype(BF)
        remote(tsend.at[1, rc], trecv.at[1, rc], e_half[c], partner).start()
        send_dx(c)

    for c in range(chunks):
        rc = slice(c * MC, (c + 1) * MC)
        own = dot_nn(a_s[rc], wout_s[:, pl.ds(col, HW)])
        finish(tsend.at[1, rc], e_half[c])
        es[c * KC : (c + 1) * KC] = (
            (own + trecv[1, rc].astype(F32) + ebout_ref[:, pl.ds(col, HW)]).reshape(KC, R, HW).astype(BF)
        )
    dgate = rowsum(gr[tn].reshape(M, HW).astype(F32) * es[...].reshape(M, HW).astype(F32))
    dg_rows = jnp.zeros((n, LANES), F32)
    for part in halves(jnp.where(one_slot, dgate, 0.0)):
        dg_rows = dg_rows + dot_tn(sel, part)
    dgst[:, 0, :] = dg_rows
    dg_same, dg_cross, dg_own = next(counter), next(counter), next(counter)
    spread(1, n, dgst, dgr.at[tn], behind, dg_same)
    spread(1, n, dgst, dgr.at[tn], behind, dg_cross, other)
    own_gate = remote(dgst.at[0], dgr.at[tn, 0], dg_own, partner)
    own_gate.start()
    dgr[tn, 0] = dgst[0]
    def grads(i, _):
        f = pl.ds(pl.multiple_of(i * FT, FT), FT)
        gwout_ref[f, :] = dot_tn(a_s[:, f], c2[...])
        gwin_ref[:, f] = dot_tn(x2[...], dh_s[:, f])
        return 0

    lax.fori_loop(0, F // FT, grads, 0)
    e_sem = next(counter)
    spread(1, n, es, er, behind, e_sem)
    er[0] = es[0]

    finish(dgr.at[tn, pl.ds(0, n - 1)], dg_same)
    finish(dgr.at[other, pl.ds(0, n - 1)], dg_cross)
    own_gate.wait()
    dg_all = dgr[0, :, 0, :] + dgr[1, :, 0, :]
    hb0, hb1 = hk0.astype(F32).astype(BF), hk1.astype(F32).astype(BF)
    dg0 = rowsum(jnp.where(slot0 == islot, pick_nn(hb0, dg_all), 0.0))
    dg1 = rowsum(jnp.where(slot1 == islot, pick_nn(hb1, dg_all), 0.0))
    mean_gate = gate0 * dg0 + gate1 * dg1
    dl0, dl1 = gate0 * (dg0 - mean_gate), gate1 * (dg1 - mean_gate)
    dlog = (jnp.where(h0, dl0, 0.0) + jnp.where(h1, dl1, 0.0)).astype(BF)

    for c in range(chunks):
        low = max(1, c * KC)
        finish(dxr.at[pl.ds(low, (c + 1) * KC - low)], dx_sems[c])

    hsend[...] = dot_tn(pt_s[...], dxr[...].reshape(M, HW))
    h_sem = next(counter)
    hc = remote(hsend, hrecv.at[tn], h_sem, partner)
    hc.start()
    hrecv[tn] = hsend[...]
    by_router = dot_nn(dlog, wr)

    hc.wait()
    cot_copy.wait()

    dxn2 = jnp.concatenate([hrecv[0], hrecv[1]], -1) + by_router
    hat2 = hat2_s[...]
    gg2, gb2 = colsum(dxn2 * hat2), colsum(dxn2)
    u = dxn2 * ga2
    dx1 = jnp.concatenate([cotf[0], cotf[1]], -1).astype(F32) + rstd2 * (u - rowmean(u) - hat2 * rowmean(u * hat2))
    dx1_s[...] = dx1
    datt = dx1.astype(BF)
    do = dot_nn(datt, weight(3)).astype(BF)

    first_sems = [next(counter) for _ in range(5)]
    second_sems = [next(counter) for _ in range(5)]

    def to_plane(i, src, dst):
        for j in range(1, plane):
            remote(src.at[:, lax.rem(spot + j, plane)], dst.at[j - 1], first_sems[i], {"expert": in_plane(j)}).start()

    def to_line(i, src, got, mid, dst):
        finish(got, first_sems[i])
        total = src[:, spot].astype(F32)
        for j in range(plane - 1):
            total = total + got[j].astype(F32)
        mid[...] = total.astype(BF)
        for k in range(1, lines):
            there = in_line(k)
            remote(mid.at[there], dst.at[k], second_sems[i], {"expert": there * plane + spot}).start()
        dst[0] = mid[line]

    def gradient(i, value):
        gsend[i] = value.reshape(lines, plane, rows, HW).astype(BF)
        to_plane(i, gsend.at[i], r1.at[i])

    gradient(0, dot_tn(datt, o_s[...]))

    dqs, dks, dvs = [], [], []
    for h in range(heads):
        sl = slice(h * HEAD_DIM, (h + 1) * HEAD_DIM)
        p = p_s[h]
        doh = do[:, sl]
        dp = dot_nt(doh, qkv_s[2, :, sl])
        dvs.append(dot_tn(p.astype(BF), doh))
        ds = (p * (dp - rowsum(p * dp))).astype(BF)
        dqs.append(dot_nn(ds, qkv_s[1, :, sl]) * scale)
        dks.append(dot_tn(ds, qkv_s[0, :, sl]) * scale)
    for i, v in enumerate((dqs, dks, dvs)):
        dqkv_s[i] = jnp.concatenate(v, -1).astype(BF)

    bfpart[0] = (
        dot_nt(dqkv_s[0], weight(0)) + dot_nt(dqkv_s[1], weight(1)) + dot_nt(dqkv_s[2], weight(2))
    ).astype(BF)
    b_sem = next(counter)
    bc = remote(bfpart.at[0], bfpart.at[1], b_sem, partner)
    bc.start()

    for i in range(3):
        gradient(i + 1, dot_tn(xn1_s[...], dqkv_s[i]))

    bc.wait()
    dxn1 = bfpart[0].astype(F32) + bfpart[1].astype(F32)
    hat1 = hat1_s[...]
    gg1, gb1 = colsum(dxn1 * hat1), colsum(dxn1)
    u = dxn1 * ga1
    gx_ref[...] = dx1_s[...] + rstd1 * (u - rowmean(u) - hat1 * rowmean(u * hat1))

    smsend[...] = jnp.zeros(smsend.shape, F32)
    smsend[0:n] = dot_tn(dlog, xn2_s[...])
    smsend[n : n + 1] = gg1
    smsend[n + 1 : n + 2] = gb1
    smsend[n + 2 : n + 3] = gg2
    smsend[n + 3 : n + 4] = gb2
    ssend[...] = smsend[...].T.reshape(lines, plane, rows, ssend.shape[3]).astype(BF)
    to_plane(4, ssend, sr1)
    to_line(0, gsend.at[0], r1.at[0], r2s.at[0], rs_ref.at[0])

    finish(er.at[pl.ds(0, n - 1)], e_sem)

    rows_e = er[...].reshape(M, HW)
    slot_lane = iota((T, M), 1).astype(F32)
    y = x1_s[:, pl.ds(col, HW)]
    y = y + gate0 * dot_nn((slot_lane == pos0).astype(F32).astype(BF), rows_e)
    y = y + gate1 * dot_nn((slot_lane == pos1).astype(F32).astype(BF), rows_e)
    y_ref[...] = y.astype(BF)

    for i in range(1, 4):
        to_line(i, gsend.at[i], r1.at[i], r2s.at[i], rs_ref.at[i])
    to_line(4, ssend, sr1, s2s, rsmall_ref)

    for i in range(4):
        finish(rs_ref.at[i, pl.ds(1, lines - 1)], second_sems[i])
    finish(rsmall_ref.at[pl.ds(1, lines - 1)], second_sems[4])


def last_kernel(
    y_in, gx_in, rs, rsmall, gwin_in, gbin_in, gwout_in, gbout_in,
    y, gx, gq, gk, gv, go, gr, a1, b1, a2, b2, gwin, gbin, gwout, gbout, sem,
):
    copies = [
        pltpu.make_async_copy(src, dst, sem.at[i])
        for i, (src, dst) in enumerate(((gwin_in, gwin), (gwout_in, gwout), (gx_in, gx), (y_in, y)))
    ]
    for c in copies:
        c.start()
    gbin[...] = gbin_in[...]
    gbout[...] = gbout_in[...]
    for i, ref in enumerate((go, gq, gk, gv)):
        ref[...] = jnp.sum(rs[i].astype(F32), 0)
    n, rows = gr.shape
    small = jnp.sum(rsmall[...].astype(F32), 0).T
    gr[...] = small[0:n, 0:rows]
    for i, ref in enumerate((a1, b1, a2, b2)):
        ref[...] = small[n + i : n + i + 1, 0:rows]
    for c in copies:
        c.wait()


def shards(
    block_input, routes, w_query, w_key, w_value, w_output, w_router, norm1_gain, norm1_bias, norm2_gain, norm2_bias,
    expert_in, expert_in_bias, expert_out, expert_out_bias, cotangent,
):
    z = Sizes()
    z.n = lax.axis_size("expert")
    z.T, z.D = block_input.shape
    z.HW = cotangent.shape[1]
    z.F = expert_in.shape[2]
    z.rows = w_query.shape[0]
    z.heads = z.HW // HEAD_DIM
    experts, topk = w_router.shape[1], routes.shape[1]
    cap = max(2, 2 * topk * z.T // experts)
    z.R = -(-cap // 8) * 8
    z.M = z.n * z.R
    z.lines = 4
    z.plane = z.n // z.lines
    z.chunks = CHUNKS
    z.sems = 64
    n, T, D, HW, R, F, rows, M = z.n, z.T, z.D, z.HW, z.R, z.F, z.rows, z.M
    lines, plane = z.lines, z.plane
    wide = -(-(n + 4) // LANES) * LANES
    vm = pl.BlockSpec(memory_space=pltpu.VMEM)
    hbm = pl.BlockSpec(memory_space=pl.ANY)
    out_shape = (
        jax.ShapeDtypeStruct((T, HW), BF),
        jax.ShapeDtypeStruct((T, D), F32),
        jax.ShapeDtypeStruct((4, lines, rows, HW), BF),
        jax.ShapeDtypeStruct((lines, rows, wide), BF),
        jax.ShapeDtypeStruct((D, F), F32),
        jax.ShapeDtypeStruct((1, F), F32),
        jax.ShapeDtypeStruct((F, D), F32),
        jax.ShapeDtypeStruct((1, D), F32),
    )
    V = pltpu.VMEM
    tp = -(-T // LANES) * LANES
    scratch = [
        V((D, F), F32), V((F, D), F32), V((D, F), BF), V((F, D), BF), V((wide, LANES), F32), V((8, tp), F32), V((tp, LANES), F32),
        V((4, rows, HW), BF), V((n, 4, rows, HW), BF), V((rows, wide), BF), V((n, rows, wide), BF),
        V((M, T), BF), V((T, D), F32), V((T, D), BF), V((3, T, HW), BF), V((z.heads, T, T), F32),
        V((T, HW), BF), V((T, D), BF), V((T, D), BF),
        V((T, D), F32), V((T, D), F32), V((T, D), BF), V((2, T, HW), BF),
        V((n, R, HW), BF), V((2, n, R, HW), BF), V((n, R, HW), BF), V((2, n, R, HW), BF),
        V((n, 1, LANES), F32), V((n, 1, LANES), F32), V((M, D), BF), V((M, D), BF), V((M, F), BF), V((M, F), BF),
        V((2, M, HW), BF), V((2, M, HW), BF), V((n, R, HW), BF), V((n, R, HW), BF), V((n, R, HW), BF), V((n, R, HW), BF),
        V((n, 1, LANES), F32), V((2, n, 1, LANES), F32), V((T, HW), F32), V((2, T, HW), F32), V((T, D), F32), V((3, T, HW), BF),
        V((4, lines, plane, rows, HW), BF), V((4, plane - 1, lines, rows, HW), BF), V((4, lines, rows, HW), BF), V((wide, D), F32),
        V((lines, plane, rows, wide), BF), V((plane - 1, lines, rows, wide), BF), V((lines, rows, wide), BF), V((2, T, D), BF),
        pltpu.SemaphoreType.DMA((2,)), pltpu.SemaphoreType.DMA((z.sems,)), pltpu.SemaphoreType.DMA((z.sems,)),
    ]
    kept = [pltpu.VMEM(v.shape, v.dtype) for v in out_shape]
    done = pl.pallas_call(
        functools.partial(block_kernel, z),
        out_shape=kept,
        in_specs=[vm] * 14 + [pl.BlockSpec(memory_space=pltpu.HBM)] * 2,
        out_specs=[vm] * 8,
        scratch_shapes=scratch,
        compiler_params=pltpu.CompilerParams(collective_id=0, has_side_effects=True, vmem_limit_bytes=40 << 20),
        name="block",
    )(
        *(
            pltpu.with_memory_space_constraint(v, pltpu.HBM)
            for v in (
                block_input, routes.T, w_query, w_key, w_value, w_output.T, w_router.T,
                norm1_gain[None], norm1_bias[None], norm2_gain[None], norm2_bias[None],
                expert_in_bias, expert_out_bias, cotangent, expert_in, expert_out,
            )
        )
    )
    square = jax.ShapeDtypeStruct((rows, HW), F32)
    line = jax.ShapeDtypeStruct((1, rows), F32)
    last_shape = (
        out_shape[0], out_shape[1], square, square, square, square, jax.ShapeDtypeStruct((n, rows), F32), line, line, line, line,
        out_shape[4], out_shape[5], out_shape[6], out_shape[7],
    )
    y, gx, gq, gk, gv, go, gr, a1, b1, a2, b2, gwin, gbin, gwout, gbout = pl.pallas_call(
        last_kernel,
        out_shape=last_shape,
        in_specs=[vm] * 8,
        out_specs=[hbm] * 2 + [vm] * 9 + [hbm, vm, hbm, vm],
        scratch_shapes=[pltpu.SemaphoreType.DMA((4,))],
        compiler_params=pltpu.CompilerParams(vmem_limit_bytes=8 << 20),
        name="last",
    )(*done)
    return (y, gx, gq, gk, gv, go.T, gr.T, a1[0], b1[0], a2[0], b2[0], gwin[None], gbin, gwout[None], gbout)


def solution(mesh):
    row, col = P("expert", None), P("expert", "tensor")
    vec = P("expert")
    in_specs = (
        row, row, col, col, col, P("tensor", "expert"), row, vec, vec, vec, vec,
        P("expert", None, "tensor"), col, P("expert", "tensor", None), row, col,
    )
    out_specs = (
        col, row, col, col, col, P("tensor", "expert"), row, vec, vec, vec, vec,
        P("expert", None, "tensor"), col, P("expert", "tensor", None), row,
    )
    return jax.shard_map(shards, mesh=mesh, in_specs=in_specs, out_specs=out_specs, check_vma=False)
```

```python
import functools
import math

import jax
import jax.numpy as jnp
from jax import lax
from jax.experimental import pallas as pl
from jax.experimental.pallas import tpu as pltpu
from jax.sharding import PartitionSpec as P

HEAD_DIM = 64
EPS = 1e-06
MESH = pl.DeviceIdType.MESH
BF = jnp.bfloat16
F32 = jnp.float32
LANES = 128
CHUNKS = 4
EARLY = 3


def dot_nn(a, b):
    return lax.dot_general(a, b, (((1,), (0,)), ((), ())), preferred_element_type=F32)


def dot_nt(a, b):
    return lax.dot_general(a, b, (((1,), (1,)), ((), ())), preferred_element_type=F32)


def dot_tn(a, b):
    return lax.dot_general(a, b, (((0,), (0,)), ((), ())), preferred_element_type=F32)


def halves(v):
    first = v.astype(BF)
    rest = v - first.astype(F32)
    second = rest.astype(BF)
    return first, second, (rest - second.astype(F32)).astype(BF)


def pick_nn(select, v):
    a, b, c = halves(v)
    return dot_nn(select, a) + dot_nn(select, b) + dot_nn(select, c)


def colsum(v):
    return jnp.sum(v, axis=0, keepdims=True)


def rowmean(v):
    return jnp.mean(v, -1, keepdims=True)


def rowsum(v):
    return jnp.sum(v, -1, keepdims=True)


def iota(shape, axis):
    return lax.broadcasted_iota(jnp.int32, shape, axis)


class Sizes:
    pass


def block_kernel(
    z,
    x_ref, routes_ref, wq_ref, wk_ref, wv_ref, wo_ref, wr_ref, ga1_ref, be1_ref, ga2_ref, be2_ref, ebin_ref, ebout_ref, cot_ref,
    win_hbm, wout_hbm,
    y_ref, gx_ref, rs_ref, rsmall_ref, gwin_ref, gbin_ref, gwout_ref, gbout_ref,
    win32, wout32, win_s, wout_s, square, flat, pads,
    wst, wg, smst, smg, pt_s, pick_s, sel_s, selt_s, one_s, dgp_s, hat1_s, xn1_s, qkv_s, p_s, o_s, parts, partr,
    x1_s, hat2_s, xn2_s, cotf, gs, gr, xs, xr, growst, grow, x2, c2, a_s, dh_s,
    tsend, trecv, es, er, dxs, dxr, dgst, dgr, hsend, hrecv, dx1_s, dqkv_s, gsend, r1, r2s, smsend, ssend, sr1, s2s, bfpart,
    hbm_sem, send_sem, recv_sem,
):
    n, T, D, HW, R, F, rows, M, heads = z.n, z.T, z.D, z.HW, z.R, z.F, z.rows, z.M, z.heads
    lines, plane, chunks = z.lines, z.plane, z.chunks
    KC = n // chunks
    me = lax.axis_index("expert")
    tn = lax.axis_index("tensor")
    other = 1 - tn
    partner = {"tensor": other}
    line, spot = me // plane, lax.rem(me, plane)
    col = pl.multiple_of(tn * HW, HW)
    ocol = pl.multiple_of(other * HW, HW)
    counter = iter(range(z.sems))

    low_bit, high_bit = lax.rem(line, 2), line // 2

    def other_line(c):
        a, b = lax.rem(c, 2), c // 2
        return (high_bit + b - 2 * high_bit * b) * 2 + low_bit + a - 2 * low_bit * a

    def ahead(k):
        return other_line(lax.rem(k, lines)) * plane + lax.rem(spot + k // lines, plane)

    def behind(k):
        return other_line(lax.rem(k, lines)) * plane + lax.rem(spot - k // lines + plane, plane)

    def in_line(k):
        return lax.rem(line + k, lines)

    def in_plane(j):
        return line * plane + lax.rem(spot + j, plane)

    barrier = pltpu.get_barrier_semaphore()

    def greet(k, _):
        pl.semaphore_signal(barrier, inc=1, device_id={"expert": ahead(k)}, device_id_type=MESH)
        return 0

    lax.fori_loop(1, n, greet, 0)
    pl.semaphore_signal(barrier, inc=1, device_id=partner, device_id_type=MESH)

    win_copy = pltpu.make_async_copy(win_hbm.at[0], win32, hbm_sem.at[0])
    wout_copy = pltpu.make_async_copy(wout_hbm.at[0], wout32, hbm_sem.at[1])
    win_copy.start()
    wout_copy.start()

    def remote(src, dst, i, dev):
        return pltpu.make_async_remote_copy(
            src_ref=src, dst_ref=dst, send_sem=send_sem.at[i], recv_sem=recv_sem.at[i], device_id=dev, device_id_type=MESH
        )

    def spread(low, high, src, dst, to, i, core=None):
        def step(at, _):
            k = high - 1 - at
            dev = {"expert": to(k)}
            if core is not None:
                dev["tensor"] = core
            remote(src.at[k], dst.at[k], i, dev).start()
            return 0

        lax.fori_loop(0, high - low, step, 0)

    def finish(ref, i):
        d = remote(ref, ref, i, partner)
        d.wait_send()
        d.wait_recv()

    wst[0] = wq_ref[...].astype(BF)
    wst[1] = wk_ref[...].astype(BF)
    wst[2] = wv_ref[...].astype(BF)
    wst[3] = wo_ref[...].astype(BF)
    square[...] = jnp.zeros(square.shape, F32)
    square[0:n, 0:rows] = wr_ref[...]
    for i, ref in enumerate((ga1_ref, be1_ref, ga2_ref, be2_ref)):
        square[n + i : n + i + 1, 0:rows] = ref[...]
    smst[...] = square[...].T[0:rows].astype(BF)
    wg[me] = wst[...]
    smg[me] = smst[...]

    flat[0:2, 0:T] = routes_ref[...].astype(F32)
    r = flat[...].T
    r0, r1_ = r[0:T, 0:1], r[0:T, 1:2]
    ie = iota((T, n), 1).astype(F32)
    h0, h1 = r0 == ie, r1_ == ie
    above = [(ie >= i * plane).astype(F32) for i in range(1, lines)]
    line_of = sum(above)
    high_of = above[1]
    low_of = line_of - 2 * high_of
    low_f, high_f = low_bit.astype(F32), high_bit.astype(F32)
    turn = ie - line_of * plane - spot.astype(F32)
    turn = jnp.where(turn < 0, turn + plane, turn)
    place = (high_of - high_f) ** 2 * 2 + (low_of - low_f) ** 2 + turn * lines
    k0, k1 = rowsum(jnp.where(h0, place, 0.0)), rowsum(jnp.where(h1, place, 0.0))
    hk0, hk1 = k0 == ie, k1 == ie
    hit = jnp.logical_or(hk0, hk1).astype(F32).astype(BF)
    tri = (iota((T, T), 0) > iota((T, T), 1)).astype(F32).astype(BF)
    count = dot_nn(tri, hit)
    slot0 = rowsum(jnp.where(hk0, count, 0.0))
    slot1 = rowsum(jnp.where(hk1, count, 0.0))
    pos0 = k0 * R + slot0
    pos1 = k1 * R + slot1
    pads[...] = jnp.full(pads.shape, -1.0, F32)
    pads[0:T, 0:1] = pos0
    pads[0:T, 1:2] = pos1
    post = pads[...].T
    slots = iota((M, T), 0).astype(F32)
    pt_s[...] = jnp.logical_or(slots == post[0:1, 0:T], slots == post[1:2, 0:T]).astype(F32).astype(BF)

    gs[...] = dot_nn(pt_s[...], cot_ref[...]).reshape(n, R, HW).astype(BF)
    cotf[tn] = cot_ref[...]

    x = x_ref[...].astype(F32)
    center = x - rowmean(x)
    rstd1 = lax.rsqrt(rowmean(center * center) + EPS)
    hat1_s[...] = center * rstd1

    pl.semaphore_wait(barrier, n)

    line_sems = [next(counter) for _ in range(lines - 1)]
    small_sems = [next(counter) for _ in range(lines - 1)]
    plane_sem, small_plane_sem = next(counter), next(counter)

    def share(block):
        for j in range(1, plane):
            dev = {"expert": in_plane(j)}
            remote(wg.at[block], wg.at[block], plane_sem, dev).start()
            remote(smg.at[block], smg.at[block], small_plane_sem, dev).start()

    for k in range(1, lines):
        dev = {"expert": in_line(k) * plane + spot}
        remote(smst, smg.at[me], small_sems[k - 1], dev).start()
        remote(wst, wg.at[me], line_sems[k - 1], dev).start()
    share(me)
    cot_sem = next(counter)
    cot_copy = remote(cot_ref, cotf.at[tn], cot_sem, partner)
    cot_copy.start()

    slot_lane = iota((T, M), 1).astype(F32)
    pick_s[0] = (slot_lane == pos0).astype(F32).astype(BF)
    pick_s[1] = (slot_lane == pos1).astype(F32).astype(BF)
    gr[tn, 0] = gs[0]
    win_copy.wait()
    win_s[...] = win32[...].astype(BF)
    wout_copy.wait()
    wout_s[...] = wout32[...].astype(BF)

    for k in range(1, lines):
        finish(wst, line_sems[k - 1])
        finish(smst, small_sems[k - 1])
        share(in_line(lines - k) * plane + spot)

    g_sems = [next(counter) for _ in range(chunks)]

    def send_cotangent(c):
        spread(max(1, c * KC), (c + 1) * KC, gs, gr.at[tn], ahead, g_sems[c])

    send_cotangent(0)

    finish(smg.at[pl.ds(0, (plane - 1) * lines)], small_plane_sem)
    small = smg[...].astype(F32).reshape(n * rows, smg.shape[2]).T
    ga1, be1 = small[n : n + 1], small[n + 1 : n + 2]
    ga2, be2 = small[n + 2 : n + 3], small[n + 3 : n + 4]
    wr = small[0:n].astype(BF)
    xn1 = (hat1_s[...] * ga1 + be1).astype(BF)
    xn1_s[...] = xn1

    finish(wg.at[pl.ds(0, (plane - 1) * lines)], plane_sem)
    scale = 1.0 / math.sqrt(HEAD_DIM)

    for c in range(1, EARLY):
        send_cotangent(c)

    def weight(i):
        return wg[:, i].reshape(D, HW)

    for i in range(3):
        qkv_s[i] = dot_nn(xn1, weight(i)).astype(BF)

    outs = []
    for h in range(heads):
        sl = slice(h * HEAD_DIM, (h + 1) * HEAD_DIM)
        s = dot_nt(qkv_s[0, :, sl], qkv_s[1, :, sl]) * scale
        ex = jnp.exp(s - jnp.max(s, -1, keepdims=True))
        p = ex / rowsum(ex)
        p_s[h] = p
        outs.append(dot_nn(p.astype(BF), qkv_s[2, :, sl]))
    o_s[...] = jnp.concatenate(outs, -1).astype(BF)

    parts[...] = dot_nt(o_s[...], weight(3)).astype(BF)
    part_sem = next(counter)
    part_copy = remote(parts, partr, part_sem, partner)
    part_copy.start()

    part_copy.wait()
    x1 = x_ref[...].astype(F32) + (parts[...].astype(F32) + partr[...].astype(F32))
    x1_s[...] = x1

    center = x1 - rowmean(x1)
    rstd2 = lax.rsqrt(rowmean(center * center) + EPS)
    hat2 = center * rstd2
    hat2_s[...] = hat2
    xn2 = (hat2 * ga2 + be2).astype(BF)
    xn2_s[...] = xn2
    xs[...] = dot_nn(pt_s[...], xn2_s[:, pl.ds(col, HW)]).reshape(n, R, HW).astype(BF)

    row_sems = [next(counter) for _ in range(chunks)]

    def send_rows(c):
        spread(max(1, c * KC), (c + 1) * KC, xs, xr.at[tn], ahead, row_sems[c])

    send_rows(0)
    xr[tn, 0] = xs[0]

    logits = dot_nt(xn2, wr)
    l0 = rowsum(jnp.where(h0, logits, 0.0))
    l1 = rowsum(jnp.where(h1, logits, 0.0))
    top = jnp.maximum(l0, l1)
    e0, e1 = jnp.exp(l0 - top), jnp.exp(l1 - top)
    gate0, gate1 = e0 / (e0 + e1), e1 / (e0 + e1)
    islot = iota((T, LANES), 1).astype(F32)
    at0 = (slot0 == islot).astype(F32).astype(BF)
    at1 = (slot1 == islot).astype(F32).astype(BF)
    gate_rows = jnp.zeros((n, LANES), F32)
    for hh, gg, at in ((hk0, gate0, at0), (hk1, gate1, at1)):
        for part in halves(jnp.where(hh, gg, 0.0)):
            gate_rows = gate_rows + dot_tn(part, at)
    growst[:, 0, :] = gate_rows
    gate_sem = next(counter)
    spread(1, n, growst, grow, ahead, gate_sem)
    grow[0] = growst[0]
    for c in range(1, chunks):
        if c >= EARLY:
            send_cotangent(c)
        send_rows(c)

    FT = 256
    c0 = math.sqrt(2.0 / math.pi)
    MC = KC * R
    half_sems = [next(counter) for _ in range(chunks)]
    g_half_sems = [next(counter) for _ in range(chunks)]
    dx_half = [next(counter) for _ in range(chunks)]
    e_half = [next(counter) for _ in range(chunks)]
    dx_sems = [next(counter) for _ in range(chunks)]

    def send_dx(c):
        rc = slice(c * MC, (c + 1) * MC)
        kc = pl.ds(c * KC, KC)
        finish(tsend.at[0, rc], dx_half[c])
        own = dot_nt(dh_s[rc], win_s[pl.ds(col, HW), :])
        dxs[c * KC : (c + 1) * KC] = (own + trecv[0, rc].astype(F32)).reshape(KC, R, HW).astype(BF)
        spread(max(1, c * KC), (c + 1) * KC, dxs, dxr, behind, dx_sems[c])
        if c == 0:
            dxr[0] = dxs[0]

    def arrive(c):
        low = max(1, c * KC)
        kc = pl.ds(c * KC, KC)
        copies = []
        for buf, came, half in ((gr, g_sems, g_half_sems), (xr, row_sems, half_sems)):
            finish(buf.at[tn, pl.ds(low, (c + 1) * KC - low)], came[c])
            copies.append(remote(buf.at[tn, kc], buf.at[tn, kc], half[c], partner))
            copies[-1].start()
        return copies

    block_of = iota((M, n), 0) - iota((M, n), 1) * R
    in_block = jnp.logical_and(block_of >= 0, block_of < R)
    sel_s[...] = in_block.astype(F32).astype(BF)
    at_slot = rowsum(jnp.where(in_block, block_of.astype(F32), 0.0))
    one_s[...] = (at_slot == iota((M, LANES), 1).astype(F32)).astype(F32)
    along = iota((n, M), 1) - iota((n, M), 0) * R
    selt_s[...] = jnp.logical_and(along >= 0, along < R).astype(F32).astype(BF)

    copies = arrive(0)
    for c in range(chunks):
        rc = slice(c * MC, (c + 1) * MC)
        for copy in copies:
            copy.wait()
        for hf in range(2):
            wide = slice(hf * HW, (hf + 1) * HW)
            x2[rc, wide] = xr[hf, c * KC : (c + 1) * KC].reshape(MC, HW)
            c2[rc, wide] = gr[hf, c * KC : (c + 1) * KC].reshape(MC, HW)

        def first(i, _):
            f = pl.ds(pl.multiple_of(i * FT, FT), FT)
            h = dot_nn(x2[rc], win_s[:, f]) + ebin_ref[:, f]
            hh = h * h
            half = 0.5 + 0.5 * jnp.tanh(h * (c0 + (0.044715 * c0) * hh))
            act = (h * half).astype(BF)
            a_s[rc, f] = act
            slope = half + (half - half * half) * (h * (2 * c0 + (6 * 0.044715 * c0) * hh))
            da = dot_nt(c2[rc], wout_s[f, :])
            dh_s[rc, f] = (slope * da).astype(BF)
            both = act.astype(F32) * da
            for j in range(FT // LANES):
                dgp_s[rc] = dgp_s[rc] + both[:, j * LANES : (j + 1) * LANES]
            return 0

        own_g = gr[tn, c * KC : (c + 1) * KC].reshape(MC, HW).astype(F32) * ebout_ref[:, pl.ds(col, HW)]
        dgp_s[rc] = sum(own_g[:, j * LANES : (j + 1) * LANES] for j in range(HW // LANES))
        lax.fori_loop(0, F // FT // 2, first, 0)
        if c + 1 < chunks:
            copies = arrive(c + 1)
        lax.fori_loop(F // FT // 2, F // FT, first, 0)
        if c > 0:
            send_dx(c - 1)
        tsend[0, rc] = dot_nt(dh_s[rc], win_s[pl.ds(ocol, HW), :]).astype(BF)
        remote(tsend.at[0, rc], trecv.at[0, rc], dx_half[c], partner).start()
    dgate = rowsum(dgp_s[...])
    dg_rows = jnp.zeros((n, LANES), F32)
    for part in halves(one_s[...] * dgate):
        dg_rows = dg_rows + dot_nn(selt_s[...], part)
    dgst[:, 0, :] = dg_rows
    dg_same, dg_cross, dg_own = next(counter), next(counter), next(counter)
    spread(1, n, dgst, dgr.at[tn], behind, dg_same)
    spread(1, n, dgst, dgr.at[tn], behind, dg_cross, other)
    own_gate = remote(dgst.at[0], dgr.at[tn, 0], dg_own, partner)
    own_gate.start()
    dgr[tn, 0] = dgst[0]
    send_dx(chunks - 1)

    for c in range(chunks):
        rc = slice(c * MC, (c + 1) * MC)
        tsend[1, rc] = dot_nn(a_s[rc], wout_s[:, pl.ds(ocol, HW)]).astype(BF)
        remote(tsend.at[1, rc], trecv.at[1, rc], e_half[c], partner).start()
    for c in range(chunks):
        rc = slice(c * MC, (c + 1) * MC)
        own = dot_nn(a_s[rc], wout_s[:, pl.ds(col, HW)])
        finish(tsend.at[1, rc], e_half[c])
        es[c * KC : (c + 1) * KC] = (
            (own + trecv[1, rc].astype(F32) + ebout_ref[:, pl.ds(col, HW)]).reshape(KC, R, HW).astype(BF)
        )
    e_sem = next(counter)
    spread(1, n, es, er, behind, e_sem)
    er[0] = es[0]

    finish(dgr.at[tn, pl.ds(0, n - 1)], dg_same)
    finish(dgr.at[other, pl.ds(0, n - 1)], dg_cross)
    own_gate.wait()
    dg_all = dgr[0, :, 0, :] + dgr[1, :, 0, :]
    hb0, hb1 = hk0.astype(F32).astype(BF), hk1.astype(F32).astype(BF)
    dg0 = rowsum(jnp.where(slot0 == islot, pick_nn(hb0, dg_all), 0.0))
    dg1 = rowsum(jnp.where(slot1 == islot, pick_nn(hb1, dg_all), 0.0))
    mean_gate = gate0 * dg0 + gate1 * dg1
    dl0, dl1 = gate0 * (dg0 - mean_gate), gate1 * (dg1 - mean_gate)
    dlog = (jnp.where(h0, dl0, 0.0) + jnp.where(h1, dl1, 0.0)).astype(BF)

    for c in range(chunks):
        low = max(1, c * KC)
        finish(dxr.at[pl.ds(low, (c + 1) * KC - low)], dx_sems[c])

    rows_dx = dxr[...].reshape(M, HW)
    hsend[...] = gate0 * dot_nn(pick_s[0], rows_dx) + gate1 * dot_nn(pick_s[1], rows_dx)
    h_sem = next(counter)
    hc = remote(hsend, hrecv.at[tn], h_sem, partner)
    hc.start()
    hrecv[tn] = hsend[...]
    by_router = dot_nn(dlog, wr)

    hc.wait()
    cot_copy.wait()

    dxn2 = jnp.concatenate([hrecv[0], hrecv[1]], -1) + by_router
    hat2 = hat2_s[...]
    gg2, gb2 = colsum(dxn2 * hat2), colsum(dxn2)
    u = dxn2 * ga2
    dx1 = jnp.concatenate([cotf[0], cotf[1]], -1).astype(F32) + rstd2 * (u - rowmean(u) - hat2 * rowmean(u * hat2))
    dx1_s[...] = dx1
    datt = dx1.astype(BF)
    do = dot_nn(datt, weight(3)).astype(BF)

    first_sems = [next(counter) for _ in range(5)]
    second_sems = [next(counter) for _ in range(5)]

    def to_plane(i, src, dst):
        for j in range(1, plane):
            remote(src.at[:, lax.rem(spot + j, plane)], dst.at[j - 1], first_sems[i], {"expert": in_plane(j)}).start()

    def to_line(i, src, got, mid, dst):
        finish(got, first_sems[i])
        total = src[:, spot].astype(F32)
        for j in range(plane - 1):
            total = total + got[j].astype(F32)
        mid[...] = total.astype(BF)
        for k in range(1, lines):
            there = in_line(k)
            remote(mid.at[there], dst.at[k], second_sems[i], {"expert": there * plane + spot}).start()
        dst[0] = mid[line]

    def gradient(i, value):
        gsend[i] = value.reshape(lines, plane, rows, HW).astype(BF)
        to_plane(i, gsend.at[i], r1.at[i])

    gradient(0, dot_tn(datt, o_s[...]))

    dqs, dks, dvs = [], [], []
    for h in range(heads):
        sl = slice(h * HEAD_DIM, (h + 1) * HEAD_DIM)
        p = p_s[h]
        doh = do[:, sl]
        dp = dot_nt(doh, qkv_s[2, :, sl])
        dvs.append(dot_tn(p.astype(BF), doh))
        ds = (p * (dp - rowsum(p * dp))).astype(BF)
        dqs.append(dot_nn(ds, qkv_s[1, :, sl]) * scale)
        dks.append(dot_tn(ds, qkv_s[0, :, sl]) * scale)
    for i, v in enumerate((dqs, dks, dvs)):
        dqkv_s[i] = jnp.concatenate(v, -1).astype(BF)

    bfpart[0] = (
        dot_nt(dqkv_s[0], weight(0)) + dot_nt(dqkv_s[1], weight(1)) + dot_nt(dqkv_s[2], weight(2))
    ).astype(BF)
    b_sem = next(counter)
    bc = remote(bfpart.at[0], bfpart.at[1], b_sem, partner)
    bc.start()

    for i in range(3):
        gradient(i + 1, dot_tn(xn1_s[...], dqkv_s[i]))

    bc.wait()
    dxn1 = bfpart[0].astype(F32) + bfpart[1].astype(F32)
    hat1 = hat1_s[...]
    gg1, gb1 = colsum(dxn1 * hat1), colsum(dxn1)
    u = dxn1 * ga1
    gx_ref[...] = dx1_s[...] + rstd1 * (u - rowmean(u) - hat1 * rowmean(u * hat1))

    smsend[...] = jnp.zeros(smsend.shape, F32)
    smsend[0:n] = dot_tn(dlog, xn2_s[...])
    smsend[n : n + 1] = gg1
    smsend[n + 1 : n + 2] = gb1
    smsend[n + 2 : n + 3] = gg2
    smsend[n + 3 : n + 4] = gb2
    ssend[...] = smsend[...].T.reshape(lines, plane, rows, ssend.shape[3]).astype(BF)
    to_plane(4, ssend, sr1)
    to_line(0, gsend.at[0], r1.at[0], r2s.at[0], rs_ref.at[0])

    finish(grow.at[pl.ds(0, n - 1)], gate_sem)
    gate_col = rowsum(one_s[...] * pick_nn(sel_s[...], grow[:, 0, :]))
    gated = gate_col * c2[...].astype(F32)
    c2[...] = gated.astype(BF)
    gbout_ref[...] = colsum(gated)
    x2[...] = (gate_col * x2[...].astype(F32)).astype(BF)
    lane = iota((M, LANES), 1)
    gate_parts = halves(gate_col)
    gate_lanes = sum(jnp.where(lane == i, part.astype(F32), 0.0) for i, part in enumerate(gate_parts)).astype(BF)

    def grads(i, _):
        f = pl.ds(pl.multiple_of(i * FT, FT), FT)
        gwout_ref[f, :] = dot_tn(a_s[:, f], c2[...])
        gwin_ref[:, f] = dot_tn(x2[...], dh_s[:, f])
        gbin_ref[:, f] = colsum(dot_tn(gate_lanes, dh_s[:, f]))
        return 0

    lax.fori_loop(0, F // FT, grads, 0)

    finish(er.at[pl.ds(0, n - 1)], e_sem)

    rows_e = er[...].reshape(M, HW)
    y = x1_s[:, pl.ds(col, HW)]
    y = y + gate0 * dot_nn(pick_s[0], rows_e)
    y = y + gate1 * dot_nn(pick_s[1], rows_e)
    y_ref[...] = y.astype(BF)

    for i in range(1, 4):
        to_line(i, gsend.at[i], r1.at[i], r2s.at[i], rs_ref.at[i])
    to_line(4, ssend, sr1, s2s, rsmall_ref)

    for i in range(4):
        finish(rs_ref.at[i, pl.ds(1, lines - 1)], second_sems[i])
    finish(rsmall_ref.at[pl.ds(1, lines - 1)], second_sems[4])


def last_kernel(
    y_in, gx_in, rs, rsmall, gwin_in, gbin_in, gwout_in, gbout_in,
    y, gx, gq, gk, gv, go, gr, a1, b1, a2, b2, gwin, gbin, gwout, gbout, sem,
):
    copies = [
        pltpu.make_async_copy(src, dst, sem.at[i])
        for i, (src, dst) in enumerate(((gwin_in, gwin), (gwout_in, gwout), (gx_in, gx), (y_in, y)))
    ]
    for c in copies:
        c.start()
    gbin[...] = gbin_in[...]
    gbout[...] = gbout_in[...]
    for i, ref in enumerate((go, gq, gk, gv)):
        ref[...] = jnp.sum(rs[i].astype(F32), 0)
    n, rows = gr.shape
    small = jnp.sum(rsmall[...].astype(F32), 0).T
    gr[...] = small[0:n, 0:rows]
    for i, ref in enumerate((a1, b1, a2, b2)):
        ref[...] = small[n + i : n + i + 1, 0:rows]
    for c in copies:
        c.wait()


def shards(
    block_input, routes, w_query, w_key, w_value, w_output, w_router, norm1_gain, norm1_bias, norm2_gain, norm2_bias,
    expert_in, expert_in_bias, expert_out, expert_out_bias, cotangent,
):
    z = Sizes()
    z.n = lax.axis_size("expert")
    z.T, z.D = block_input.shape
    z.HW = cotangent.shape[1]
    z.F = expert_in.shape[2]
    z.rows = w_query.shape[0]
    z.heads = z.HW // HEAD_DIM
    experts, topk = w_router.shape[1], routes.shape[1]
    cap = max(2, 2 * topk * z.T // experts)
    z.R = -(-cap // 8) * 8
    z.M = z.n * z.R
    z.lines = 4
    z.plane = z.n // z.lines
    z.chunks = CHUNKS
    z.sems = 64
    n, T, D, HW, R, F, rows, M = z.n, z.T, z.D, z.HW, z.R, z.F, z.rows, z.M
    lines, plane = z.lines, z.plane
    wide = -(-(n + 4) // LANES) * LANES
    vm = pl.BlockSpec(memory_space=pltpu.VMEM)
    hbm = pl.BlockSpec(memory_space=pl.ANY)
    out_shape = (
        jax.ShapeDtypeStruct((T, HW), BF),
        jax.ShapeDtypeStruct((T, D), F32),
        jax.ShapeDtypeStruct((4, lines, rows, HW), BF),
        jax.ShapeDtypeStruct((lines, rows, wide), BF),
        jax.ShapeDtypeStruct((D, F), F32),
        jax.ShapeDtypeStruct((1, F), F32),
        jax.ShapeDtypeStruct((F, D), F32),
        jax.ShapeDtypeStruct((1, D), F32),
    )
    V = pltpu.VMEM
    tp = -(-T // LANES) * LANES
    scratch = [
        V((D, F), F32), V((F, D), F32), V((D, F), BF), V((F, D), BF), V((wide, LANES), F32), V((8, tp), F32), V((tp, LANES), F32),
        V((4, rows, HW), BF), V((n, 4, rows, HW), BF), V((rows, wide), BF), V((n, rows, wide), BF),
        V((M, T), BF), V((2, T, M), BF), V((M, n), BF), V((n, M), BF), V((M, LANES), F32), V((M, LANES), F32), V((T, D), F32), V((T, D), BF), V((3, T, HW), BF), V((z.heads, T, T), F32),
        V((T, HW), BF), V((T, D), BF), V((T, D), BF),
        V((T, D), F32), V((T, D), F32), V((T, D), BF), V((2, T, HW), BF),
        V((n, R, HW), BF), V((2, n, R, HW), BF), V((n, R, HW), BF), V((2, n, R, HW), BF),
        V((n, 1, LANES), F32), V((n, 1, LANES), F32), V((M, D), BF), V((M, D), BF), V((M, F), BF), V((M, F), BF),
        V((2, M, HW), BF), V((2, M, HW), BF), V((n, R, HW), BF), V((n, R, HW), BF), V((n, R, HW), BF), V((n, R, HW), BF),
        V((n, 1, LANES), F32), V((2, n, 1, LANES), F32), V((T, HW), F32), V((2, T, HW), F32), V((T, D), F32), V((3, T, HW), BF),
        V((4, lines, plane, rows, HW), BF), V((4, plane - 1, lines, rows, HW), BF), V((4, lines, rows, HW), BF), V((wide, D), F32),
        V((lines, plane, rows, wide), BF), V((plane - 1, lines, rows, wide), BF), V((lines, rows, wide), BF), V((2, T, D), BF),
        pltpu.SemaphoreType.DMA((2,)), pltpu.SemaphoreType.DMA((z.sems,)), pltpu.SemaphoreType.DMA((z.sems,)),
    ]
    kept = [pltpu.VMEM(v.shape, v.dtype) for v in out_shape]
    done = pl.pallas_call(
        functools.partial(block_kernel, z),
        out_shape=kept,
        in_specs=[vm] * 14 + [pl.BlockSpec(memory_space=pltpu.HBM)] * 2,
        out_specs=[vm] * 8,
        scratch_shapes=scratch,
        compiler_params=pltpu.CompilerParams(collective_id=0, has_side_effects=True, vmem_limit_bytes=40 << 20),
        name="block",
    )(
        *(
            pltpu.with_memory_space_constraint(v, pltpu.HBM)
            for v in (
                block_input, routes.T, w_query, w_key, w_value, w_output.T, w_router.T,
                norm1_gain[None], norm1_bias[None], norm2_gain[None], norm2_bias[None],
                expert_in_bias, expert_out_bias, cotangent, expert_in, expert_out,
            )
        )
    )
    square = jax.ShapeDtypeStruct((rows, HW), F32)
    line = jax.ShapeDtypeStruct((1, rows), F32)
    last_shape = (
        out_shape[0], out_shape[1], square, square, square, square, jax.ShapeDtypeStruct((n, rows), F32), line, line, line, line,
        out_shape[4], out_shape[5], out_shape[6], out_shape[7],
    )
    y, gx, gq, gk, gv, go, gr, a1, b1, a2, b2, gwin, gbin, gwout, gbout = pl.pallas_call(
        last_kernel,
        out_shape=last_shape,
        in_specs=[vm] * 8,
        out_specs=[hbm] * 2 + [vm] * 9 + [hbm, vm, hbm, vm],
        scratch_shapes=[pltpu.SemaphoreType.DMA((4,))],
        compiler_params=pltpu.CompilerParams(vmem_limit_bytes=8 << 20),
        name="last",
    )(*done)
    return (y, gx, gq, gk, gv, go.T, gr.T, a1[0], b1[0], a2[0], b2[0], gwin[None], gbin, gwout[None], gbout)


def solution(mesh):
    row, col = P("expert", None), P("expert", "tensor")
    vec = P("expert")
    in_specs = (
        row, row, col, col, col, P("tensor", "expert"), row, vec, vec, vec, vec,
        P("expert", None, "tensor"), col, P("expert", "tensor", None), row, col,
    )
    out_specs = (
        col, row, col, col, col, P("tensor", "expert"), row, vec, vec, vec, vec,
        P("expert", None, "tensor"), col, P("expert", "tensor", None), row,
    )
    return jax.shard_map(shards, mesh=mesh, in_specs=in_specs, out_specs=out_specs, check_vma=False)
```

```python
import functools
import math

import jax
import jax.numpy as jnp
from jax import lax
from jax.experimental import pallas as pl
from jax.experimental.pallas import tpu as pltpu
from jax.sharding import PartitionSpec as P

HEAD_DIM = 64
EPS = 1e-06
MESH = pl.DeviceIdType.MESH
BF = jnp.bfloat16
F32 = jnp.float32
LANES = 128
CHUNKS = 4
EARLY = 3


def dot_nn(a, b):
    return lax.dot_general(a, b, (((1,), (0,)), ((), ())), preferred_element_type=F32)


def dot_nt(a, b):
    return lax.dot_general(a, b, (((1,), (1,)), ((), ())), preferred_element_type=F32)


def dot_tn(a, b):
    return lax.dot_general(a, b, (((0,), (0,)), ((), ())), preferred_element_type=F32)


def halves(v):
    first = v.astype(BF)
    rest = v - first.astype(F32)
    second = rest.astype(BF)
    return first, second, (rest - second.astype(F32)).astype(BF)


def pick_nn(select, v):
    a, b, c = halves(v)
    return dot_nn(select, a) + dot_nn(select, b) + dot_nn(select, c)


def colsum(v):
    return jnp.sum(v, axis=0, keepdims=True)


def rowmean(v):
    return jnp.mean(v, -1, keepdims=True)


def rowsum(v):
    return jnp.sum(v, -1, keepdims=True)


def iota(shape, axis):
    return lax.broadcasted_iota(jnp.int32, shape, axis)


class Sizes:
    pass


def block_kernel(
    z,
    x_hbm, routes_hbm, wq_hbm, wk_hbm, wv_hbm, wo_hbm, wr_hbm, ga1_hbm, be1_hbm, ga2_hbm, be2_hbm, ebin_hbm, ebout_hbm, cot_hbm,
    win_hbm, wout_hbm,
    y_out, gx_out, rs_ref, rsmall_ref, gwin_out, gbin_out, gwout_out, gbout_out,
    y_ref, gx_ref, gwin_ref, gbin_ref, gwout_ref, gbout_ref,
    win32, wout32, win_s, wout_s, square, flat, pads,
    wa, wb, pt_s, pick_s, sel_s, selt_s, one_s, dgp_s, own_s, hat1_s, xn1_s, qkv_s, p_s, o_s, parts, partr,
    x1_s, hat2_s, xn2_s, cotf, gs, gr, xs, xr, gst, grt, xst, xrt, est, ert, dxst, dxrt, growst, grow, x2, c2, a_s, dh_s,
    tsend, trecv, es, er, dxs, dxr, dgst, dgr, hsend, hrecv, dx1_s, dqkv_s, gsend, r1, r2s, smsend, ssend, sr1, s2s, bfpart,
    x_ref, routes_ref, wq_ref, wk_ref, wv_ref, wo_ref, wr_ref, ga1_ref, be1_ref, ga2_ref, be2_ref, ebin_ref, ebout_ref, cot_ref,
    hbm_sem, send_sem, recv_sem,
):
    tail = z.tail
    n, T, D, HW, R, F, rows, M, heads = z.n, z.T, z.D, z.HW, z.R, z.F, z.rows, z.M, z.heads
    lines, plane, chunks = z.lines, z.plane, z.chunks
    KC = n // chunks
    me = lax.axis_index("expert")
    tn = lax.axis_index("tensor")
    other = 1 - tn
    partner = {"tensor": other}
    line, spot = me // plane, lax.rem(me, plane)
    col = pl.multiple_of(tn * HW, HW)
    ocol = pl.multiple_of(other * HW, HW)
    counter = iter(range(z.sems))

    low_bit, high_bit = lax.rem(line, 2), line // 2

    def other_line(c):
        a, b = lax.rem(c, 2), c // 2
        return (high_bit + b - 2 * high_bit * b) * 2 + low_bit + a - 2 * low_bit * a

    def ahead(k):
        return other_line(lax.rem(k, lines)) * plane + lax.rem(spot + k // lines, plane)

    def behind(k):
        return other_line(lax.rem(k, lines)) * plane + lax.rem(spot - k // lines + plane, plane)

    def in_line(k):
        return lax.rem(line + k, lines)

    def in_plane(j):
        return line * plane + lax.rem(spot + j, plane)

    barrier = pltpu.get_barrier_semaphore()

    def greet(k, _):
        pl.semaphore_signal(barrier, inc=1, device_id={"expert": ahead(k)}, device_id_type=MESH)
        return 0

    lax.fori_loop(1, n, greet, 0)
    pl.semaphore_signal(barrier, inc=1, device_id=partner, device_id_type=MESH)

    moves = (
        (wq_hbm, wq_ref), (wk_hbm, wk_ref), (wv_hbm, wv_ref), (wo_hbm, wo_ref), (wr_hbm, wr_ref),
        (ga1_hbm, ga1_ref), (be1_hbm, be1_ref), (ga2_hbm, ga2_ref), (be2_hbm, be2_ref),
        (routes_hbm, routes_ref), (cot_hbm, cot_ref), (x_hbm, x_ref), (ebin_hbm, ebin_ref), (ebout_hbm, ebout_ref),
        (win_hbm.at[0], win32), (wout_hbm.at[0], wout32),
    )
    moves = [pltpu.make_async_copy(src, dst, hbm_sem.at[i]) for i, (src, dst) in enumerate(moves)]
    for move in moves:
        move.start()
    win_copy, wout_copy = moves[14:]

    def remote(src, dst, i, dev):
        return pltpu.make_async_remote_copy(
            src_ref=src, dst_ref=dst, send_sem=send_sem.at[i], recv_sem=recv_sem.at[i], device_id=dev, device_id_type=MESH
        )

    def spread(low, high, src, dst, to, i, core=None):
        def step(at, _):
            k = high - 1 - at
            dev = {"expert": to(k)}
            if core is not None:
                dev["tensor"] = core
            remote(src.at[k], dst.at[k], i, dev).start()
            return 0

        lax.fori_loop(0, high - low, step, 0)

    def finish(ref, i):
        d = remote(ref, ref, i, partner)
        d.wait_send()
        d.wait_recv()

    def put(value, body, odd):
        body[...] = value[0 : n * R].reshape(n, R, HW).astype(BF)
        if tail:
            odd[:, 0, :] = value[n * R :].astype(BF)

    def picked(body, odd):
        total = 0.0
        for pick, gate in ((pick_s.at[0], gate0), (pick_s.at[1], gate1)):
            value = dot_nn(pick[:, 0 : n * R], body[...].reshape(n * R, HW))
            if tail:
                value = value + dot_nn(pick[:, n * R :], odd[:, 0, :])
            total = total + gate * value
        return total

    for move in moves[:9]:
        move.wait()
    wide, sr = square.shape[0], wa.shape[1] - 2 * rows
    wa[me, 0:rows] = wq_ref[...].astype(BF)
    wa[me, rows : 2 * rows] = wk_ref[...].astype(BF)
    wb[me, 0:rows] = wv_ref[...].astype(BF)
    wb[me, rows : 2 * rows] = wo_ref[...].astype(BF)
    square[...] = jnp.zeros(square.shape, F32)
    square[0:n, 0:rows] = wr_ref[...]
    for i, ref in enumerate((ga1_ref, be1_ref, ga2_ref, be2_ref)):
        square[n + i : n + i + 1, 0:rows] = ref[...]
    turned = square[...].T
    for i in range(HW // wide):
        wa[me, 2 * rows :, i * wide : (i + 1) * wide] = turned[i * sr : (i + 1) * sr].astype(BF)

    pl.semaphore_wait(barrier, n)

    line_a = [None] + [next(counter) for _ in range(lines - 1)]
    line_b = [None] + [next(counter) for _ in range(lines - 1)]
    square_plane = plane == 4
    if square_plane:
        near_a = [next(counter) for _ in range(lines)]
        near_b = [next(counter) for _ in range(lines)]
        far_a, far_b = next(counter), next(counter)
        side, over = spot + 1 - 2 * lax.rem(spot, 2), lax.rem(spot + 2, 4)
        to_side, to_over = {"expert": line * plane + side}, {"expert": line * plane + over}
    else:
        plane_a, plane_b = next(counter), next(counter)

    def share(s):
        block = other_line(s) * plane + spot
        if square_plane:
            remote(wa.at[block], wa.at[block], near_a[s], to_side).start()
            remote(wb.at[block], wb.at[block], near_b[s], to_over).start()
            remote(wa.at[block], wa.at[block], far_a, to_over).start()
            remote(wb.at[block], wb.at[block], far_b, to_side).start()
        else:
            for j in range(1, plane):
                remote(wa.at[block], wa.at[block], plane_a, {"expert": in_plane(j)}).start()
                remote(wb.at[block], wb.at[block], plane_b, {"expert": in_plane(j)}).start()

    def hand_on(s):
        if square_plane:
            finish(wa.at[0], near_a[s])
            block = other_line(s) * plane + side
            remote(wa.at[block], wa.at[block], far_a, to_over).start()
            finish(wb.at[0], near_b[s])
            block = other_line(s) * plane + over
            remote(wb.at[block], wb.at[block], far_b, to_side).start()

    for k in range(1, lines):
        dev = {"expert": other_line(k) * plane + spot}
        remote(wa.at[me], wa.at[me], line_a[k], dev).start()
        remote(wb.at[me], wb.at[me], line_b[k], dev).start()
    share(0)

    moves[9].wait()
    flat[0:2, 0:T] = routes_ref[...].astype(F32)
    r = flat[...].T
    r0, r1_ = r[0:T, 0:1], r[0:T, 1:2]
    ie = iota((T, n), 1).astype(F32)
    h0, h1 = r0 == ie, r1_ == ie
    above = [(ie >= i * plane).astype(F32) for i in range(1, lines)]
    line_of = sum(above)
    high_of = above[1]
    low_of = line_of - 2 * high_of
    low_f, high_f = low_bit.astype(F32), high_bit.astype(F32)
    turn = ie - line_of * plane - spot.astype(F32)
    turn = jnp.where(turn < 0, turn + plane, turn)
    place = (high_of - high_f) ** 2 * 2 + (low_of - low_f) ** 2 + turn * lines
    k0, k1 = rowsum(jnp.where(h0, place, 0.0)), rowsum(jnp.where(h1, place, 0.0))
    hk0, hk1 = k0 == ie, k1 == ie
    hit = jnp.logical_or(hk0, hk1).astype(F32).astype(BF)
    tri = (iota((T, T), 0) > iota((T, T), 1)).astype(F32).astype(BF)
    count = dot_nn(tri, hit)
    slot0 = rowsum(jnp.where(hk0, count, 0.0))
    slot1 = rowsum(jnp.where(hk1, count, 0.0))
    pos0 = jnp.where(slot0 < R, k0 * R + slot0, k0 + n * R)
    pos1 = jnp.where(slot1 < R, k1 * R + slot1, k1 + n * R)
    pads[...] = jnp.full(pads.shape, -1.0, F32)
    pads[0:T, 0:1] = pos0
    pads[0:T, 1:2] = pos1
    post = pads[...].T
    slots = iota((M, T), 0).astype(F32)
    pt_s[...] = jnp.logical_or(slots == post[0:1, 0:T], slots == post[1:2, 0:T]).astype(F32).astype(BF)

    moves[10].wait()
    put(dot_nn(pt_s[...], cot_ref[...]), gs, gst)
    cotf[tn] = cot_ref[...]
    cot_sem = next(counter)
    cot_copy = remote(cot_ref, cotf.at[tn], cot_sem, partner)
    cot_copy.start()

    for move in moves[11:14]:
        move.wait()
    x = x_ref[...].astype(F32)
    center = x - rowmean(x)
    rstd1 = lax.rsqrt(rowmean(center * center) + EPS)
    hat1_s[...] = center * rstd1

    slot_lane = iota((T, M), 1).astype(F32)
    pick_s[0] = (slot_lane == pos0).astype(F32).astype(BF)
    pick_s[1] = (slot_lane == pos1).astype(F32).astype(BF)
    gr[tn, 0] = gs[0]
    if tail:
        grt[tn, 0] = gst[0]
    win_copy.wait()
    win_s[...] = win32[...].astype(BF)
    wout_copy.wait()
    wout_s[...] = wout32[...].astype(BF)

    for k in range(1, lines):
        finish(wa.at[0], line_a[k])
        finish(wb.at[0], line_b[k])
        share(k)
        hand_on(k - 1)

    row_sems = [next(counter) for _ in range(chunks)]
    odd_rows, odd_half, odd_dx, odd_e = (next(counter) for _ in range(4))

    def send_cotangent(c):
        spread(max(1, c * KC), (c + 1) * KC, gs, gr.at[tn], ahead, row_sems[c])
        if tail and c + 1 == chunks:
            spread(1, n, gst, grt.at[tn], ahead, odd_rows)

    send_cotangent(0)

    hand_on(lines - 1)

    if square_plane:
        finish(wa.at[pl.ds(0, 2 * lines)], far_a)
    else:
        finish(wa.at[pl.ds(0, (plane - 1) * lines)], plane_a)
    small = jnp.concatenate([wa[:, 2 * rows :, i * wide : (i + 1) * wide] for i in range(HW // wide)], 1)
    small = small.astype(F32).reshape(n * rows, wide).T
    ga1, be1 = small[n : n + 1], small[n + 1 : n + 2]
    ga2, be2 = small[n + 2 : n + 3], small[n + 3 : n + 4]
    wr = small[0:n].astype(BF)
    xn1 = (hat1_s[...] * ga1 + be1).astype(BF)
    xn1_s[...] = xn1

    def weight(i):
        ref = wb if i >= 2 else wa
        return ref[:, i % 2 * rows : (i % 2 + 1) * rows].reshape(D, HW)

    for i in range(2):
        qkv_s[i] = dot_nn(xn1, weight(i)).astype(BF)

    if square_plane:
        finish(wb.at[pl.ds(0, 2 * lines)], far_b)
    else:
        finish(wb.at[pl.ds(0, (plane - 1) * lines)], plane_b)
    scale = 1.0 / math.sqrt(HEAD_DIM)

    for c in range(1, EARLY):
        send_cotangent(c)

    qkv_s[2] = dot_nn(xn1, weight(2)).astype(BF)

    outs = []
    for h in range(heads):
        sl = slice(h * HEAD_DIM, (h + 1) * HEAD_DIM)
        s = dot_nt(qkv_s[0, :, sl], qkv_s[1, :, sl]) * scale
        ex = jnp.exp(s - jnp.max(s, -1, keepdims=True))
        p = ex / rowsum(ex)
        p_s[h] = p
        outs.append(dot_nn(p.astype(BF), qkv_s[2, :, sl]))
    o_s[...] = jnp.concatenate(outs, -1).astype(BF)

    parts[...] = dot_nt(o_s[...], weight(3)).astype(BF)
    part_sem = next(counter)
    part_copy = remote(parts, partr, part_sem, partner)
    part_copy.start()

    part_copy.wait()
    x1 = x_ref[...].astype(F32) + (parts[...].astype(F32) + partr[...].astype(F32))
    x1_s[...] = x1

    center = x1 - rowmean(x1)
    rstd2 = lax.rsqrt(rowmean(center * center) + EPS)
    hat2 = center * rstd2
    hat2_s[...] = hat2
    xn2 = (hat2 * ga2 + be2).astype(BF)
    xn2_s[...] = xn2
    put(dot_nn(pt_s[...], xn2_s[:, pl.ds(col, HW)]), xs, xst)


    def send_rows(c):
        spread(max(1, c * KC), (c + 1) * KC, xs, xr.at[tn], ahead, row_sems[c])
        if tail and c + 1 == chunks:
            spread(1, n, xst, xrt.at[tn], ahead, odd_rows)

    send_rows(0)
    xr[tn, 0] = xs[0]
    if tail:
        xrt[tn, 0] = xst[0]

    logits = dot_nt(xn2, wr)
    l0 = rowsum(jnp.where(h0, logits, 0.0))
    l1 = rowsum(jnp.where(h1, logits, 0.0))
    top = jnp.maximum(l0, l1)
    e0, e1 = jnp.exp(l0 - top), jnp.exp(l1 - top)
    gate0, gate1 = e0 / (e0 + e1), e1 / (e0 + e1)
    islot = iota((T, LANES), 1).astype(F32)
    at0 = (slot0 == islot).astype(F32).astype(BF)
    at1 = (slot1 == islot).astype(F32).astype(BF)
    gate_rows = jnp.zeros((n, LANES), F32)
    for hh, gg, at in ((hk0, gate0, at0), (hk1, gate1, at1)):
        for part in halves(jnp.where(hh, gg, 0.0)):
            gate_rows = gate_rows + dot_tn(part, at)
    growst[:, 0, :] = gate_rows
    gate_sem = next(counter)
    spread(1, n, growst, grow, ahead, gate_sem)
    grow[0] = growst[0]
    for c in range(1, chunks):
        if c >= EARLY:
            send_cotangent(c)
        send_rows(c)

    FT = 256
    c0 = math.sqrt(2.0 / math.pi)
    MC = KC * R
    half_sems = [next(counter) for _ in range(chunks)]
    dx_half = [next(counter) for _ in range(chunks)]
    e_half = next(counter)
    dx_sem = next(counter)

    def rows_of(c):
        return slice(c * MC, (c + 1) * MC if c + 1 < chunks else M)

    def send_dx(c):
        rc = rows_of(c)
        finish(tsend.at[0, rc], dx_half[c])
        own = own_s[rc]
        own = own + trecv[0, rc].astype(F32)
        dxs[c * KC : (c + 1) * KC] = own[0:MC].reshape(KC, R, HW).astype(BF)
        spread(max(1, c * KC), (c + 1) * KC, dxs, dxr, behind, dx_sem)
        if c == 0:
            dxr[0] = dxs[0]
        if tail and c + 1 == chunks:
            dxst[:, 0, :] = own[MC:].astype(BF)
            spread(1, n, dxst, dxrt, behind, odd_dx)
            dxrt[0] = dxst[0]

    def arrive(c):
        low = max(1, c * KC)
        kc = pl.ds(c * KC, KC)
        finish(gr.at[:, pl.ds(low, (c + 1) * KC - low)], row_sems[c])
        for buf in (gr, xr):
            remote(buf.at[tn, kc], buf.at[tn, kc], half_sems[c], partner).start()
        if tail and c + 1 == chunks:
            finish(grt.at[:, pl.ds(0, n - 1)], odd_rows)
            for buf in (grt, xrt):
                remote(buf.at[tn], buf.at[tn], odd_half, partner).start()

    def arrived(c):
        finish(gr.at[:, pl.ds(c * KC, KC)], half_sems[c])
        if tail and c + 1 == chunks:
            finish(grt, odd_half)

    row, block = iota((M, n), 0), iota((M, n), 1)
    inner = row - block * R
    is_odd = row - n * R == block
    in_body = jnp.logical_and(jnp.logical_and(inner >= 0, inner < R), row < n * R)
    sel_s[...] = jnp.logical_or(in_body, is_odd).astype(F32).astype(BF)
    at_slot = rowsum(jnp.where(in_body, inner, 0).astype(F32)) + jnp.where(row[:, 0:1] < n * R, 0.0, float(R))
    one_s[...] = (at_slot == iota((M, LANES), 1).astype(F32)).astype(F32)
    row, block = iota((n, M), 1), iota((n, M), 0)
    inner = row - block * R
    in_body = jnp.logical_and(jnp.logical_and(inner >= 0, inner < R), row < n * R)
    selt_s[...] = jnp.logical_or(in_body, row - n * R == block).astype(F32).astype(BF)

    arrive(0)
    for c in range(chunks):
        rc = rows_of(c)
        arrived(c)
        for hf in range(2):
            wide = slice(hf * HW, (hf + 1) * HW)
            body = slice(c * MC, (c + 1) * MC)
            x2[body, wide] = xr[hf, c * KC : (c + 1) * KC].reshape(MC, HW)
            c2[body, wide] = gr[hf, c * KC : (c + 1) * KC].reshape(MC, HW)
            if tail and c + 1 == chunks:
                x2[n * R :, wide] = xrt[hf, :, 0, :]
                c2[n * R :, wide] = grt[hf, :, 0, :]

        def first(i, _):
            f = pl.ds(pl.multiple_of(i * FT, FT), FT)
            h = dot_nn(x2[rc], win_s[:, f]) + ebin_ref[:, f]
            hh = h * h
            half = 0.5 + 0.5 * jnp.tanh(h * (c0 + (0.044715 * c0) * hh))
            act = (h * half).astype(BF)
            a_s[rc, f] = act
            slope = half + (half - half * half) * (h * (2 * c0 + (6 * 0.044715 * c0) * hh))
            da = dot_nt(c2[rc], wout_s[f, :])
            dh_s[rc, f] = (slope * da).astype(BF)
            both = act.astype(F32) * da
            for j in range(FT // LANES):
                dgp_s[rc] = dgp_s[rc] + both[:, j * LANES : (j + 1) * LANES]
            return 0

        own_g = c2[rc, pl.ds(col, HW)].astype(F32) * ebout_ref[:, pl.ds(col, HW)]
        dgp_s[rc] = sum(own_g[:, j * LANES : (j + 1) * LANES] for j in range(HW // LANES))
        lax.fori_loop(0, F // FT // 2, first, 0)
        if c > 0:
            send_dx(c - 1)
        if c + 1 < chunks:
            arrive(c + 1)
        lax.fori_loop(F // FT // 2, F // FT, first, 0)
        tsend[0, rc] = dot_nt(dh_s[rc], win_s[pl.ds(ocol, HW), :]).astype(BF)
        remote(tsend.at[0, rc], trecv.at[0, rc], dx_half[c], partner).start()
        own_s[rc] = dot_nt(dh_s[rc], win_s[pl.ds(col, HW), :])
    dgate = rowsum(dgp_s[...])
    dg_rows = jnp.zeros((n, LANES), F32)
    for part in halves(one_s[...] * dgate):
        dg_rows = dg_rows + dot_nn(selt_s[...], part)
    dgst[:, 0, :] = dg_rows
    dg_sem, dg_own = next(counter), next(counter)
    spread(1, n, dgst, dgr.at[tn], behind, dg_sem)
    spread(1, n, dgst, dgr.at[tn], behind, dg_sem, other)
    own_gate = remote(dgst.at[0], dgr.at[tn, 0], dg_own, partner)
    own_gate.start()
    dgr[tn, 0] = dgst[0]
    send_dx(chunks - 1)

    for c in range(chunks):
        rc = rows_of(c)
        tsend[1, rc] = dot_nn(a_s[rc], wout_s[:, pl.ds(ocol, HW)]).astype(BF)
        remote(tsend.at[1, rc], trecv.at[1, rc], e_half, partner).start()
    for c in range(chunks):
        rc = rows_of(c)
        own_s[rc] = dot_nn(a_s[rc], wout_s[:, pl.ds(col, HW)])
    finish(tsend.at[1], e_half)
    put(own_s[...] + trecv[1].astype(F32) + ebout_ref[:, pl.ds(col, HW)], es, est)
    e_sem = next(counter)
    spread(1, n, es, er, behind, e_sem)
    er[0] = es[0]
    if tail:
        spread(1, n, est, ert, behind, odd_e)
        ert[0] = est[0]

    finish(dgr.at[:, pl.ds(0, n - 1)], dg_sem)
    own_gate.wait()
    dg_all = dgr[0, :, 0, :] + dgr[1, :, 0, :]
    hb0, hb1 = hk0.astype(F32).astype(BF), hk1.astype(F32).astype(BF)
    dg0 = rowsum(jnp.where(slot0 == islot, pick_nn(hb0, dg_all), 0.0))
    dg1 = rowsum(jnp.where(slot1 == islot, pick_nn(hb1, dg_all), 0.0))
    mean_gate = gate0 * dg0 + gate1 * dg1
    dl0, dl1 = gate0 * (dg0 - mean_gate), gate1 * (dg1 - mean_gate)
    dlog = (jnp.where(h0, dl0, 0.0) + jnp.where(h1, dl1, 0.0)).astype(BF)

    finish(dxr.at[pl.ds(0, n - 1)], dx_sem)
    if tail:
        finish(dxrt.at[pl.ds(0, n - 1)], odd_dx)

    hsend[...] = picked(dxr, dxrt)
    h_sem = next(counter)
    hc = remote(hsend, hrecv.at[tn], h_sem, partner)
    hc.start()
    hrecv[tn] = hsend[...]
    by_router = dot_nn(dlog, wr)

    hc.wait()
    cot_copy.wait()

    dxn2 = jnp.concatenate([hrecv[0], hrecv[1]], -1) + by_router
    hat2 = hat2_s[...]
    gg2, gb2 = colsum(dxn2 * hat2), colsum(dxn2)
    u = dxn2 * ga2
    dx1 = jnp.concatenate([cotf[0], cotf[1]], -1).astype(F32) + rstd2 * (u - rowmean(u) - hat2 * rowmean(u * hat2))
    dx1_s[...] = dx1
    datt = dx1.astype(BF)
    do = dot_nn(datt, weight(3)).astype(BF)

    first_sems = [next(counter) for _ in range(5)]
    second_sems = [next(counter)] * 4 + [next(counter)]

    def to_plane(i, src, dst):
        for j in range(1, plane):
            remote(src.at[:, lax.rem(spot + j, plane)], dst.at[j - 1], first_sems[i], {"expert": in_plane(j)}).start()

    def to_line(i, src, got, mid, dst):
        finish(got, first_sems[i])
        total = src[:, spot].astype(F32)
        for j in range(plane - 1):
            total = total + got[j].astype(F32)
        mid[...] = total.astype(BF)
        for k in range(1, lines):
            there = in_line(k)
            remote(mid.at[there], dst.at[k], second_sems[i], {"expert": there * plane + spot}).start()
        dst[0] = mid[line]

    def gradient(i, value):
        gsend[i] = value.reshape(lines, plane, rows, HW).astype(BF)
        to_plane(i, gsend.at[i], r1.at[i])

    gradient(0, dot_tn(datt, o_s[...]))

    dqs, dks, dvs = [], [], []
    for h in range(heads):
        sl = slice(h * HEAD_DIM, (h + 1) * HEAD_DIM)
        p = p_s[h]
        doh = do[:, sl]
        dp = dot_nt(doh, qkv_s[2, :, sl])
        dvs.append(dot_tn(p.astype(BF), doh))
        ds = (p * (dp - rowsum(p * dp))).astype(BF)
        dqs.append(dot_nn(ds, qkv_s[1, :, sl]) * scale)
        dks.append(dot_tn(ds, qkv_s[0, :, sl]) * scale)
    for i, v in enumerate((dqs, dks, dvs)):
        dqkv_s[i] = jnp.concatenate(v, -1).astype(BF)

    bfpart[0] = (
        dot_nt(dqkv_s[0], weight(0)) + dot_nt(dqkv_s[1], weight(1)) + dot_nt(dqkv_s[2], weight(2))
    ).astype(BF)
    b_sem = next(counter)
    bc = remote(bfpart.at[0], bfpart.at[1], b_sem, partner)
    bc.start()

    for i in range(3):
        gradient(i + 1, dot_tn(xn1_s[...], dqkv_s[i]))

    bc.wait()
    dxn1 = bfpart[0].astype(F32) + bfpart[1].astype(F32)
    hat1 = hat1_s[...]
    gg1, gb1 = colsum(dxn1 * hat1), colsum(dxn1)
    u = dxn1 * ga1
    gx_ref[...] = dx1_s[...] + rstd1 * (u - rowmean(u) - hat1 * rowmean(u * hat1))

    smsend[...] = jnp.zeros(smsend.shape, F32)
    smsend[0:n] = dot_tn(dlog, xn2_s[...])
    smsend[n : n + 1] = gg1
    smsend[n + 1 : n + 2] = gb1
    smsend[n + 2 : n + 3] = gg2
    smsend[n + 3 : n + 4] = gb2
    ssend[...] = smsend[...].T.reshape(lines, plane, rows, ssend.shape[3]).astype(BF)
    to_plane(4, ssend, sr1)
    to_line(0, gsend.at[0], r1.at[0], r2s.at[0], rs_ref.at[0])

    finish(grow.at[pl.ds(0, n - 1)], gate_sem)
    gate_col = rowsum(one_s[...] * pick_nn(sel_s[...], grow[:, 0, :]))
    gated = gate_col * c2[...].astype(F32)
    c2[...] = gated.astype(BF)
    gbout_ref[...] = colsum(gated)
    x2[...] = (gate_col * x2[...].astype(F32)).astype(BF)
    lane = iota((M, LANES), 1)
    gate_parts = halves(gate_col)
    gate_lanes = sum(jnp.where(lane == i, part.astype(F32), 0.0) for i, part in enumerate(gate_parts)).astype(BF)

    def grads(i, _):
        f = pl.ds(pl.multiple_of(i * FT, FT), FT)
        gwout_ref[f, :] = dot_tn(a_s[:, f], c2[...])
        gwin_ref[:, f] = dot_tn(x2[...], dh_s[:, f])
        gbin_ref[:, f] = colsum(dot_tn(gate_lanes, dh_s[:, f]))
        return 0

    lax.fori_loop(0, F // FT, grads, 0)
    outs = [(gwin_ref, gwin_out), (gwout_ref, gwout_out), (gbin_ref, gbin_out), (gbout_ref, gbout_out), (gx_ref, gx_out)]
    outs = [pltpu.make_async_copy(src, dst, hbm_sem.at[i]) for i, (src, dst) in enumerate(outs)]
    for move in outs:
        move.start()

    finish(er.at[pl.ds(0, n - 1)], e_sem)
    if tail:
        finish(ert.at[pl.ds(0, n - 1)], odd_e)

    y = x1_s[:, pl.ds(col, HW)] + picked(er, ert)
    y_ref[...] = y.astype(BF)
    outs.append(pltpu.make_async_copy(y_ref, y_out, hbm_sem.at[5]))
    outs[-1].start()

    for i in range(1, 4):
        to_line(i, gsend.at[i], r1.at[i], r2s.at[i], rs_ref.at[i])
    to_line(4, ssend, sr1, s2s, rsmall_ref)

    for move in outs:
        move.wait()

    finish(rs_ref.at[:, pl.ds(1, lines - 1)], second_sems[0])
    finish(rsmall_ref.at[pl.ds(1, lines - 1)], second_sems[4])


def last_kernel(
    y_in, gx_in, rs, rsmall, gwin_in, gbin_in, gwout_in, gbout_in,
    y, gx, gq, gk, gv, go, gr, a1, b1, a2, b2, gwin, gbin, gwout, gbout,
    sums, turned, lines_s, sem,
):
    n, rows = gr.shape
    moves = [(gwin_in, gwin), (gwout_in, gwout), (gx_in, gx), (y_in, y), (gbin_in, gbin), (gbout_in, gbout)]
    moves += [(sums.at[i], ref) for i, ref in enumerate((go, gq, gk, gv))]
    moves += [(turned, gr)] + [(lines_s.at[i], ref) for i, ref in enumerate((a1, b1, a2, b2))]
    copies = [pltpu.make_async_copy(src, dst, sem.at[i]) for i, (src, dst) in enumerate(moves)]
    for c in copies[:6]:
        c.start()
    small = jnp.sum(rsmall[...].astype(F32), 0).T
    turned[...] = small[0:n, 0:rows]
    for i in range(4):
        lines_s[i] = small[n + i : n + i + 1, 0:rows]
        sums[i] = jnp.sum(rs[i].astype(F32), 0)
    for c in copies[6:]:
        c.start()
    for c in copies:
        c.wait()


def shards(
    block_input, routes, w_query, w_key, w_value, w_output, w_router, norm1_gain, norm1_bias, norm2_gain, norm2_bias,
    expert_in, expert_in_bias, expert_out, expert_out_bias, cotangent,
):
    z = Sizes()
    z.n = lax.axis_size("expert")
    z.T, z.D = block_input.shape
    z.HW = cotangent.shape[1]
    z.F = expert_in.shape[2]
    z.rows = w_query.shape[0]
    z.heads = z.HW // HEAD_DIM
    experts, topk = w_router.shape[1], routes.shape[1]
    cap = max(2, 2 * topk * z.T // experts)
    z.tail = 1 if cap > 8 and cap % 8 == 1 else 0
    z.R = cap - 1 if z.tail else -(-cap // 8) * 8
    z.M = z.n * (z.R + z.tail)
    z.lines = 4
    z.plane = z.n // z.lines
    z.chunks = CHUNKS
    z.sems = 49
    n, T, D, HW, R, F, rows, M = z.n, z.T, z.D, z.HW, z.R, z.F, z.rows, z.M
    lines, plane = z.lines, z.plane
    wide = -(-(n + 4) // LANES) * LANES
    vm = pl.BlockSpec(memory_space=pltpu.VMEM)
    hbm = pl.BlockSpec(memory_space=pl.ANY)
    out_shape = (
        jax.ShapeDtypeStruct((T, HW), BF),
        jax.ShapeDtypeStruct((T, D), F32),
        jax.ShapeDtypeStruct((4, lines, rows, HW), BF),
        jax.ShapeDtypeStruct((lines, rows, wide), BF),
        jax.ShapeDtypeStruct((D, F), F32),
        jax.ShapeDtypeStruct((1, F), F32),
        jax.ShapeDtypeStruct((F, D), F32),
        jax.ShapeDtypeStruct((1, D), F32),
    )
    V = pltpu.VMEM
    args = (
        block_input, routes.T, w_query, w_key, w_value, w_output.T, w_router.T,
        norm1_gain[None], norm1_bias[None], norm2_gain[None], norm2_bias[None],
        expert_in_bias, expert_out_bias, cotangent, expert_in, expert_out,
    )
    tp = -(-T // LANES) * LANES
    scratch = [
        *(V(out_shape[i].shape, out_shape[i].dtype) for i in (0, 1, 4, 5, 6, 7)),
        V((D, F), F32), V((F, D), F32), V((D, F), BF), V((F, D), BF), V((wide, LANES), F32), V((8, tp), F32), V((tp, LANES), F32),
        V((n, 2 * rows + rows * wide // HW, HW), BF), V((n, 2 * rows, HW), BF),
        V((M, T), BF), V((2, T, M), BF), V((M, n), BF), V((n, M), BF), V((M, LANES), F32), V((M, LANES), F32), V((M, HW), F32), V((T, D), F32), V((T, D), BF), V((3, T, HW), BF), V((z.heads, T, T), F32),
        V((T, HW), BF), V((T, D), BF), V((T, D), BF),
        V((T, D), F32), V((T, D), F32), V((T, D), BF), V((2, T, HW), BF),
        V((n, R, HW), BF), V((2, n, R, HW), BF), V((n, R, HW), BF), V((2, n, R, HW), BF),
        V((n, 1, HW), BF), V((2, n, 1, HW), BF), V((n, 1, HW), BF), V((2, n, 1, HW), BF),
        *[V((n, 1, HW), BF)] * 4,
        V((n, 1, LANES), F32), V((n, 1, LANES), F32), V((M, D), BF), V((M, D), BF), V((M, F), BF), V((M, F), BF),
        V((2, M, HW), BF), V((2, M, HW), BF), V((n, R, HW), BF), V((n, R, HW), BF), V((n, R, HW), BF), V((n, R, HW), BF),
        V((n, 1, LANES), F32), V((2, n, 1, LANES), F32), V((T, HW), F32), V((2, T, HW), F32), V((T, D), F32), V((3, T, HW), BF),
        V((4, lines, plane, rows, HW), BF), V((4, plane - 1, lines, rows, HW), BF), V((4, lines, rows, HW), BF), V((wide, D), F32),
        V((lines, plane, rows, wide), BF), V((plane - 1, lines, rows, wide), BF), V((lines, rows, wide), BF), V((2, T, D), BF),
        *(V(v.shape, v.dtype) for v in args[:14]),
        pltpu.SemaphoreType.DMA((16,)), pltpu.SemaphoreType.DMA((z.sems,)), pltpu.SemaphoreType.DMA((z.sems,)),
    ]
    kept = [pltpu.VMEM(v.shape, v.dtype) for v in out_shape]
    done = pl.pallas_call(
        functools.partial(block_kernel, z),
        out_shape=kept,
        in_specs=[pl.BlockSpec(memory_space=pltpu.HBM)] * 16,
        out_specs=[hbm] * 2 + [vm] * 2 + [hbm] * 4,
        scratch_shapes=scratch,
        compiler_params=pltpu.CompilerParams(collective_id=0, has_side_effects=True, vmem_limit_bytes=52 << 20),
        name="block",
    )(
        *(pltpu.with_memory_space_constraint(v, pltpu.HBM) for v in args)
    )
    square = jax.ShapeDtypeStruct((rows, HW), F32)
    line = jax.ShapeDtypeStruct((1, rows), F32)
    last_shape = (
        out_shape[0], out_shape[1], square, square, square, square, jax.ShapeDtypeStruct((n, rows), F32), line, line, line, line,
        out_shape[4], out_shape[5], out_shape[6], out_shape[7],
    )
    y, gx, gq, gk, gv, go, gr, a1, b1, a2, b2, gwin, gbin, gwout, gbout = pl.pallas_call(
        last_kernel,
        out_shape=last_shape,
        in_specs=[hbm] * 2 + [vm] * 2 + [hbm] * 4,
        out_specs=[hbm] * 15,
        scratch_shapes=[
            V((4, rows, HW), F32), V((n, rows), F32), V((4, 1, rows), F32), pltpu.SemaphoreType.DMA((15,)),
        ],
        compiler_params=pltpu.CompilerParams(vmem_limit_bytes=8 << 20),
        name="last",
    )(*done)
    return (y, gx, gq, gk, gv, go.T, gr.T, a1[0], b1[0], a2[0], b2[0], gwin[None], gbin, gwout[None], gbout)


def solution(mesh):
    row, col = P("expert", None), P("expert", "tensor")
    vec = P("expert")
    in_specs = (
        row, row, col, col, col, P("tensor", "expert"), row, vec, vec, vec, vec,
        P("expert", None, "tensor"), col, P("expert", "tensor", None), row, col,
    )
    out_specs = (
        col, row, col, col, col, P("tensor", "expert"), row, vec, vec, vec, vec,
        P("expert", None, "tensor"), col, P("expert", "tensor", None), row,
    )
    return jax.shard_map(shards, mesh=mesh, in_specs=in_specs, out_specs=out_specs, check_vma=False)
```

```python
import functools
import math

import jax
import jax.numpy as jnp
from jax import lax
from jax.experimental import pallas as pl
from jax.experimental.pallas import tpu as pltpu
from jax.sharding import PartitionSpec as P

HEAD_DIM = 64
EPS = 1e-06
MESH = pl.DeviceIdType.MESH
BF = jnp.bfloat16
F32 = jnp.float32
LANES = 128
CHUNKS = 4
LINE_FIRST = (1,)
ORDER = (1, 2, 3)
EARLY = 3


def dot_nn(a, b):
    return lax.dot_general(a, b, (((1,), (0,)), ((), ())), preferred_element_type=F32)


def dot_nt(a, b):
    return lax.dot_general(a, b, (((1,), (1,)), ((), ())), preferred_element_type=F32)


def dot_tn(a, b):
    return lax.dot_general(a, b, (((0,), (0,)), ((), ())), preferred_element_type=F32)


def halves(v):
    first = v.astype(BF)
    rest = v - first.astype(F32)
    second = rest.astype(BF)
    return first, second, (rest - second.astype(F32)).astype(BF)


def pick_nn(select, v):
    a, b, c = halves(v)
    return dot_nn(select, a) + dot_nn(select, b) + dot_nn(select, c)


def colsum(v):
    return jnp.sum(v, axis=0, keepdims=True)


def rowmean(v):
    return jnp.mean(v, -1, keepdims=True)


def rowsum(v):
    return jnp.sum(v, -1, keepdims=True)


def iota(shape, axis):
    return lax.broadcasted_iota(jnp.int32, shape, axis)


class Sizes:
    pass


def block_kernel(
    z,
    x_hbm, routes_hbm, wq_hbm, wk_hbm, wv_hbm, wo_hbm, wr_hbm, ga1_hbm, be1_hbm, ga2_hbm, be2_hbm, ebin_hbm, ebout_hbm, cot_hbm,
    win_hbm, wout_hbm,
    y_out, gx_out, rs_ref, rsmall_ref, gwin_out, gbin_out, gwout_out, gbout_out,
    y_ref, gx_ref, gwin_ref, gbin_ref, gwout_ref, gbout_ref,
    win32, wout32, win_s, wout_s, square, flat, pads,
    wa, wb, pt_s, pick_s, sel_s, selt_s, one_s, dgp_s, own_s, hat1_s, xn1_s, qkv_s, p_s, o_s, parts, partr,
    x1_s, hat2_s, xn2_s, cotf, gs, gr, xs, xr, gst, grt, xst, xrt, est, ert, dxst, dxrt, growst, grow, x2, c2, a_s, dh_s,
    tsend, trecv, es, er, dxs, dxr, dgst, dgr, hsend, hrecv, dx1_s, dqkv_s, gsend, r1, r2s, smsend, ssend, sr1, s2s, bfpart,
    x_ref, routes_ref, wq_ref, wk_ref, wv_ref, wo_ref, wr_ref, ga1_ref, be1_ref, ga2_ref, be2_ref, ebin_ref, ebout_ref, cot_ref,
    hbm_sem, send_sem, recv_sem,
):
    tail = z.tail
    n, T, D, HW, R, F, rows, M, heads = z.n, z.T, z.D, z.HW, z.R, z.F, z.rows, z.M, z.heads
    lines, plane, chunks = z.lines, z.plane, z.chunks
    KC = n // chunks
    me = lax.axis_index("expert")
    tn = lax.axis_index("tensor")
    other = 1 - tn
    partner = {"tensor": other}
    line, spot = me // plane, lax.rem(me, plane)
    col = pl.multiple_of(tn * HW, HW)
    ocol = pl.multiple_of(other * HW, HW)
    counter = iter(range(z.sems))

    low_bit, high_bit = lax.rem(line, 2), line // 2

    def other_line(c):
        a, b = lax.rem(c, 2), c // 2
        return (high_bit + b - 2 * high_bit * b) * 2 + low_bit + a - 2 * low_bit * a

    def ahead(k):
        return other_line(lax.rem(k, lines)) * plane + lax.rem(spot + k // lines, plane)

    def behind(k):
        return other_line(lax.rem(k, lines)) * plane + lax.rem(spot - k // lines + plane, plane)

    def in_line(k):
        return lax.rem(line + k, lines)

    def in_plane(j):
        return line * plane + lax.rem(spot + j, plane)

    barrier = pltpu.get_barrier_semaphore()

    def greet(k, _):
        pl.semaphore_signal(barrier, inc=1, device_id={"expert": ahead(k)}, device_id_type=MESH)
        return 0

    lax.fori_loop(1, n, greet, 0)
    pl.semaphore_signal(barrier, inc=1, device_id=partner, device_id_type=MESH)

    moves = (
        (wq_hbm, wq_ref), (wk_hbm, wk_ref), (wv_hbm, wv_ref), (wo_hbm, wo_ref), (wr_hbm, wr_ref),
        (ga1_hbm, ga1_ref), (be1_hbm, be1_ref), (ga2_hbm, ga2_ref), (be2_hbm, be2_ref),
        (routes_hbm, routes_ref), (cot_hbm, cot_ref), (x_hbm, x_ref), (ebin_hbm, ebin_ref), (ebout_hbm, ebout_ref),
        (win_hbm.at[0], win32), (wout_hbm.at[0], wout32),
    )
    moves = [pltpu.make_async_copy(src, dst, hbm_sem.at[i]) for i, (src, dst) in enumerate(moves)]
    for move in moves:
        move.start()
    win_copy, wout_copy = moves[14:]

    def remote(src, dst, i, dev):
        return pltpu.make_async_remote_copy(
            src_ref=src, dst_ref=dst, send_sem=send_sem.at[i], recv_sem=recv_sem.at[i], device_id=dev, device_id_type=MESH
        )

    def spread(low, high, src, dst, to, i, core=None):
        def step(at, _):
            k = high - 1 - at
            dev = {"expert": to(k)}
            if core is not None:
                dev["tensor"] = core
            remote(src.at[k], dst.at[k], i, dev).start()
            return 0

        lax.fori_loop(0, high - low, step, 0)

    def finish(ref, i):
        d = remote(ref, ref, i, partner)
        d.wait_send()
        d.wait_recv()

    def put(value, body, odd):
        body[...] = value[0 : n * R].reshape(n, R, HW).astype(BF)
        if tail:
            odd[:, 0, :] = value[n * R :].astype(BF)

    def picked(body, odd):
        total = 0.0
        for pick, gate in ((pick_s.at[0], gate0), (pick_s.at[1], gate1)):
            value = dot_nn(pick[:, 0 : n * R], body[...].reshape(n * R, HW))
            if tail:
                value = value + dot_nn(pick[:, n * R :], odd[:, 0, :])
            total = total + gate * value
        return total

    for move in moves[:9]:
        move.wait()
    wide, sr = square.shape[0], wa.shape[1] - 2 * rows
    wa[me, 0:rows] = wq_ref[...].astype(BF)
    wa[me, rows : 2 * rows] = wk_ref[...].astype(BF)
    wb[me, 0:rows] = wv_ref[...].astype(BF)
    wb[me, rows : 2 * rows] = wo_ref[...].astype(BF)
    square[...] = jnp.zeros(square.shape, F32)
    square[0:n, 0:rows] = wr_ref[...]
    for i, ref in enumerate((ga1_ref, be1_ref, ga2_ref, be2_ref)):
        square[n + i : n + i + 1, 0:rows] = ref[...]
    turned = square[...].T
    for i in range(HW // wide):
        wa[me, 2 * rows :, i * wide : (i + 1) * wide] = turned[i * sr : (i + 1) * sr].astype(BF)

    pl.semaphore_wait(barrier, n)

    line_a = [None] + [next(counter) for _ in range(lines - 1)]
    line_b = [None] + [next(counter) for _ in range(lines - 1)]
    square_plane = plane == 4
    if square_plane:
        near_a = [next(counter) for _ in range(lines)]
        near_b = [next(counter) for _ in range(lines)]
        far_a, far_b = next(counter), next(counter)
        side, over = spot + 1 - 2 * lax.rem(spot, 2), lax.rem(spot + 2, 4)
        to_side, to_over = {"expert": line * plane + side}, {"expert": line * plane + over}
    else:
        plane_a, plane_b = next(counter), next(counter)

    def share(s):
        block = other_line(s) * plane + spot
        if square_plane:
            remote(wa.at[block], wa.at[block], near_a[s], to_side).start()
            remote(wb.at[block], wb.at[block], near_b[s], to_over).start()
            remote(wa.at[block], wa.at[block], far_a, to_over).start()
            remote(wb.at[block], wb.at[block], far_b, to_side).start()
        else:
            for j in range(1, plane):
                remote(wa.at[block], wa.at[block], plane_a, {"expert": in_plane(j)}).start()
                remote(wb.at[block], wb.at[block], plane_b, {"expert": in_plane(j)}).start()

    def hand_on(s):
        if square_plane:
            finish(wa.at[0], near_a[s])
            block = other_line(s) * plane + side
            remote(wa.at[block], wa.at[block], far_a, to_over).start()
            finish(wb.at[0], near_b[s])
            block = other_line(s) * plane + over
            remote(wb.at[block], wb.at[block], far_b, to_side).start()

    for k in range(1, lines):
        dev = {"expert": other_line(k) * plane + spot}
        remote(wa.at[me], wa.at[me], line_a[k], dev).start()
        remote(wb.at[me], wb.at[me], line_b[k], dev).start()
    share(0)

    moves[9].wait()
    flat[0:2, 0:T] = routes_ref[...].astype(F32)
    r = flat[...].T
    r0, r1_ = r[0:T, 0:1], r[0:T, 1:2]
    ie = iota((T, n), 1).astype(F32)
    h0, h1 = r0 == ie, r1_ == ie
    above = [(ie >= i * plane).astype(F32) for i in range(1, lines)]
    line_of = sum(above)
    high_of = above[1]
    low_of = line_of - 2 * high_of
    low_f, high_f = low_bit.astype(F32), high_bit.astype(F32)
    turn = ie - line_of * plane - spot.astype(F32)
    turn = jnp.where(turn < 0, turn + plane, turn)
    place = (high_of - high_f) ** 2 * 2 + (low_of - low_f) ** 2 + turn * lines
    k0, k1 = rowsum(jnp.where(h0, place, 0.0)), rowsum(jnp.where(h1, place, 0.0))
    hk0, hk1 = k0 == ie, k1 == ie
    hit = jnp.logical_or(hk0, hk1).astype(F32).astype(BF)
    tri = (iota((T, T), 0) > iota((T, T), 1)).astype(F32).astype(BF)
    count = dot_nn(tri, hit)
    slot0 = rowsum(jnp.where(hk0, count, 0.0))
    slot1 = rowsum(jnp.where(hk1, count, 0.0))
    pos0 = jnp.where(slot0 < R, k0 * R + slot0, k0 + n * R)
    pos1 = jnp.where(slot1 < R, k1 * R + slot1, k1 + n * R)
    pads[...] = jnp.full(pads.shape, -1.0, F32)
    pads[0:T, 0:1] = pos0
    pads[0:T, 1:2] = pos1
    post = pads[...].T
    slots = iota((M, T), 0).astype(F32)
    pt_s[...] = jnp.logical_or(slots == post[0:1, 0:T], slots == post[1:2, 0:T]).astype(F32).astype(BF)

    moves[10].wait()
    put(dot_nn(pt_s[...], cot_ref[...]), gs, gst)
    cotf[tn] = cot_ref[...]
    cot_sem = next(counter)
    cot_copy = remote(cot_ref, cotf.at[tn], cot_sem, partner)
    cot_copy.start()

    for move in moves[11:14]:
        move.wait()
    x = x_ref[...].astype(F32)
    center = x - rowmean(x)
    rstd1 = lax.rsqrt(rowmean(center * center) + EPS)
    hat1_s[...] = center * rstd1

    slot_lane = iota((T, M), 1).astype(F32)
    pick_s[0] = (slot_lane == pos0).astype(F32).astype(BF)
    pick_s[1] = (slot_lane == pos1).astype(F32).astype(BF)
    gr[tn, 0] = gs[0]
    if tail:
        grt[tn, 0] = gst[0]
    win_copy.wait()
    win_s[...] = win32[...].astype(BF)
    wout_copy.wait()
    wout_s[...] = wout32[...].astype(BF)

    for k in range(1, lines):
        finish(wa.at[0], line_a[k])
        finish(wb.at[0], line_b[k])
        share(k)
        hand_on(k - 1)

    row_sems = [next(counter) for _ in range(chunks)]
    odd_rows, odd_half, odd_dx, odd_e = (next(counter) for _ in range(4))

    def send_cotangent(c):
        spread(max(1, c * KC), (c + 1) * KC, gs, gr.at[tn], ahead, row_sems[c])
        if tail and c + 1 == chunks:
            spread(1, n, gst, grt.at[tn], ahead, odd_rows)

    send_cotangent(0)

    hand_on(lines - 1)

    if square_plane:
        finish(wa.at[pl.ds(0, 2 * lines)], far_a)
    else:
        finish(wa.at[pl.ds(0, (plane - 1) * lines)], plane_a)
    small = jnp.concatenate([wa[:, 2 * rows :, i * wide : (i + 1) * wide] for i in range(HW // wide)], 1)
    small = small.astype(F32).reshape(n * rows, wide).T
    ga1, be1 = small[n : n + 1], small[n + 1 : n + 2]
    ga2, be2 = small[n + 2 : n + 3], small[n + 3 : n + 4]
    wr = small[0:n].astype(BF)
    xn1 = (hat1_s[...] * ga1 + be1).astype(BF)
    xn1_s[...] = xn1

    def weight(i):
        ref = wb if i >= 2 else wa
        return ref[:, i % 2 * rows : (i % 2 + 1) * rows].reshape(D, HW)

    for i in range(2):
        qkv_s[i] = dot_nn(xn1, weight(i)).astype(BF)

    if square_plane:
        finish(wb.at[pl.ds(0, 2 * lines)], far_b)
    else:
        finish(wb.at[pl.ds(0, (plane - 1) * lines)], plane_b)
    scale = 1.0 / math.sqrt(HEAD_DIM)

    for c in range(1, EARLY):
        send_cotangent(c)

    qkv_s[2] = dot_nn(xn1, weight(2)).astype(BF)

    outs = []
    for h in range(heads):
        sl = slice(h * HEAD_DIM, (h + 1) * HEAD_DIM)
        s = dot_nt(qkv_s[0, :, sl], qkv_s[1, :, sl]) * scale
        ex = jnp.exp(s - jnp.max(s, -1, keepdims=True))
        p = ex / rowsum(ex)
        p_s[h] = p
        outs.append(dot_nn(p.astype(BF), qkv_s[2, :, sl]))
    o_s[...] = jnp.concatenate(outs, -1).astype(BF)

    parts[...] = dot_nt(o_s[...], weight(3)).astype(BF)
    part_sem = next(counter)
    part_copy = remote(parts, partr, part_sem, partner)
    part_copy.start()

    part_copy.wait()
    x1 = x_ref[...].astype(F32) + (parts[...].astype(F32) + partr[...].astype(F32))
    x1_s[...] = x1

    center = x1 - rowmean(x1)
    rstd2 = lax.rsqrt(rowmean(center * center) + EPS)
    hat2 = center * rstd2
    hat2_s[...] = hat2
    xn2 = (hat2 * ga2 + be2).astype(BF)
    xn2_s[...] = xn2
    put(dot_nn(pt_s[...], xn2_s[:, pl.ds(col, HW)]), xs, xst)


    def send_rows(c):
        spread(max(1, c * KC), (c + 1) * KC, xs, xr.at[tn], ahead, row_sems[c])
        if tail and c + 1 == chunks:
            spread(1, n, xst, xrt.at[tn], ahead, odd_rows)

    send_rows(0)
    xr[tn, 0] = xs[0]
    if tail:
        xrt[tn, 0] = xst[0]

    logits = dot_nt(xn2, wr)
    l0 = rowsum(jnp.where(h0, logits, 0.0))
    l1 = rowsum(jnp.where(h1, logits, 0.0))
    top = jnp.maximum(l0, l1)
    e0, e1 = jnp.exp(l0 - top), jnp.exp(l1 - top)
    gate0, gate1 = e0 / (e0 + e1), e1 / (e0 + e1)
    islot = iota((T, LANES), 1).astype(F32)
    at0 = (slot0 == islot).astype(F32).astype(BF)
    at1 = (slot1 == islot).astype(F32).astype(BF)
    gate_rows = jnp.zeros((n, LANES), F32)
    for hh, gg, at in ((hk0, gate0, at0), (hk1, gate1, at1)):
        for part in halves(jnp.where(hh, gg, 0.0)):
            gate_rows = gate_rows + dot_tn(part, at)
    growst[:, 0, :] = gate_rows
    gate_sem = next(counter)
    spread(1, n, growst, grow, ahead, gate_sem)
    grow[0] = growst[0]
    for c in range(1, chunks):
        if c >= EARLY:
            send_cotangent(c)
        send_rows(c)

    FT = 256
    c0 = math.sqrt(2.0 / math.pi)
    MC = KC * R
    half_sems = [next(counter) for _ in range(chunks)]
    dx_half = [next(counter) for _ in range(chunks)]
    e_half = next(counter)
    dx_sem = next(counter)

    def rows_of(c):
        return slice(c * MC, (c + 1) * MC if c + 1 < chunks else M)

    def send_dx(c):
        rc = rows_of(c)
        finish(tsend.at[0, rc], dx_half[c])
        own = own_s[rc]
        own = own + trecv[0, rc].astype(F32)
        dxs[c * KC : (c + 1) * KC] = own[0:MC].reshape(KC, R, HW).astype(BF)
        spread(max(1, c * KC), (c + 1) * KC, dxs, dxr, behind, dx_sem)
        if c == 0:
            dxr[0] = dxs[0]
        if tail and c + 1 == chunks:
            dxst[:, 0, :] = own[MC:].astype(BF)
            spread(1, n, dxst, dxrt, behind, odd_dx)
            dxrt[0] = dxst[0]

    def arrive(c):
        low = max(1, c * KC)
        kc = pl.ds(c * KC, KC)
        finish(gr.at[:, pl.ds(low, (c + 1) * KC - low)], row_sems[c])
        for buf in (gr, xr):
            remote(buf.at[tn, kc], buf.at[tn, kc], half_sems[c], partner).start()
        if tail and c + 1 == chunks:
            finish(grt.at[:, pl.ds(0, n - 1)], odd_rows)
            for buf in (grt, xrt):
                remote(buf.at[tn], buf.at[tn], odd_half, partner).start()

    def arrived(c):
        finish(gr.at[:, pl.ds(c * KC, KC)], half_sems[c])
        if tail and c + 1 == chunks:
            finish(grt, odd_half)

    row, block = iota((M, n), 0), iota((M, n), 1)
    inner = row - block * R
    is_odd = row - n * R == block
    in_body = jnp.logical_and(jnp.logical_and(inner >= 0, inner < R), row < n * R)
    sel_s[...] = jnp.logical_or(in_body, is_odd).astype(F32).astype(BF)
    at_slot = rowsum(jnp.where(in_body, inner, 0).astype(F32)) + jnp.where(row[:, 0:1] < n * R, 0.0, float(R))
    one_s[...] = (at_slot == iota((M, LANES), 1).astype(F32)).astype(F32)
    row, block = iota((n, M), 1), iota((n, M), 0)
    inner = row - block * R
    in_body = jnp.logical_and(jnp.logical_and(inner >= 0, inner < R), row < n * R)
    selt_s[...] = jnp.logical_or(in_body, row - n * R == block).astype(F32).astype(BF)

    arrive(0)
    for c in range(chunks):
        rc = rows_of(c)
        arrived(c)
        for hf in range(2):
            wide = slice(hf * HW, (hf + 1) * HW)
            body = slice(c * MC, (c + 1) * MC)
            x2[body, wide] = xr[hf, c * KC : (c + 1) * KC].reshape(MC, HW)
            c2[body, wide] = gr[hf, c * KC : (c + 1) * KC].reshape(MC, HW)
            if tail and c + 1 == chunks:
                x2[n * R :, wide] = xrt[hf, :, 0, :]
                c2[n * R :, wide] = grt[hf, :, 0, :]

        def first(i, _):
            f = pl.ds(pl.multiple_of(i * FT, FT), FT)
            h = dot_nn(x2[rc], win_s[:, f]) + ebin_ref[:, f]
            hh = h * h
            half = 0.5 + 0.5 * jnp.tanh(h * (c0 + (0.044715 * c0) * hh))
            act = (h * half).astype(BF)
            a_s[rc, f] = act
            slope = half + (half - half * half) * (h * (2 * c0 + (6 * 0.044715 * c0) * hh))
            da = dot_nt(c2[rc], wout_s[f, :])
            dh_s[rc, f] = (slope * da).astype(BF)
            both = act.astype(F32) * da
            for j in range(FT // LANES):
                dgp_s[rc] = dgp_s[rc] + both[:, j * LANES : (j + 1) * LANES]
            return 0

        own_g = c2[rc, pl.ds(col, HW)].astype(F32) * ebout_ref[:, pl.ds(col, HW)]
        dgp_s[rc] = sum(own_g[:, j * LANES : (j + 1) * LANES] for j in range(HW // LANES))
        lax.fori_loop(0, F // FT // 2, first, 0)
        if c > 0:
            send_dx(c - 1)
        if c + 1 < chunks:
            arrive(c + 1)
        lax.fori_loop(F // FT // 2, F // FT, first, 0)
        tsend[0, rc] = dot_nt(dh_s[rc], win_s[pl.ds(ocol, HW), :]).astype(BF)
        remote(tsend.at[0, rc], trecv.at[0, rc], dx_half[c], partner).start()
        own_s[rc] = dot_nt(dh_s[rc], win_s[pl.ds(col, HW), :])
    dgate = rowsum(dgp_s[...])
    dg_rows = jnp.zeros((n, LANES), F32)
    for part in halves(one_s[...] * dgate):
        dg_rows = dg_rows + dot_nn(selt_s[...], part)
    dgst[:, 0, :] = dg_rows
    dg_sem, dg_own = next(counter), next(counter)
    spread(1, n, dgst, dgr.at[tn], behind, dg_sem)
    spread(1, n, dgst, dgr.at[tn], behind, dg_sem, other)
    own_gate = remote(dgst.at[0], dgr.at[tn, 0], dg_own, partner)
    own_gate.start()
    dgr[tn, 0] = dgst[0]
    send_dx(chunks - 1)

    for c in range(chunks):
        rc = rows_of(c)
        tsend[1, rc] = dot_nn(a_s[rc], wout_s[:, pl.ds(ocol, HW)]).astype(BF)
        remote(tsend.at[1, rc], trecv.at[1, rc], e_half, partner).start()
    for c in range(chunks):
        rc = rows_of(c)
        own_s[rc] = dot_nn(a_s[rc], wout_s[:, pl.ds(col, HW)])
    finish(tsend.at[1], e_half)
    put(own_s[...] + trecv[1].astype(F32) + ebout_ref[:, pl.ds(col, HW)], es, est)
    e_sem = next(counter)
    spread(1, n, es, er, behind, e_sem)
    er[0] = es[0]
    if tail:
        spread(1, n, est, ert, behind, odd_e)
        ert[0] = est[0]

    finish(dgr.at[:, pl.ds(0, n - 1)], dg_sem)
    own_gate.wait()
    dg_all = dgr[0, :, 0, :] + dgr[1, :, 0, :]
    hb0, hb1 = hk0.astype(F32).astype(BF), hk1.astype(F32).astype(BF)
    dg0 = rowsum(jnp.where(slot0 == islot, pick_nn(hb0, dg_all), 0.0))
    dg1 = rowsum(jnp.where(slot1 == islot, pick_nn(hb1, dg_all), 0.0))
    mean_gate = gate0 * dg0 + gate1 * dg1
    dl0, dl1 = gate0 * (dg0 - mean_gate), gate1 * (dg1 - mean_gate)
    dlog = (jnp.where(h0, dl0, 0.0) + jnp.where(h1, dl1, 0.0)).astype(BF)

    finish(dxr.at[pl.ds(0, n - 1)], dx_sem)
    if tail:
        finish(dxrt.at[pl.ds(0, n - 1)], odd_dx)

    hsend[...] = picked(dxr, dxrt)
    h_sem = next(counter)
    hc = remote(hsend, hrecv.at[tn], h_sem, partner)
    hc.start()
    hrecv[tn] = hsend[...]
    by_router = dot_nn(dlog, wr)

    hc.wait()
    cot_copy.wait()

    dxn2 = jnp.concatenate([hrecv[0], hrecv[1]], -1) + by_router
    hat2 = hat2_s[...]
    gg2, gb2 = colsum(dxn2 * hat2), colsum(dxn2)
    u = dxn2 * ga2
    dx1 = jnp.concatenate([cotf[0], cotf[1]], -1).astype(F32) + rstd2 * (u - rowmean(u) - hat2 * rowmean(u * hat2))
    dx1_s[...] = dx1
    datt = dx1.astype(BF)
    do = dot_nn(datt, weight(3)).astype(BF)

    first_sems = [next(counter) for _ in range(5)]
    second_sems = [next(counter)] * 4 + [next(counter)]

    def to_plane(i, src, dst):
        for j in range(1, plane):
            remote(src.at[:, lax.rem(spot + j, plane)], dst.at[j - 1], first_sems[i], {"expert": in_plane(j)}).start()

    def to_line(i, src, got, mid, dst):
        finish(got, first_sems[i])
        total = src[:, spot].astype(F32)
        for j in range(plane - 1):
            total = total + got[j].astype(F32)
        mid[...] = total.astype(BF)
        for k in range(1, lines):
            there = in_line(k)
            remote(mid.at[there], dst.at[k], second_sems[i], {"expert": there * plane + spot}).start()
        dst[0] = mid[line]

    def line_first(i):
        return plane == lines and i in LINE_FIRST

    def gradient(i, value):
        gsend[i] = value.reshape(lines, plane, rows, HW).astype(BF)
        if line_first(i):
            for k in range(1, lines):
                there = in_line(k)
                remote(gsend.at[i, there], r1.at[i, k - 1], first_sems[i], {"expert": there * plane + spot}).start()
        else:
            to_plane(i, gsend.at[i], r1.at[i])

    def deliver(i):
        if line_first(i):
            finish(r1.at[i], first_sems[i])
            total = gsend[i, line].astype(F32)
            for k in range(lines - 1):
                total = total + r1[i, k].astype(F32)
            r2s[i] = total.astype(BF)
            for j in range(1, plane):
                target = lax.rem(spot + j, plane)
                remote(r2s.at[i, target], rs_ref.at[i, j], second_sems[i], {"expert": in_plane(j)}).start()
            rs_ref[i, 0] = r2s[i, spot]
        else:
            to_line(i, gsend.at[i], r1.at[i], r2s.at[i], rs_ref.at[i])

    gradient(0, dot_tn(datt, o_s[...]))

    dqs, dks, dvs = [], [], []
    for h in range(heads):
        sl = slice(h * HEAD_DIM, (h + 1) * HEAD_DIM)
        p = p_s[h]
        doh = do[:, sl]
        dp = dot_nt(doh, qkv_s[2, :, sl])
        dvs.append(dot_tn(p.astype(BF), doh))
        ds = (p * (dp - rowsum(p * dp))).astype(BF)
        dqs.append(dot_nn(ds, qkv_s[1, :, sl]) * scale)
        dks.append(dot_tn(ds, qkv_s[0, :, sl]) * scale)
    for i, v in enumerate((dqs, dks, dvs)):
        dqkv_s[i] = jnp.concatenate(v, -1).astype(BF)

    bfpart[0] = (
        dot_nt(dqkv_s[0], weight(0)) + dot_nt(dqkv_s[1], weight(1)) + dot_nt(dqkv_s[2], weight(2))
    ).astype(BF)
    b_sem = next(counter)
    bc = remote(bfpart.at[0], bfpart.at[1], b_sem, partner)
    bc.start()

    for i in range(3):
        gradient(i + 1, dot_tn(xn1_s[...], dqkv_s[i]))

    bc.wait()
    dxn1 = bfpart[0].astype(F32) + bfpart[1].astype(F32)
    hat1 = hat1_s[...]
    gg1, gb1 = colsum(dxn1 * hat1), colsum(dxn1)
    u = dxn1 * ga1
    gx_ref[...] = dx1_s[...] + rstd1 * (u - rowmean(u) - hat1 * rowmean(u * hat1))

    smsend[...] = jnp.zeros(smsend.shape, F32)
    smsend[0:n] = dot_tn(dlog, xn2_s[...])
    smsend[n : n + 1] = gg1
    smsend[n + 1 : n + 2] = gb1
    smsend[n + 2 : n + 3] = gg2
    smsend[n + 3 : n + 4] = gb2
    ssend[...] = smsend[...].T.reshape(lines, plane, rows, ssend.shape[3]).astype(BF)
    to_plane(4, ssend, sr1)
    deliver(0)

    finish(grow.at[pl.ds(0, n - 1)], gate_sem)
    gate_col = rowsum(one_s[...] * pick_nn(sel_s[...], grow[:, 0, :]))
    gated = gate_col * c2[...].astype(F32)
    c2[...] = gated.astype(BF)
    gbout_ref[...] = colsum(gated)
    x2[...] = (gate_col * x2[...].astype(F32)).astype(BF)
    lane = iota((M, LANES), 1)
    gate_parts = halves(gate_col)
    gate_lanes = sum(jnp.where(lane == i, part.astype(F32), 0.0) for i, part in enumerate(gate_parts)).astype(BF)

    def grads(i, _):
        f = pl.ds(pl.multiple_of(i * FT, FT), FT)
        gwout_ref[f, :] = dot_tn(a_s[:, f], c2[...])
        gwin_ref[:, f] = dot_tn(x2[...], dh_s[:, f])
        gbin_ref[:, f] = colsum(dot_tn(gate_lanes, dh_s[:, f]))
        return 0

    lax.fori_loop(0, F // FT, grads, 0)
    outs = [(gwin_ref, gwin_out), (gwout_ref, gwout_out), (gbin_ref, gbin_out), (gbout_ref, gbout_out), (gx_ref, gx_out)]
    outs = [pltpu.make_async_copy(src, dst, hbm_sem.at[i]) for i, (src, dst) in enumerate(outs)]
    for move in outs:
        move.start()

    finish(er.at[pl.ds(0, n - 1)], e_sem)
    if tail:
        finish(ert.at[pl.ds(0, n - 1)], odd_e)

    y = x1_s[:, pl.ds(col, HW)] + picked(er, ert)
    y_ref[...] = y.astype(BF)
    outs.append(pltpu.make_async_copy(y_ref, y_out, hbm_sem.at[5]))
    outs[-1].start()

    for i in ORDER:
        deliver(i)
    to_line(4, ssend, sr1, s2s, rsmall_ref)

    for move in outs:
        move.wait()

    finish(rs_ref.at[:, pl.ds(1, lines - 1)], second_sems[0])
    finish(rsmall_ref.at[pl.ds(1, lines - 1)], second_sems[4])


def last_kernel(
    y_in, gx_in, rs, rsmall, gwin_in, gbin_in, gwout_in, gbout_in,
    y, gx, gq, gk, gv, go, gr, a1, b1, a2, b2, gwin, gbin, gwout, gbout,
    sums, turned, lines_s, sem,
):
    n, rows = gr.shape
    moves = [(gwin_in, gwin), (gwout_in, gwout), (gx_in, gx), (y_in, y), (gbin_in, gbin), (gbout_in, gbout)]
    moves += [(sums.at[i], ref) for i, ref in enumerate((go, gq, gk, gv))]
    moves += [(turned, gr)] + [(lines_s.at[i], ref) for i, ref in enumerate((a1, b1, a2, b2))]
    copies = [pltpu.make_async_copy(src, dst, sem.at[i]) for i, (src, dst) in enumerate(moves)]
    for c in copies[:6]:
        c.start()
    small = jnp.sum(rsmall[...].astype(F32), 0).T
    turned[...] = small[0:n, 0:rows]
    for i in range(4):
        lines_s[i] = small[n + i : n + i + 1, 0:rows]
        sums[i] = jnp.sum(rs[i].astype(F32), 0)
    for c in copies[6:]:
        c.start()
    for c in copies:
        c.wait()


def shards(
    block_input, routes, w_query, w_key, w_value, w_output, w_router, norm1_gain, norm1_bias, norm2_gain, norm2_bias,
    expert_in, expert_in_bias, expert_out, expert_out_bias, cotangent,
):
    z = Sizes()
    z.n = lax.axis_size("expert")
    z.T, z.D = block_input.shape
    z.HW = cotangent.shape[1]
    z.F = expert_in.shape[2]
    z.rows = w_query.shape[0]
    z.heads = z.HW // HEAD_DIM
    experts, topk = w_router.shape[1], routes.shape[1]
    cap = max(2, 2 * topk * z.T // experts)
    z.tail = 1 if cap > 8 and cap % 8 == 1 else 0
    z.R = cap - 1 if z.tail else -(-cap // 8) * 8
    z.M = z.n * (z.R + z.tail)
    z.lines = 4
    z.plane = z.n // z.lines
    z.chunks = CHUNKS
    z.sems = 49
    n, T, D, HW, R, F, rows, M = z.n, z.T, z.D, z.HW, z.R, z.F, z.rows, z.M
    lines, plane = z.lines, z.plane
    wide = -(-(n + 4) // LANES) * LANES
    vm = pl.BlockSpec(memory_space=pltpu.VMEM)
    hbm = pl.BlockSpec(memory_space=pl.ANY)
    out_shape = (
        jax.ShapeDtypeStruct((T, HW), BF),
        jax.ShapeDtypeStruct((T, D), F32),
        jax.ShapeDtypeStruct((4, lines, rows, HW), BF),
        jax.ShapeDtypeStruct((lines, rows, wide), BF),
        jax.ShapeDtypeStruct((D, F), F32),
        jax.ShapeDtypeStruct((1, F), F32),
        jax.ShapeDtypeStruct((F, D), F32),
        jax.ShapeDtypeStruct((1, D), F32),
    )
    V = pltpu.VMEM
    args = (
        block_input, routes.T, w_query, w_key, w_value, w_output.T, w_router.T,
        norm1_gain[None], norm1_bias[None], norm2_gain[None], norm2_bias[None],
        expert_in_bias, expert_out_bias, cotangent, expert_in, expert_out,
    )
    tp = -(-T // LANES) * LANES
    scratch = [
        *(V(out_shape[i].shape, out_shape[i].dtype) for i in (0, 1, 4, 5, 6, 7)),
        V((D, F), F32), V((F, D), F32), V((D, F), BF), V((F, D), BF), V((wide, LANES), F32), V((8, tp), F32), V((tp, LANES), F32),
        V((n, 2 * rows + rows * wide // HW, HW), BF), V((n, 2 * rows, HW), BF),
        V((M, T), BF), V((2, T, M), BF), V((M, n), BF), V((n, M), BF), V((M, LANES), F32), V((M, LANES), F32), V((M, HW), F32), V((T, D), F32), V((T, D), BF), V((3, T, HW), BF), V((z.heads, T, T), F32),
        V((T, HW), BF), V((T, D), BF), V((T, D), BF),
        V((T, D), F32), V((T, D), F32), V((T, D), BF), V((2, T, HW), BF),
        V((n, R, HW), BF), V((2, n, R, HW), BF), V((n, R, HW), BF), V((2, n, R, HW), BF),
        V((n, 1, HW), BF), V((2, n, 1, HW), BF), V((n, 1, HW), BF), V((2, n, 1, HW), BF),
        *[V((n, 1, HW), BF)] * 4,
        V((n, 1, LANES), F32), V((n, 1, LANES), F32), V((M, D), BF), V((M, D), BF), V((M, F), BF), V((M, F), BF),
        V((2, M, HW), BF), V((2, M, HW), BF), V((n, R, HW), BF), V((n, R, HW), BF), V((n, R, HW), BF), V((n, R, HW), BF),
        V((n, 1, LANES), F32), V((2, n, 1, LANES), F32), V((T, HW), F32), V((2, T, HW), F32), V((T, D), F32), V((3, T, HW), BF),
        V((4, lines, plane, rows, HW), BF), V((4, plane - 1, lines, rows, HW), BF), V((4, lines, rows, HW), BF), V((wide, D), F32),
        V((lines, plane, rows, wide), BF), V((plane - 1, lines, rows, wide), BF), V((lines, rows, wide), BF), V((2, T, D), BF),
        *(V(v.shape, v.dtype) for v in args[:14]),
        pltpu.SemaphoreType.DMA((16,)), pltpu.SemaphoreType.DMA((z.sems,)), pltpu.SemaphoreType.DMA((z.sems,)),
    ]
    kept = [pltpu.VMEM(v.shape, v.dtype) for v in out_shape]
    done = pl.pallas_call(
        functools.partial(block_kernel, z),
        out_shape=kept,
        in_specs=[pl.BlockSpec(memory_space=pltpu.HBM)] * 16,
        out_specs=[hbm] * 2 + [vm] * 2 + [hbm] * 4,
        scratch_shapes=scratch,
        compiler_params=pltpu.CompilerParams(collective_id=0, has_side_effects=True, vmem_limit_bytes=52 << 20),
        name="block",
    )(
        *(pltpu.with_memory_space_constraint(v, pltpu.HBM) for v in args)
    )
    square = jax.ShapeDtypeStruct((rows, HW), F32)
    line = jax.ShapeDtypeStruct((1, rows), F32)
    last_shape = (
        out_shape[0], out_shape[1], square, square, square, square, jax.ShapeDtypeStruct((n, rows), F32), line, line, line, line,
        out_shape[4], out_shape[5], out_shape[6], out_shape[7],
    )
    y, gx, gq, gk, gv, go, gr, a1, b1, a2, b2, gwin, gbin, gwout, gbout = pl.pallas_call(
        last_kernel,
        out_shape=last_shape,
        in_specs=[hbm] * 2 + [vm] * 2 + [hbm] * 4,
        out_specs=[hbm] * 15,
        scratch_shapes=[
            V((4, rows, HW), F32), V((n, rows), F32), V((4, 1, rows), F32), pltpu.SemaphoreType.DMA((15,)),
        ],
        compiler_params=pltpu.CompilerParams(vmem_limit_bytes=8 << 20),
        name="last",
    )(*done)
    return (y, gx, gq, gk, gv, go.T, gr.T, a1[0], b1[0], a2[0], b2[0], gwin[None], gbin, gwout[None], gbout)


def solution(mesh):
    row, col = P("expert", None), P("expert", "tensor")
    vec = P("expert")
    in_specs = (
        row, row, col, col, col, P("tensor", "expert"), row, vec, vec, vec, vec,
        P("expert", None, "tensor"), col, P("expert", "tensor", None), row, col,
    )
    out_specs = (
        col, row, col, col, col, P("tensor", "expert"), row, vec, vec, vec, vec,
        P("expert", None, "tensor"), col, P("expert", "tensor", None), row,
    )
    return jax.shard_map(shards, mesh=mesh, in_specs=in_specs, out_specs=out_specs, check_vma=False)
```

```python
import functools
import math

import jax
import jax.numpy as jnp
from jax import lax
from jax.experimental import pallas as pl
from jax.experimental.pallas import tpu as pltpu
from jax.sharding import PartitionSpec as P

HEAD_DIM = 64
EPS = 1e-06
MESH = pl.DeviceIdType.MESH
BF = jnp.bfloat16
F32 = jnp.float32
LANES = 128
CHUNKS = 4
LINE_FIRST = (1,)
ORDER = (1, 2, 3)
EARLY = 3


def dot_nn(a, b):
    return lax.dot_general(a, b, (((1,), (0,)), ((), ())), preferred_element_type=F32)


def dot_nt(a, b):
    return lax.dot_general(a, b, (((1,), (1,)), ((), ())), preferred_element_type=F32)


def dot_tn(a, b):
    return lax.dot_general(a, b, (((0,), (0,)), ((), ())), preferred_element_type=F32)


def halves(v):
    first = v.astype(BF)
    rest = v - first.astype(F32)
    second = rest.astype(BF)
    return first, second, (rest - second.astype(F32)).astype(BF)


def pick_nn(select, v):
    a, b, c = halves(v)
    return dot_nn(select, a) + dot_nn(select, b) + dot_nn(select, c)


def colsum(v):
    return jnp.sum(v, axis=0, keepdims=True)


def rowmean(v):
    return jnp.mean(v, -1, keepdims=True)


def rowsum(v):
    return jnp.sum(v, -1, keepdims=True)


def iota(shape, axis):
    return lax.broadcasted_iota(jnp.int32, shape, axis)


class Sizes:
    pass


def block_kernel(
    z,
    x_hbm, routes_hbm, wq_hbm, wk_hbm, wv_hbm, wo_hbm, wr_hbm, ga1_hbm, be1_hbm, ga2_hbm, be2_hbm, ebin_hbm, ebout_hbm, cot_hbm,
    win_hbm, wout_hbm,
    y_out, gx_out, rs_ref, rsmall_ref, gwin_out, gbin_out, gwout_out, gbout_out,
    y_ref, gx_ref, gwin_ref, gbin_ref, gwout_ref, gbout_ref,
    win32, wout32, win_s, wout_s, square, flat, pads,
    wa, wb, pt_s, pick_s, sel_s, selt_s, one_s, dgp_s, own_s, own_e, hat1_s, xn1_s, qkv_s, p_s, o_s, parts, partr,
    x1_s, hat2_s, xn2_s, cotf, gs, gr, xs, xr, gst, grt, xst, xrt, est, ert, dxst, dxrt, growst, grow, x2, c2, a_s, dh_s,
    tsend, trecv, es, er, dxs, dxr, dgst, dgr, hsend, hrecv, dx1_s, dqkv_s, gsend, r1, r2s, smsend, ssend, sr1, s2s, bfpart,
    x_ref, routes_ref, wq_ref, wk_ref, wv_ref, wo_ref, wr_ref, ga1_ref, be1_ref, ga2_ref, be2_ref, ebin_ref, ebout_ref, cot_ref,
    hbm_sem, send_sem, recv_sem,
):
    tail = z.tail
    n, T, D, HW, R, F, rows, M, heads = z.n, z.T, z.D, z.HW, z.R, z.F, z.rows, z.M, z.heads
    lines, plane, chunks = z.lines, z.plane, z.chunks
    KC = n // chunks
    me = lax.axis_index("expert")
    tn = lax.axis_index("tensor")
    other = 1 - tn
    partner = {"tensor": other}
    line, spot = me // plane, lax.rem(me, plane)
    col = pl.multiple_of(tn * HW, HW)
    ocol = pl.multiple_of(other * HW, HW)
    counter = iter(range(z.sems))

    low_bit, high_bit = lax.rem(line, 2), line // 2

    def other_line(c):
        a, b = lax.rem(c, 2), c // 2
        return (high_bit + b - 2 * high_bit * b) * 2 + low_bit + a - 2 * low_bit * a

    def ahead(k):
        return other_line(lax.rem(k, lines)) * plane + lax.rem(spot + k // lines, plane)

    def behind(k):
        return other_line(lax.rem(k, lines)) * plane + lax.rem(spot - k // lines + plane, plane)

    def in_line(k):
        return lax.rem(line + k, lines)

    def in_plane(j):
        return line * plane + lax.rem(spot + j, plane)

    barrier = pltpu.get_barrier_semaphore()

    def greet(k, _):
        pl.semaphore_signal(barrier, inc=1, device_id={"expert": ahead(k)}, device_id_type=MESH)
        return 0

    lax.fori_loop(1, n, greet, 0)
    pl.semaphore_signal(barrier, inc=1, device_id=partner, device_id_type=MESH)

    moves = (
        (wq_hbm, wq_ref), (wk_hbm, wk_ref), (wv_hbm, wv_ref), (wo_hbm, wo_ref), (wr_hbm, wr_ref),
        (ga1_hbm, ga1_ref), (be1_hbm, be1_ref), (ga2_hbm, ga2_ref), (be2_hbm, be2_ref),
        (routes_hbm, routes_ref), (cot_hbm, cot_ref), (x_hbm, x_ref), (ebin_hbm, ebin_ref), (ebout_hbm, ebout_ref),
        (win_hbm.at[0], win32), (wout_hbm.at[0], wout32),
    )
    moves = [pltpu.make_async_copy(src, dst, hbm_sem.at[i]) for i, (src, dst) in enumerate(moves)]
    for move in moves:
        move.start()
    win_copy, wout_copy = moves[14:]

    def remote(src, dst, i, dev):
        return pltpu.make_async_remote_copy(
            src_ref=src, dst_ref=dst, send_sem=send_sem.at[i], recv_sem=recv_sem.at[i], device_id=dev, device_id_type=MESH
        )

    def spread(low, high, src, dst, to, i, core=None):
        def step(at, _):
            k = high - 1 - at
            dev = {"expert": to(k)}
            if core is not None:
                dev["tensor"] = core
            remote(src.at[k], dst.at[k], i, dev).start()
            return 0

        lax.fori_loop(0, high - low, step, 0)

    def finish(ref, i):
        d = remote(ref, ref, i, partner)
        d.wait_send()
        d.wait_recv()

    def put(value, body, odd):
        body[...] = value[0 : n * R].reshape(n, R, HW).astype(BF)
        if tail:
            odd[:, 0, :] = value[n * R :].astype(BF)

    def picked(body, odd):
        total = 0.0
        for pick, gate in ((pick_s.at[0], gate0), (pick_s.at[1], gate1)):
            value = dot_nn(pick[:, 0 : n * R], body[...].reshape(n * R, HW))
            if tail:
                value = value + dot_nn(pick[:, n * R :], odd[:, 0, :])
            total = total + gate * value
        return total

    for move in moves[:9]:
        move.wait()
    wide, sr = square.shape[0], wa.shape[1] - 2 * rows
    wa[me, 0:rows] = wq_ref[...].astype(BF)
    wa[me, rows : 2 * rows] = wk_ref[...].astype(BF)
    wb[me, 0:rows] = wv_ref[...].astype(BF)
    wb[me, rows : 2 * rows] = wo_ref[...].astype(BF)
    square[...] = jnp.zeros(square.shape, F32)
    square[0:n, 0:rows] = wr_ref[...]
    for i, ref in enumerate((ga1_ref, be1_ref, ga2_ref, be2_ref)):
        square[n + i : n + i + 1, 0:rows] = ref[...]
    turned = square[...].T
    for i in range(HW // wide):
        wa[me, 2 * rows :, i * wide : (i + 1) * wide] = turned[i * sr : (i + 1) * sr].astype(BF)

    pl.semaphore_wait(barrier, n)

    line_a = [None] + [next(counter) for _ in range(lines - 1)]
    line_b = [None] + [next(counter) for _ in range(lines - 1)]
    square_plane = plane == 4
    if square_plane:
        near_a = [next(counter) for _ in range(lines)]
        near_b = [next(counter) for _ in range(lines)]
        far_a, far_b = next(counter), next(counter)
        side, over = spot + 1 - 2 * lax.rem(spot, 2), lax.rem(spot + 2, 4)
        to_side, to_over = {"expert": line * plane + side}, {"expert": line * plane + over}
    else:
        plane_a, plane_b = next(counter), next(counter)

    def share(s):
        block = other_line(s) * plane + spot
        if square_plane:
            remote(wa.at[block], wa.at[block], near_a[s], to_side).start()
            remote(wb.at[block], wb.at[block], near_b[s], to_over).start()
            remote(wa.at[block], wa.at[block], far_a, to_over).start()
            remote(wb.at[block], wb.at[block], far_b, to_side).start()
        else:
            for j in range(1, plane):
                remote(wa.at[block], wa.at[block], plane_a, {"expert": in_plane(j)}).start()
                remote(wb.at[block], wb.at[block], plane_b, {"expert": in_plane(j)}).start()

    def hand_on(s):
        if square_plane:
            finish(wa.at[0], near_a[s])
            block = other_line(s) * plane + side
            remote(wa.at[block], wa.at[block], far_a, to_over).start()
            finish(wb.at[0], near_b[s])
            block = other_line(s) * plane + over
            remote(wb.at[block], wb.at[block], far_b, to_side).start()

    for k in range(1, lines):
        dev = {"expert": other_line(k) * plane + spot}
        remote(wa.at[me], wa.at[me], line_a[k], dev).start()
        remote(wb.at[me], wb.at[me], line_b[k], dev).start()
    share(0)

    moves[9].wait()
    flat[0:2, 0:T] = routes_ref[...].astype(F32)
    r = flat[...].T
    r0, r1_ = r[0:T, 0:1], r[0:T, 1:2]
    ie = iota((T, n), 1).astype(F32)
    h0, h1 = r0 == ie, r1_ == ie
    above = [(ie >= i * plane).astype(F32) for i in range(1, lines)]
    line_of = sum(above)
    high_of = above[1]
    low_of = line_of - 2 * high_of
    low_f, high_f = low_bit.astype(F32), high_bit.astype(F32)
    turn = ie - line_of * plane - spot.astype(F32)
    turn = jnp.where(turn < 0, turn + plane, turn)
    place = (high_of - high_f) ** 2 * 2 + (low_of - low_f) ** 2 + turn * lines
    k0, k1 = rowsum(jnp.where(h0, place, 0.0)), rowsum(jnp.where(h1, place, 0.0))
    hk0, hk1 = k0 == ie, k1 == ie
    hit = jnp.logical_or(hk0, hk1).astype(F32).astype(BF)
    tri = (iota((T, T), 0) > iota((T, T), 1)).astype(F32).astype(BF)
    count = dot_nn(tri, hit)
    slot0 = rowsum(jnp.where(hk0, count, 0.0))
    slot1 = rowsum(jnp.where(hk1, count, 0.0))
    pos0 = jnp.where(slot0 < R, k0 * R + slot0, k0 + n * R)
    pos1 = jnp.where(slot1 < R, k1 * R + slot1, k1 + n * R)
    pads[...] = jnp.full(pads.shape, -1.0, F32)
    pads[0:T, 0:1] = pos0
    pads[0:T, 1:2] = pos1
    post = pads[...].T
    slots = iota((M, T), 0).astype(F32)
    pt_s[...] = jnp.logical_or(slots == post[0:1, 0:T], slots == post[1:2, 0:T]).astype(F32).astype(BF)

    moves[10].wait()
    put(dot_nn(pt_s[...], cot_ref[...]), gs, gst)
    cotf[tn] = cot_ref[...]
    cot_sem = next(counter)
    cot_copy = remote(cot_ref, cotf.at[tn], cot_sem, partner)
    cot_copy.start()

    for move in moves[11:14]:
        move.wait()
    x = x_ref[...].astype(F32)
    center = x - rowmean(x)
    rstd1 = lax.rsqrt(rowmean(center * center) + EPS)
    hat1_s[...] = center * rstd1

    slot_lane = iota((T, M), 1).astype(F32)
    pick_s[0] = (slot_lane == pos0).astype(F32).astype(BF)
    pick_s[1] = (slot_lane == pos1).astype(F32).astype(BF)
    gr[tn, 0] = gs[0]
    if tail:
        grt[tn, 0] = gst[0]
    win_copy.wait()
    win_s[...] = win32[...].astype(BF)
    wout_copy.wait()
    wout_s[...] = wout32[...].astype(BF)

    for k in range(1, lines):
        finish(wa.at[0], line_a[k])
        finish(wb.at[0], line_b[k])
        share(k)
        hand_on(k - 1)

    row_sems = [next(counter) for _ in range(chunks)]
    odd_rows, odd_half, odd_dx, odd_e = (next(counter) for _ in range(4))

    def send_cotangent(c):
        spread(max(1, c * KC), (c + 1) * KC, gs, gr.at[tn], ahead, row_sems[c])
        if tail and c + 1 == chunks:
            spread(1, n, gst, grt.at[tn], ahead, odd_rows)

    send_cotangent(0)

    hand_on(lines - 1)

    if square_plane:
        finish(wa.at[pl.ds(0, 2 * lines)], far_a)
    else:
        finish(wa.at[pl.ds(0, (plane - 1) * lines)], plane_a)
    small = jnp.concatenate([wa[:, 2 * rows :, i * wide : (i + 1) * wide] for i in range(HW // wide)], 1)
    small = small.astype(F32).reshape(n * rows, wide).T
    ga1, be1 = small[n : n + 1], small[n + 1 : n + 2]
    ga2, be2 = small[n + 2 : n + 3], small[n + 3 : n + 4]
    wr = small[0:n].astype(BF)
    xn1 = (hat1_s[...] * ga1 + be1).astype(BF)
    xn1_s[...] = xn1

    def weight(i):
        ref = wb if i >= 2 else wa
        return ref[:, i % 2 * rows : (i % 2 + 1) * rows].reshape(D, HW)

    for i in range(2):
        qkv_s[i] = dot_nn(xn1, weight(i)).astype(BF)

    if square_plane:
        finish(wb.at[pl.ds(0, 2 * lines)], far_b)
    else:
        finish(wb.at[pl.ds(0, (plane - 1) * lines)], plane_b)
    scale = 1.0 / math.sqrt(HEAD_DIM)

    for c in range(1, EARLY):
        send_cotangent(c)

    qkv_s[2] = dot_nn(xn1, weight(2)).astype(BF)

    outs = []
    for h in range(heads):
        sl = slice(h * HEAD_DIM, (h + 1) * HEAD_DIM)
        s = dot_nt(qkv_s[0, :, sl], qkv_s[1, :, sl]) * scale
        ex = jnp.exp(s - jnp.max(s, -1, keepdims=True))
        p = ex / rowsum(ex)
        p_s[h] = p
        outs.append(dot_nn(p.astype(BF), qkv_s[2, :, sl]))
    o_s[...] = jnp.concatenate(outs, -1).astype(BF)

    parts[...] = dot_nt(o_s[...], weight(3)).astype(BF)
    part_sem = next(counter)
    part_copy = remote(parts, partr, part_sem, partner)
    part_copy.start()

    part_copy.wait()
    x1 = x_ref[...].astype(F32) + (parts[...].astype(F32) + partr[...].astype(F32))
    x1_s[...] = x1

    center = x1 - rowmean(x1)
    rstd2 = lax.rsqrt(rowmean(center * center) + EPS)
    hat2 = center * rstd2
    hat2_s[...] = hat2
    xn2 = (hat2 * ga2 + be2).astype(BF)
    xn2_s[...] = xn2
    put(dot_nn(pt_s[...], xn2_s[:, pl.ds(col, HW)]), xs, xst)


    def send_rows(c):
        spread(max(1, c * KC), (c + 1) * KC, xs, xr.at[tn], ahead, row_sems[c])
        if tail and c + 1 == chunks:
            spread(1, n, xst, xrt.at[tn], ahead, odd_rows)

    send_rows(0)
    xr[tn, 0] = xs[0]
    if tail:
        xrt[tn, 0] = xst[0]

    logits = dot_nt(xn2, wr)
    l0 = rowsum(jnp.where(h0, logits, 0.0))
    l1 = rowsum(jnp.where(h1, logits, 0.0))
    top = jnp.maximum(l0, l1)
    e0, e1 = jnp.exp(l0 - top), jnp.exp(l1 - top)
    gate0, gate1 = e0 / (e0 + e1), e1 / (e0 + e1)
    islot = iota((T, LANES), 1).astype(F32)
    at0 = (slot0 == islot).astype(F32).astype(BF)
    at1 = (slot1 == islot).astype(F32).astype(BF)
    gate_rows = jnp.zeros((n, LANES), F32)
    for hh, gg, at in ((hk0, gate0, at0), (hk1, gate1, at1)):
        for part in halves(jnp.where(hh, gg, 0.0)):
            gate_rows = gate_rows + dot_tn(part, at)
    growst[:, 0, :] = gate_rows
    gate_sem = next(counter)
    spread(1, n, growst, grow, ahead, gate_sem)
    grow[0] = growst[0]
    for c in range(1, chunks):
        if c >= EARLY:
            send_cotangent(c)
        send_rows(c)

    FT = 256
    c0 = math.sqrt(2.0 / math.pi)
    MC = KC * R
    half_sems = [next(counter) for _ in range(chunks)]
    dx_half = [next(counter) for _ in range(chunks)]
    e_half = next(counter)
    dx_sem = next(counter)

    def rows_of(c):
        return slice(c * MC, (c + 1) * MC if c + 1 < chunks else M)

    def send_dx(c):
        rc = rows_of(c)
        finish(tsend.at[0, rc], dx_half[c])
        own = own_s[rc]
        own = own + trecv[0, rc].astype(F32)
        dxs[c * KC : (c + 1) * KC] = own[0:MC].reshape(KC, R, HW).astype(BF)
        spread(max(1, c * KC), (c + 1) * KC, dxs, dxr, behind, dx_sem)
        if c == 0:
            dxr[0] = dxs[0]
        if tail and c + 1 == chunks:
            dxst[:, 0, :] = own[MC:].astype(BF)
            spread(1, n, dxst, dxrt, behind, odd_dx)
            dxrt[0] = dxst[0]

    def arrive(c):
        low = max(1, c * KC)
        kc = pl.ds(c * KC, KC)
        finish(gr.at[:, pl.ds(low, (c + 1) * KC - low)], row_sems[c])
        for buf in (gr, xr):
            remote(buf.at[tn, kc], buf.at[tn, kc], half_sems[c], partner).start()
        if tail and c + 1 == chunks:
            finish(grt.at[:, pl.ds(0, n - 1)], odd_rows)
            for buf in (grt, xrt):
                remote(buf.at[tn], buf.at[tn], odd_half, partner).start()

    def arrived(c):
        finish(gr.at[:, pl.ds(c * KC, KC)], half_sems[c])
        if tail and c + 1 == chunks:
            finish(grt, odd_half)

    row, block = iota((M, n), 0), iota((M, n), 1)
    inner = row - block * R
    is_odd = row - n * R == block
    in_body = jnp.logical_and(jnp.logical_and(inner >= 0, inner < R), row < n * R)
    sel_s[...] = jnp.logical_or(in_body, is_odd).astype(F32).astype(BF)
    at_slot = rowsum(jnp.where(in_body, inner, 0).astype(F32)) + jnp.where(row[:, 0:1] < n * R, 0.0, float(R))
    one_s[...] = (at_slot == iota((M, LANES), 1).astype(F32)).astype(F32)
    row, block = iota((n, M), 1), iota((n, M), 0)
    inner = row - block * R
    in_body = jnp.logical_and(jnp.logical_and(inner >= 0, inner < R), row < n * R)
    selt_s[...] = jnp.logical_or(in_body, row - n * R == block).astype(F32).astype(BF)

    def output_half(c):
        rc = rows_of(c)
        tsend[1, rc] = dot_nn(a_s[rc], wout_s[:, pl.ds(ocol, HW)]).astype(BF)
        remote(tsend.at[1, rc], trecv.at[1, rc], e_half, partner).start()

    def output_own(c):
        rc = rows_of(c)
        own_e[rc] = dot_nn(a_s[rc], wout_s[:, pl.ds(col, HW)])

    arrive(0)
    for c in range(chunks):
        rc = rows_of(c)
        arrived(c)
        for hf in range(2):
            wide = slice(hf * HW, (hf + 1) * HW)
            body = slice(c * MC, (c + 1) * MC)
            x2[body, wide] = xr[hf, c * KC : (c + 1) * KC].reshape(MC, HW)
            c2[body, wide] = gr[hf, c * KC : (c + 1) * KC].reshape(MC, HW)
            if tail and c + 1 == chunks:
                x2[n * R :, wide] = xrt[hf, :, 0, :]
                c2[n * R :, wide] = grt[hf, :, 0, :]

        def first(i, _):
            f = pl.ds(pl.multiple_of(i * FT, FT), FT)
            h = dot_nn(x2[rc], win_s[:, f]) + ebin_ref[:, f]
            hh = h * h
            half = 0.5 + 0.5 * jnp.tanh(h * (c0 + (0.044715 * c0) * hh))
            act = (h * half).astype(BF)
            a_s[rc, f] = act
            slope = half + (half - half * half) * (h * (2 * c0 + (6 * 0.044715 * c0) * hh))
            da = dot_nt(c2[rc], wout_s[f, :])
            dh_s[rc, f] = (slope * da).astype(BF)
            both = act.astype(F32) * da
            for j in range(FT // LANES):
                dgp_s[rc] = dgp_s[rc] + both[:, j * LANES : (j + 1) * LANES]
            return 0

        own_g = c2[rc, pl.ds(col, HW)].astype(F32) * ebout_ref[:, pl.ds(col, HW)]
        dgp_s[rc] = sum(own_g[:, j * LANES : (j + 1) * LANES] for j in range(HW // LANES))
        lax.fori_loop(0, F // FT // 2, first, 0)
        if c > 0:
            send_dx(c - 1)
        if c + 1 < chunks:
            arrive(c + 1)
        lax.fori_loop(F // FT // 2, F // FT, first, 0)
        tsend[0, rc] = dot_nt(dh_s[rc], win_s[pl.ds(ocol, HW), :]).astype(BF)
        remote(tsend.at[0, rc], trecv.at[0, rc], dx_half[c], partner).start()
        own_s[rc] = dot_nt(dh_s[rc], win_s[pl.ds(col, HW), :])
        if c + 1 < chunks:
            output_half(c)
    dgate = rowsum(dgp_s[...])
    dg_rows = jnp.zeros((n, LANES), F32)
    for part in halves(one_s[...] * dgate):
        dg_rows = dg_rows + dot_nn(selt_s[...], part)
    dgst[:, 0, :] = dg_rows
    dg_sem, dg_own = next(counter), next(counter)
    spread(1, n, dgst, dgr.at[tn], behind, dg_sem)
    spread(1, n, dgst, dgr.at[tn], behind, dg_sem, other)
    own_gate = remote(dgst.at[0], dgr.at[tn, 0], dg_own, partner)
    own_gate.start()
    dgr[tn, 0] = dgst[0]
    send_dx(chunks - 1)

    output_half(chunks - 1)
    for c in range(chunks):
        output_own(c)
    finish(tsend.at[1], e_half)
    put(own_e[...] + trecv[1].astype(F32) + ebout_ref[:, pl.ds(col, HW)], es, est)
    e_sem = next(counter)
    spread(1, n, es, er, behind, e_sem)
    er[0] = es[0]
    if tail:
        spread(1, n, est, ert, behind, odd_e)
        ert[0] = est[0]

    finish(dgr.at[:, pl.ds(0, n - 1)], dg_sem)
    own_gate.wait()
    dg_all = dgr[0, :, 0, :] + dgr[1, :, 0, :]
    hb0, hb1 = hk0.astype(F32).astype(BF), hk1.astype(F32).astype(BF)
    dg0 = rowsum(jnp.where(slot0 == islot, pick_nn(hb0, dg_all), 0.0))
    dg1 = rowsum(jnp.where(slot1 == islot, pick_nn(hb1, dg_all), 0.0))
    mean_gate = gate0 * dg0 + gate1 * dg1
    dl0, dl1 = gate0 * (dg0 - mean_gate), gate1 * (dg1 - mean_gate)
    dlog = (jnp.where(h0, dl0, 0.0) + jnp.where(h1, dl1, 0.0)).astype(BF)

    finish(dxr.at[pl.ds(0, n - 1)], dx_sem)
    if tail:
        finish(dxrt.at[pl.ds(0, n - 1)], odd_dx)

    hsend[...] = picked(dxr, dxrt)
    h_sem = next(counter)
    hc = remote(hsend, hrecv.at[tn], h_sem, partner)
    hc.start()
    hrecv[tn] = hsend[...]
    by_router = dot_nn(dlog, wr)

    hc.wait()
    cot_copy.wait()

    dxn2 = jnp.concatenate([hrecv[0], hrecv[1]], -1) + by_router
    hat2 = hat2_s[...]
    gg2, gb2 = colsum(dxn2 * hat2), colsum(dxn2)
    u = dxn2 * ga2
    dx1 = jnp.concatenate([cotf[0], cotf[1]], -1).astype(F32) + rstd2 * (u - rowmean(u) - hat2 * rowmean(u * hat2))
    dx1_s[...] = dx1
    datt = dx1.astype(BF)
    do = dot_nn(datt, weight(3)).astype(BF)

    first_sems = [next(counter) for _ in range(5)]
    second_sems = [next(counter)] * 4 + [next(counter)]

    def to_plane(i, src, dst):
        for j in range(1, plane):
            remote(src.at[:, lax.rem(spot + j, plane)], dst.at[j - 1], first_sems[i], {"expert": in_plane(j)}).start()

    def to_line(i, src, got, mid, dst):
        finish(got, first_sems[i])
        total = src[:, spot].astype(F32)
        for j in range(plane - 1):
            total = total + got[j].astype(F32)
        mid[...] = total.astype(BF)
        for k in range(1, lines):
            there = in_line(k)
            remote(mid.at[there], dst.at[k], second_sems[i], {"expert": there * plane + spot}).start()
        dst[0] = mid[line]

    def line_first(i):
        return plane == lines and i in LINE_FIRST

    def gradient(i, value):
        gsend[i] = value.reshape(lines, plane, rows, HW).astype(BF)
        if line_first(i):
            for k in range(1, lines):
                there = in_line(k)
                remote(gsend.at[i, there], r1.at[i, k - 1], first_sems[i], {"expert": there * plane + spot}).start()
        else:
            to_plane(i, gsend.at[i], r1.at[i])

    def deliver(i):
        if line_first(i):
            finish(r1.at[i], first_sems[i])
            total = gsend[i, line].astype(F32)
            for k in range(lines - 1):
                total = total + r1[i, k].astype(F32)
            r2s[i] = total.astype(BF)
            for j in range(1, plane):
                target = lax.rem(spot + j, plane)
                remote(r2s.at[i, target], rs_ref.at[i, j], second_sems[i], {"expert": in_plane(j)}).start()
            rs_ref[i, 0] = r2s[i, spot]
        else:
            to_line(i, gsend.at[i], r1.at[i], r2s.at[i], rs_ref.at[i])

    gradient(0, dot_tn(datt, o_s[...]))

    dqs, dks, dvs = [], [], []
    for h in range(heads):
        sl = slice(h * HEAD_DIM, (h + 1) * HEAD_DIM)
        p = p_s[h]
        doh = do[:, sl]
        dp = dot_nt(doh, qkv_s[2, :, sl])
        dvs.append(dot_tn(p.astype(BF), doh))
        ds = (p * (dp - rowsum(p * dp))).astype(BF)
        dqs.append(dot_nn(ds, qkv_s[1, :, sl]) * scale)
        dks.append(dot_tn(ds, qkv_s[0, :, sl]) * scale)
    for i, v in enumerate((dqs, dks, dvs)):
        dqkv_s[i] = jnp.concatenate(v, -1).astype(BF)

    bfpart[0] = (
        dot_nt(dqkv_s[0], weight(0)) + dot_nt(dqkv_s[1], weight(1)) + dot_nt(dqkv_s[2], weight(2))
    ).astype(BF)
    b_sem = next(counter)
    bc = remote(bfpart.at[0], bfpart.at[1], b_sem, partner)
    bc.start()

    for i in range(3):
        gradient(i + 1, dot_tn(xn1_s[...], dqkv_s[i]))

    bc.wait()
    dxn1 = bfpart[0].astype(F32) + bfpart[1].astype(F32)
    hat1 = hat1_s[...]
    gg1, gb1 = colsum(dxn1 * hat1), colsum(dxn1)
    u = dxn1 * ga1
    gx_ref[...] = dx1_s[...] + rstd1 * (u - rowmean(u) - hat1 * rowmean(u * hat1))

    smsend[...] = jnp.zeros(smsend.shape, F32)
    smsend[0:n] = dot_tn(dlog, xn2_s[...])
    smsend[n : n + 1] = gg1
    smsend[n + 1 : n + 2] = gb1
    smsend[n + 2 : n + 3] = gg2
    smsend[n + 3 : n + 4] = gb2
    ssend[...] = smsend[...].T.reshape(lines, plane, rows, ssend.shape[3]).astype(BF)
    to_plane(4, ssend, sr1)
    deliver(0)

    finish(grow.at[pl.ds(0, n - 1)], gate_sem)
    gate_col = rowsum(one_s[...] * pick_nn(sel_s[...], grow[:, 0, :]))
    gated = gate_col * c2[...].astype(F32)
    c2[...] = gated.astype(BF)
    gbout_ref[...] = colsum(gated)
    x2[...] = (gate_col * x2[...].astype(F32)).astype(BF)
    lane = iota((M, LANES), 1)
    gate_parts = halves(gate_col)
    gate_lanes = sum(jnp.where(lane == i, part.astype(F32), 0.0) for i, part in enumerate(gate_parts)).astype(BF)

    def grads(i, _):
        f = pl.ds(pl.multiple_of(i * FT, FT), FT)
        gwout_ref[f, :] = dot_tn(a_s[:, f], c2[...])
        gwin_ref[:, f] = dot_tn(x2[...], dh_s[:, f])
        gbin_ref[:, f] = colsum(dot_tn(gate_lanes, dh_s[:, f]))
        return 0

    lax.fori_loop(0, F // FT, grads, 0)
    outs = [(gwin_ref, gwin_out), (gwout_ref, gwout_out), (gbin_ref, gbin_out), (gbout_ref, gbout_out), (gx_ref, gx_out)]
    outs = [pltpu.make_async_copy(src, dst, hbm_sem.at[i]) for i, (src, dst) in enumerate(outs)]
    for move in outs:
        move.start()

    finish(er.at[pl.ds(0, n - 1)], e_sem)
    if tail:
        finish(ert.at[pl.ds(0, n - 1)], odd_e)

    y = x1_s[:, pl.ds(col, HW)] + picked(er, ert)
    y_ref[...] = y.astype(BF)
    outs.append(pltpu.make_async_copy(y_ref, y_out, hbm_sem.at[5]))
    outs[-1].start()

    for i in ORDER:
        deliver(i)
    to_line(4, ssend, sr1, s2s, rsmall_ref)

    for move in outs:
        move.wait()

    finish(rs_ref.at[:, pl.ds(1, lines - 1)], second_sems[0])
    finish(rsmall_ref.at[pl.ds(1, lines - 1)], second_sems[4])


def last_kernel(
    y_in, gx_in, rs, rsmall, gwin_in, gbin_in, gwout_in, gbout_in,
    y, gx, gq, gk, gv, go, gr, a1, b1, a2, b2, gwin, gbin, gwout, gbout,
    sums, turned, lines_s, sem,
):
    n, rows = gr.shape
    moves = [(gwin_in, gwin), (gwout_in, gwout), (gx_in, gx), (y_in, y), (gbin_in, gbin), (gbout_in, gbout)]
    moves += [(sums.at[i], ref) for i, ref in enumerate((go, gq, gk, gv))]
    moves += [(turned, gr)] + [(lines_s.at[i], ref) for i, ref in enumerate((a1, b1, a2, b2))]
    copies = [pltpu.make_async_copy(src, dst, sem.at[i]) for i, (src, dst) in enumerate(moves)]
    for c in copies[:6]:
        c.start()
    small = jnp.sum(rsmall[...].astype(F32), 0).T
    turned[...] = small[0:n, 0:rows]
    for i in range(4):
        lines_s[i] = small[n + i : n + i + 1, 0:rows]
        sums[i] = jnp.sum(rs[i].astype(F32), 0)
    for c in copies[6:]:
        c.start()
    for c in copies:
        c.wait()


def shards(
    block_input, routes, w_query, w_key, w_value, w_output, w_router, norm1_gain, norm1_bias, norm2_gain, norm2_bias,
    expert_in, expert_in_bias, expert_out, expert_out_bias, cotangent,
):
    z = Sizes()
    z.n = lax.axis_size("expert")
    z.T, z.D = block_input.shape
    z.HW = cotangent.shape[1]
    z.F = expert_in.shape[2]
    z.rows = w_query.shape[0]
    z.heads = z.HW // HEAD_DIM
    experts, topk = w_router.shape[1], routes.shape[1]
    cap = max(2, 2 * topk * z.T // experts)
    z.tail = 1 if cap > 8 and cap % 8 == 1 else 0
    z.R = cap - 1 if z.tail else -(-cap // 8) * 8
    z.M = z.n * (z.R + z.tail)
    z.lines = 4
    z.plane = z.n // z.lines
    z.chunks = CHUNKS
    z.sems = 49
    n, T, D, HW, R, F, rows, M = z.n, z.T, z.D, z.HW, z.R, z.F, z.rows, z.M
    lines, plane = z.lines, z.plane
    wide = -(-(n + 4) // LANES) * LANES
    vm = pl.BlockSpec(memory_space=pltpu.VMEM)
    hbm = pl.BlockSpec(memory_space=pl.ANY)
    out_shape = (
        jax.ShapeDtypeStruct((T, HW), BF),
        jax.ShapeDtypeStruct((T, D), F32),
        jax.ShapeDtypeStruct((4, lines, rows, HW), BF),
        jax.ShapeDtypeStruct((lines, rows, wide), BF),
        jax.ShapeDtypeStruct((D, F), F32),
        jax.ShapeDtypeStruct((1, F), F32),
        jax.ShapeDtypeStruct((F, D), F32),
        jax.ShapeDtypeStruct((1, D), F32),
    )
    V = pltpu.VMEM
    args = (
        block_input, routes.T, w_query, w_key, w_value, w_output.T, w_router.T,
        norm1_gain[None], norm1_bias[None], norm2_gain[None], norm2_bias[None],
        expert_in_bias, expert_out_bias, cotangent, expert_in, expert_out,
    )
    tp = -(-T // LANES) * LANES
    scratch = [
        *(V(out_shape[i].shape, out_shape[i].dtype) for i in (0, 1, 4, 5, 6, 7)),
        V((D, F), F32), V((F, D), F32), V((D, F), BF), V((F, D), BF), V((wide, LANES), F32), V((8, tp), F32), V((tp, LANES), F32),
        V((n, 2 * rows + rows * wide // HW, HW), BF), V((n, 2 * rows, HW), BF),
        V((M, T), BF), V((2, T, M), BF), V((M, n), BF), V((n, M), BF), V((M, LANES), F32), V((M, LANES), F32), V((M, HW), F32), V((M, HW), F32), V((T, D), F32), V((T, D), BF), V((3, T, HW), BF), V((z.heads, T, T), F32),
        V((T, HW), BF), V((T, D), BF), V((T, D), BF),
        V((T, D), F32), V((T, D), F32), V((T, D), BF), V((2, T, HW), BF),
        V((n, R, HW), BF), V((2, n, R, HW), BF), V((n, R, HW), BF), V((2, n, R, HW), BF),
        V((n, 1, HW), BF), V((2, n, 1, HW), BF), V((n, 1, HW), BF), V((2, n, 1, HW), BF),
        *[V((n, 1, HW), BF)] * 4,
        V((n, 1, LANES), F32), V((n, 1, LANES), F32), V((M, D), BF), V((M, D), BF), V((M, F), BF), V((M, F), BF),
        V((2, M, HW), BF), V((2, M, HW), BF), V((n, R, HW), BF), V((n, R, HW), BF), V((n, R, HW), BF), V((n, R, HW), BF),
        V((n, 1, LANES), F32), V((2, n, 1, LANES), F32), V((T, HW), F32), V((2, T, HW), F32), V((T, D), F32), V((3, T, HW), BF),
        V((4, lines, plane, rows, HW), BF), V((4, plane - 1, lines, rows, HW), BF), V((4, lines, rows, HW), BF), V((wide, D), F32),
        V((lines, plane, rows, wide), BF), V((plane - 1, lines, rows, wide), BF), V((lines, rows, wide), BF), V((2, T, D), BF),
        *(V(v.shape, v.dtype) for v in args[:14]),
        pltpu.SemaphoreType.DMA((16,)), pltpu.SemaphoreType.DMA((z.sems,)), pltpu.SemaphoreType.DMA((z.sems,)),
    ]
    kept = [pltpu.VMEM(v.shape, v.dtype) for v in out_shape]
    done = pl.pallas_call(
        functools.partial(block_kernel, z),
        out_shape=kept,
        in_specs=[pl.BlockSpec(memory_space=pltpu.HBM)] * 16,
        out_specs=[hbm] * 2 + [vm] * 2 + [hbm] * 4,
        scratch_shapes=scratch,
        compiler_params=pltpu.CompilerParams(collective_id=0, has_side_effects=True, vmem_limit_bytes=52 << 20),
        name="block",
    )(
        *(pltpu.with_memory_space_constraint(v, pltpu.HBM) for v in args)
    )
    square = jax.ShapeDtypeStruct((rows, HW), F32)
    line = jax.ShapeDtypeStruct((1, rows), F32)
    last_shape = (
        out_shape[0], out_shape[1], square, square, square, square, jax.ShapeDtypeStruct((n, rows), F32), line, line, line, line,
        out_shape[4], out_shape[5], out_shape[6], out_shape[7],
    )
    y, gx, gq, gk, gv, go, gr, a1, b1, a2, b2, gwin, gbin, gwout, gbout = pl.pallas_call(
        last_kernel,
        out_shape=last_shape,
        in_specs=[hbm] * 2 + [vm] * 2 + [hbm] * 4,
        out_specs=[hbm] * 15,
        scratch_shapes=[
            V((4, rows, HW), F32), V((n, rows), F32), V((4, 1, rows), F32), pltpu.SemaphoreType.DMA((15,)),
        ],
        compiler_params=pltpu.CompilerParams(vmem_limit_bytes=8 << 20),
        name="last",
    )(*done)
    return (y, gx, gq, gk, gv, go.T, gr.T, a1[0], b1[0], a2[0], b2[0], gwin[None], gbin, gwout[None], gbout)


def solution(mesh):
    row, col = P("expert", None), P("expert", "tensor")
    vec = P("expert")
    in_specs = (
        row, row, col, col, col, P("tensor", "expert"), row, vec, vec, vec, vec,
        P("expert", None, "tensor"), col, P("expert", "tensor", None), row, col,
    )
    out_specs = (
        col, row, col, col, col, P("tensor", "expert"), row, vec, vec, vec, vec,
        P("expert", None, "tensor"), col, P("expert", "tensor", None), row,
    )
    return jax.shard_map(shards, mesh=mesh, in_specs=in_specs, out_specs=out_specs, check_vma=False)
```
